256 devices in a mesh: blk: 16 (over z, core), red: 16 (over x, y).
Axes of the slice: x: 4, y: 4, z: 8, core: 2. Of those that a mesh axis runs over, the one named last changes fastest.
Arguments:
- amplitudes: bfloat16 [8, 192, 128, 128], P(None, 'blk', 'red'), may hold values from -6 to 6
- ladder_ints: bfloat16 [16384, 16384], P('red', 'blk'), may hold values from -0.046875 to 0.046875
- cycle_ints: bfloat16 [24576, 24576], P('blk', 'red'), may hold values from -0.0390625 to 0.0390625
- occ_energy: float32 [192], replicated, may hold values from -2 to -0.3
- vir_energy: float32 [128], replicated, may hold values from 0.2 to 3
- slab_index: int32 [8], replicated, may hold values from 0 to 191
Outputs:
- update: float32 [8, 192, 128, 128], P(None, 'red', 'blk')
The draws below stay inside these ranges and needn't reach their ends.
All inputs are finite; a program needn't handle non-finite values.
Results may differ from the reference program's by a relative error of at most 0.0003.
Values may be sent and summed in bfloat16 or wider, within the bound.
A program may use at most 64 MiB of HBM per device.

```python
import jax
import jax.numpy as jnp

OCC = 192
VIRT = 128
SLAB = 8


def plant(result, stream_key, low, largest):
    longest = result.shape.index(max(result.shape))
    spots = []
    for shift in (0, 1):
        where = [jax.random.randint(jax.random.fold_in(stream_key, axis), (), 0, length) for axis, length in enumerate(result.shape)]
        where[longest] = (where[longest] + shift) % result.shape[longest]
        spots.append(tuple(where))
    return result.at[spots[0]].set(low).at[spots[1]].set(largest)


def level_of(own_key, extent, pieces, least, top_value):
    level, own = 1.0, jax.random.fold_in(own_key, 6)
    for axis_at, blocks in pieces:
        heights = jnp.exp(jax.random.uniform(jax.random.fold_in(own, axis_at), (blocks,), jnp.float32, least / len(pieces), top_value / len(pieces)))
        level = level * jnp.repeat(heights, extent[axis_at] // blocks).reshape([-1 if axis == axis_at else 1 for axis in range(len(extent))])
    return level


def scatter_about(stream_key, extent, spread, reach, pieces=(), kind=jnp.bfloat16):
    array = jax.random.normal(stream_key, extent, jnp.float32) * spread
    if len(pieces) > 0:
        array = level_of(stream_key, extent, pieces, -0.22, 0.18) * array
    return jnp.clip(array, min=-reach, max=reach).astype(kind)


def setup_inputs(seed: int = 0) -> dict:
    key_list = jax.random.split(jax.random.key(seed), 7)
    amplitudes = scatter_about(key_list[0], (SLAB, OCC, VIRT, VIRT), 1.0, 6.0, ((1, 16), (2, 16)))
    ladder_ints = scatter_about(key_list[1], (VIRT * VIRT, VIRT * VIRT), (VIRT * VIRT) ** -0.5, 0.046875, ((0, 16), (1, 16)))
    cycle_ints = scatter_about(key_list[2], (OCC * VIRT, OCC * VIRT), (OCC * VIRT) ** -0.5, 0.0390625, ((0, 16), (1, 16)))
    occ_energy = jnp.clip(jax.random.uniform(key_list[3], (OCC,), jnp.float32, -2.0, -0.3), -2.0, -0.3)
    vir_energy = jnp.clip(jax.random.uniform(key_list[4], (VIRT,), jnp.float32, 0.2, 3.0), 0.2, 3.0)
    slab_index = plant(jax.random.randint(key_list[5], (SLAB,), 0, OCC), jax.random.fold_in(key_list[5], 1), 0, OCC - 1).astype(jnp.int32)
    return dict(amplitudes=amplitudes, ladder_ints=ladder_ints, cycle_ints=cycle_ints, occ_energy=occ_energy, vir_energy=vir_energy, slab_index=slab_index)


def reference(amplitudes, ladder_ints, cycle_ints, occ_energy, vir_energy, slab_index):
    flattened = amplitudes.reshape(SLAB * OCC, VIRT * VIRT)
    ladder = jnp.dot(flattened, ladder_ints, preferred_element_type=jnp.float32).reshape(SLAB, OCC, VIRT, VIRT)
    operand = jnp.transpose(amplitudes, (0, 2, 1, 3)).reshape(SLAB * VIRT, OCC * VIRT)
    cycle_term = jnp.dot(operand, cycle_ints, preferred_element_type=jnp.float32).reshape(SLAB, VIRT, OCC, VIRT)
    cycle_term = jnp.transpose(cycle_term, (0, 2, 1, 3))
    orbital_ids = jnp.arange(OCC, dtype=jnp.int32)
    chosen = (slab_index.astype(jnp.int32)[:, None] == orbital_ids[None, :])
    slab_energy = jnp.sum(jnp.where(chosen, occ_energy[None, :], jnp.float32(0.0)), axis=1)
    denominator = (vir_energy[None, None, :, None] + vir_energy[None, None, None, :]
                   - slab_energy[:, None, None, None] - occ_energy[None, :, None, None])
    return (ladder + cycle_term) / denominator
```

```python
import functools

import jax
import jax.numpy as jnp
from jax import lax
from jax.experimental import pallas as pl
from jax.experimental.pallas import tpu as pltpu
from jax.sharding import PartitionSpec as P

MESH = pl.DeviceIdType.MESH


def _exchange_kernel(n, per_peer, src_ref, dst_ref, send_sem, recv_sem, local_sem):
    me = lax.axis_index("red")
    row = lax.axis_index("blk")

    def peer_of(o):
        return lax.rem(me + o, n)

    barrier = pltpu.get_barrier_semaphore()
    for o in range(1, n):
        pl.semaphore_signal(barrier, inc=1, device_id=(row, peer_of(o)), device_id_type=MESH)
    pl.semaphore_wait(barrier, n - 1)

    def src_for(g):
        return src_ref.at[g] if per_peer else src_ref

    for o in range(1, n):
        g = peer_of(o)
        pltpu.make_async_remote_copy(
            src_ref=src_for(g),
            dst_ref=dst_ref.at[me],
            send_sem=send_sem.at[g],
            recv_sem=recv_sem.at[me],
            device_id=(row, g),
            device_id_type=MESH,
        ).start()
    local = pltpu.make_async_copy(src_for(me), dst_ref.at[me], local_sem)
    local.start()
    local.wait()
    for o in range(1, n):
        g = peer_of(o)
        pltpu.make_async_remote_copy(
            src_ref=src_for(g),
            dst_ref=dst_ref.at[g],
            send_sem=send_sem.at[g],
            recv_sem=recv_sem.at[g],
            device_id=(row, g),
            device_id_type=MESH,
        ).wait()


def _exchange(x, n, per_peer, collective_id):
    out_shape = x.shape if per_peer else (n,) + x.shape
    nbytes = x.size * x.dtype.itemsize * (1 if per_peer else n)
    return pl.pallas_call(
        functools.partial(_exchange_kernel, n, per_peer),
        out_shape=jax.ShapeDtypeStruct(out_shape, x.dtype),
        in_specs=[pl.BlockSpec(memory_space=pl.ANY)],
        out_specs=pl.BlockSpec(memory_space=pl.ANY),
        scratch_shapes=[
            pltpu.SemaphoreType.DMA((n,)),
            pltpu.SemaphoreType.DMA((n,)),
            pltpu.SemaphoreType.DMA,
        ],
        compiler_params=pltpu.CompilerParams(collective_id=collective_id, has_side_effects=True),
        cost_estimate=pl.CostEstimate(flops=0, bytes_accessed=2 * nbytes, transcendentals=0),
    )(x)


def shards(amplitudes, ladder_ints, cycle_ints, occ_energy, vir_energy, slab_index):
    slab_rows, occ_local, vir_local, virt_width = amplitudes.shape
    n_red = lax.axis_size("red")
    n_blk = lax.axis_size("blk")
    occ_all = occ_local * n_blk
    occ_red = occ_all // n_red

    swapped = jnp.transpose(amplitudes, (0, 2, 1, 3))
    gathered = _exchange(swapped, n_red, False, 0)
    operand = gathered.reshape(n_red * slab_rows * vir_local, occ_local * virt_width)
    product = jnp.dot(operand, cycle_ints, preferred_element_type=jnp.float32)
    product = product.reshape(n_red, slab_rows, vir_local, cycle_ints.shape[1])
    cycle_own = lax.psum_scatter(product, "blk", scatter_dimension=0, tiled=True)[0]
    cycle_own = jnp.transpose(
        cycle_own.reshape(slab_rows, vir_local, occ_red, virt_width), (0, 2, 1, 3)
    )

    shard_piece = lax.all_gather(amplitudes, "blk", axis=0, tiled=False)
    flattened = shard_piece.reshape(n_blk * slab_rows * occ_local, vir_local * virt_width)
    product = jnp.dot(flattened, ladder_ints, preferred_element_type=jnp.float32)
    product = product.reshape(n_blk, slab_rows, occ_local, ladder_ints.shape[1])
    received = _exchange(product, n_red, True, 1)
    ladder_own = jnp.sum(received, axis=0).reshape(slab_rows, occ_red, -1, virt_width)

    vir_block = cycle_own.shape[2]
    orbital_ids = jnp.arange(occ_energy.shape[0], dtype=jnp.int32)
    chosen = slab_index[:, None] == orbital_ids[None, :]
    slab_energy = jnp.sum(jnp.where(chosen, occ_energy[None, :], jnp.float32(0.0)), axis=1)
    pair_energy = lax.dynamic_slice_in_dim(occ_energy, lax.axis_index("red") * occ_red, occ_red)
    first_virtual = lax.dynamic_slice_in_dim(
        vir_energy, lax.axis_index("blk") * vir_block, vir_block
    )
    denominator = (
        first_virtual[None, None, :, None]
        + vir_energy[None, None, None, :]
        - slab_energy[:, None, None, None]
        - pair_energy[None, :, None, None]
    )
    return (ladder_own + cycle_own) / denominator


def solution(mesh):
    placed = (P(None, "blk", "red", None), P("red", "blk"), P("blk", "red"), P(), P(), P())
    return jax.shard_map(
        shards, mesh=mesh, in_specs=placed, out_specs=P(None, "red", "blk", None), check_vma=False
    )
```

```python
import functools

import jax
import jax.numpy as jnp
from jax import lax
from jax.experimental import pallas as pl
from jax.experimental.pallas import tpu as pltpu
from jax.sharding import PartitionSpec as P

MESH = pl.DeviceIdType.MESH


NY = 4


def _group(kind, n_red):
    r = lax.axis_index("red")
    x, y = r // NY, lax.rem(r, NY)
    if kind == "y":
        return y, NY, lambda pos: x * NY + pos
    if kind == "x":
        return x, n_red // NY, lambda pos: pos * NY + y
    return r, n_red, lambda pos: pos


def _exchange_kernel(jobs, n_red, *refs):
    k = len(jobs)
    srcs, dsts = refs[:k], refs[k:2 * k]
    send_sem, recv_sem, local_sem = refs[2 * k:]
    row = lax.axis_index("blk")

    barrier = pltpu.get_barrier_semaphore()
    count = 0
    for kind in sorted(set(kind for kind, _ in jobs)):
        me, n, red_of = _group(kind, n_red)
        for o in range(1, n):
            pl.semaphore_signal(
                barrier, inc=1, device_id=(row, red_of(lax.rem(me + o, n))), device_id_type=MESH
            )
            count += 1
    pl.semaphore_wait(barrier, count)

    def remote(j, pos, slot):
        kind, src_view = jobs[j]
        _, _, red_of = _group(kind, n_red)
        return pltpu.make_async_remote_copy(
            src_ref=src_view(srcs[j], pos),
            dst_ref=dsts[j].at[slot],
            send_sem=send_sem.at[j, pos],
            recv_sem=recv_sem.at[j, slot],
            device_id=(row, red_of(pos)),
            device_id_type=MESH,
        )

    for j, (kind, src_view) in enumerate(jobs):
        me, n, _ = _group(kind, n_red)
        for o in range(1, n):
            remote(j, lax.rem(me + o, n), me).start()
    for j, (kind, src_view) in enumerate(jobs):
        me, n, _ = _group(kind, n_red)
        local = pltpu.make_async_copy(src_view(srcs[j], me), dsts[j].at[me], local_sem.at[j])
        local.start()
        local.wait()
    for j, (kind, src_view) in enumerate(jobs):
        me, n, _ = _group(kind, n_red)
        for o in range(1, n):
            g = lax.rem(me + o, n)
            remote(j, g, g).wait()


def _exchange(jobs, srcs, out_shapes, n_red, collective_id):
    nbytes = sum(s.size * s.dtype.itemsize for s in srcs)
    nmax = max(_group_size(kind, n_red) for kind, _ in jobs)
    return pl.pallas_call(
        functools.partial(_exchange_kernel, tuple(jobs), n_red),
        out_shape=tuple(jax.ShapeDtypeStruct(s, x.dtype) for s, x in zip(out_shapes, srcs)),
        in_specs=[pl.BlockSpec(memory_space=pl.ANY)] * len(srcs),
        out_specs=tuple(pl.BlockSpec(memory_space=pl.ANY) for _ in srcs),
        scratch_shapes=[
            pltpu.SemaphoreType.DMA((len(jobs), nmax)),
            pltpu.SemaphoreType.DMA((len(jobs), nmax)),
            pltpu.SemaphoreType.DMA((len(jobs),)),
        ],
        compiler_params=pltpu.CompilerParams(collective_id=collective_id, has_side_effects=True),
        cost_estimate=pl.CostEstimate(flops=0, bytes_accessed=4 * nbytes, transcendentals=0),
    )(*srcs)


def _group_size(kind, n_red):
    return {"y": NY, "x": n_red // NY}.get(kind, n_red)


def _whole(ref, pos):
    return ref


def _slot(ref, pos):
    return ref.at[pos]


def shards(amplitudes, ladder_ints, cycle_ints, occ_energy, vir_energy, slab_index):
    slab_rows, occ_local, vir_local, virt_width = amplitudes.shape
    n_red = lax.axis_size("red")
    n_blk = lax.axis_size("blk")
    occ_all = occ_local * n_blk
    occ_red = occ_all // n_red
    n_x = n_red // NY

    swapped = jnp.transpose(amplitudes, (0, 2, 1, 3)).reshape(
        slab_rows * vir_local, occ_local * virt_width
    )
    (gathered,) = _exchange(
        [("all", _whole)], [swapped], [(n_red,) + swapped.shape], n_red, 0
    )
    operand = gathered.reshape(n_red * slab_rows * vir_local, occ_local * virt_width)
    product = jnp.dot(operand, cycle_ints, preferred_element_type=jnp.float32)
    product = product.reshape(n_red, slab_rows * vir_local, cycle_ints.shape[1])
    cycle_own = lax.psum_scatter(product, "blk", scatter_dimension=0, tiled=True)[0]
    cycle_own = jnp.transpose(
        cycle_own.reshape(slab_rows, vir_local, occ_red, virt_width), (0, 2, 1, 3)
    )

    rows = slab_rows * occ_local
    flat = amplitudes.reshape(rows, vir_local * virt_width)
    shard_piece = lax.all_gather(flat, "blk", axis=0, tiled=False)
    product = jnp.dot(
        shard_piece.reshape(n_blk * rows, -1), ladder_ints, preferred_element_type=jnp.float32
    )
    cols = ladder_ints.shape[1]
    product = product.reshape(n_x, NY, rows, cols)
    half = rows // 2
    first_a, first_b = _exchange(
        [
            ("y", lambda ref, pos: ref.at[:, pos, pl.ds(0, half)]),
            ("x", lambda ref, pos: ref.at[pos, :, pl.ds(half, half)]),
        ],
        [product, product],
        [(NY, n_x, half, cols), (n_x, NY, half, cols)],
        n_red,
        1,
    )
    second_a, second_b = _exchange(
        [("x", _slot), ("y", _slot)],
        [jnp.sum(first_a, axis=0), jnp.sum(first_b, axis=0)],
        [(n_x, half, cols), (NY, half, cols)],
        n_red,
        2,
    )
    ladder_own = jnp.concatenate([jnp.sum(second_a, axis=0), jnp.sum(second_b, axis=0)], axis=0)
    ladder_own = ladder_own.reshape(slab_rows, occ_red, -1, virt_width)

    vir_block = cycle_own.shape[2]
    orbital_ids = jnp.arange(occ_energy.shape[0], dtype=jnp.int32)
    chosen = slab_index[:, None] == orbital_ids[None, :]
    slab_energy = jnp.sum(jnp.where(chosen, occ_energy[None, :], jnp.float32(0.0)), axis=1)
    pair_energy = lax.dynamic_slice_in_dim(occ_energy, lax.axis_index("red") * occ_red, occ_red)
    first_virtual = lax.dynamic_slice_in_dim(
        vir_energy, lax.axis_index("blk") * vir_block, vir_block
    )
    denominator = (
        first_virtual[None, None, :, None]
        + vir_energy[None, None, None, :]
        - slab_energy[:, None, None, None]
        - pair_energy[None, :, None, None]
    )
    return (ladder_own + cycle_own) / denominator


def solution(mesh):
    placed = (P(None, "blk", "red", None), P("red", "blk"), P("blk", "red"), P(), P(), P())
    return jax.shard_map(
        shards, mesh=mesh, in_specs=placed, out_specs=P(None, "red", "blk", None), check_vma=False
    )
```

```python
import functools

import jax
import jax.numpy as jnp
from jax import lax
from jax.experimental import pallas as pl
from jax.experimental.pallas import tpu as pltpu
from jax.sharding import PartitionSpec as P

MESH = pl.DeviceIdType.MESH


NY = 4


def _group(kind, n_red):
    r = lax.axis_index("red")
    x, y = r // NY, lax.rem(r, NY)
    if kind == "y":
        return y, NY, lambda pos: x * NY + pos
    if kind == "x":
        return x, n_red // NY, lambda pos: pos * NY + y
    return r, n_red, lambda pos: pos


def _exchange_kernel(jobs, n_in, n_out, n_red, *refs):
    ins, outs = refs[:n_in], refs[n_in:n_in + n_out]
    send_sem, recv_sem, local_sem = refs[n_in + n_out:]
    row = lax.axis_index("blk")

    barrier = pltpu.get_barrier_semaphore()
    count = 0
    for kind in sorted(set(job[0] for job in jobs)):
        me, n, red_of = _group(kind, n_red)
        for o in range(1, n):
            pl.semaphore_signal(
                barrier, inc=1, device_id=(row, red_of(lax.rem(me + o, n))), device_id_type=MESH
            )
            count += 1
    pl.semaphore_wait(barrier, count)

    def remote(j, pos, slot):
        kind, si, src_view, di, dst_view = jobs[j]
        _, _, red_of = _group(kind, n_red)
        return pltpu.make_async_remote_copy(
            src_ref=src_view(ins[si], pos),
            dst_ref=dst_view(outs[di], slot),
            send_sem=send_sem.at[j, pos],
            recv_sem=recv_sem.at[j, slot],
            device_id=(row, red_of(pos)),
            device_id_type=MESH,
        )

    for j, job in enumerate(jobs):
        me, n, _ = _group(job[0], n_red)
        for o in range(1, n):
            remote(j, lax.rem(me + o, n), me).start()
    for j, (kind, si, src_view, di, dst_view) in enumerate(jobs):
        me, n, _ = _group(kind, n_red)
        local = pltpu.make_async_copy(
            src_view(ins[si], me), dst_view(outs[di], me), local_sem.at[j]
        )
        local.start()
        local.wait()
    for j, job in enumerate(jobs):
        me, n, _ = _group(job[0], n_red)
        for o in range(1, n):
            g = lax.rem(me + o, n)
            remote(j, g, g).wait()


def _exchange(jobs, srcs, out_shapes, n_red, collective_id):
    nbytes = sum(s.size * s.dtype.itemsize for s in srcs)
    nmax = max(_group_size(job[0], n_red) for job in jobs)
    return pl.pallas_call(
        functools.partial(_exchange_kernel, tuple(jobs), len(srcs), len(out_shapes), n_red),
        out_shape=tuple(jax.ShapeDtypeStruct(s, d) for s, d in out_shapes),
        in_specs=[pl.BlockSpec(memory_space=pl.ANY)] * len(srcs),
        out_specs=tuple(pl.BlockSpec(memory_space=pl.ANY) for _ in out_shapes),
        scratch_shapes=[
            pltpu.SemaphoreType.DMA((len(jobs), nmax)),
            pltpu.SemaphoreType.DMA((len(jobs), nmax)),
            pltpu.SemaphoreType.DMA((len(jobs),)),
        ],
        compiler_params=pltpu.CompilerParams(collective_id=collective_id, has_side_effects=True),
        cost_estimate=pl.CostEstimate(flops=0, bytes_accessed=4 * nbytes, transcendentals=0),
    )(*srcs)


def _group_size(kind, n_red):
    return {"y": NY, "x": n_red // NY}.get(kind, n_red)


def _whole(ref, pos):
    return ref


def _slot(ref, pos):
    return ref.at[pos]


def shards(amplitudes, ladder_ints, cycle_ints, occ_energy, vir_energy, slab_index):
    slab_rows, occ_local, vir_local, virt_width = amplitudes.shape
    n_red = lax.axis_size("red")
    n_blk = lax.axis_size("blk")
    occ_all = occ_local * n_blk
    occ_red = occ_all // n_red
    n_x = n_red // NY

    swapped = jnp.transpose(amplitudes, (0, 2, 1, 3)).reshape(
        slab_rows * vir_local, occ_local * virt_width
    )
    width = swapped.shape[1]
    part = swapped.shape[0] // 2
    bf = swapped.dtype
    near_a, near_b = _exchange(
        [
            ("y", 0, lambda ref, pos: ref.at[pl.ds(0, part)], 0, _slot),
            ("x", 0, lambda ref, pos: ref.at[pl.ds(part, part)], 1, _slot),
        ],
        [swapped],
        [((NY, part, width), bf), ((n_x, part, width), bf)],
        n_red,
        0,
    )
    (gathered,) = _exchange(
        [
            ("x", 0, _whole, 0, lambda ref, slot: ref.at[slot, :, pl.ds(0, part)]),
            ("y", 1, _whole, 0, lambda ref, slot: ref.at[:, slot, pl.ds(part, part)]),
        ],
        [near_a, near_b],
        [((n_x, NY, 2 * part, width), bf)],
        n_red,
        3,
    )
    operand = gathered.reshape(n_red * slab_rows * vir_local, occ_local * virt_width)
    product = jnp.dot(operand, cycle_ints, preferred_element_type=jnp.float32)
    product = product.reshape(n_red, slab_rows * vir_local, cycle_ints.shape[1])
    cycle_own = lax.psum_scatter(product, "blk", scatter_dimension=0, tiled=True)[0]
    cycle_own = jnp.transpose(
        cycle_own.reshape(slab_rows, vir_local, occ_red, virt_width), (0, 2, 1, 3)
    )

    rows = slab_rows * occ_local
    flat = amplitudes.reshape(rows, vir_local * virt_width)
    shard_piece = lax.all_gather(flat, "blk", axis=0, tiled=False)
    product = jnp.dot(
        shard_piece.reshape(n_blk * rows, -1), ladder_ints, preferred_element_type=jnp.float32
    )
    cols = ladder_ints.shape[1]
    product = product.reshape(n_x, NY, rows, cols)
    half = rows // 2
    first_a, first_b = _exchange(
        [
            ("y", 0, lambda ref, pos: ref.at[:, pos, pl.ds(0, half)], 0, _slot),
            ("x", 0, lambda ref, pos: ref.at[pos, :, pl.ds(half, half)], 1, _slot),
        ],
        [product],
        [((NY, n_x, half, cols), jnp.float32), ((n_x, NY, half, cols), jnp.float32)],
        n_red,
        1,
    )
    second_a, second_b = _exchange(
        [("x", 0, _slot, 0, _slot), ("y", 1, _slot, 1, _slot)],
        [jnp.sum(first_a, axis=0), jnp.sum(first_b, axis=0)],
        [((n_x, half, cols), jnp.float32), ((NY, half, cols), jnp.float32)],
        n_red,
        2,
    )
    ladder_own = jnp.concatenate([jnp.sum(second_a, axis=0), jnp.sum(second_b, axis=0)], axis=0)
    ladder_own = ladder_own.reshape(slab_rows, occ_red, -1, virt_width)

    vir_block = cycle_own.shape[2]
    orbital_ids = jnp.arange(occ_energy.shape[0], dtype=jnp.int32)
    chosen = slab_index[:, None] == orbital_ids[None, :]
    slab_energy = jnp.sum(jnp.where(chosen, occ_energy[None, :], jnp.float32(0.0)), axis=1)
    pair_energy = lax.dynamic_slice_in_dim(occ_energy, lax.axis_index("red") * occ_red, occ_red)
    first_virtual = lax.dynamic_slice_in_dim(
        vir_energy, lax.axis_index("blk") * vir_block, vir_block
    )
    denominator = (
        first_virtual[None, None, :, None]
        + vir_energy[None, None, None, :]
        - slab_energy[:, None, None, None]
        - pair_energy[None, :, None, None]
    )
    return (ladder_own + cycle_own) / denominator


def solution(mesh):
    placed = (P(None, "blk", "red", None), P("red", "blk"), P("blk", "red"), P(), P(), P())
    return jax.shard_map(
        shards, mesh=mesh, in_specs=placed, out_specs=P(None, "red", "blk", None), check_vma=False
    )
```

```python
import functools

import jax
import jax.numpy as jnp
from jax import lax
from jax.experimental import pallas as pl
from jax.experimental.pallas import tpu as pltpu
from jax.sharding import PartitionSpec as P

MESH = pl.DeviceIdType.MESH


NY = 4


def _group(kind, n_red):
    r = lax.axis_index("red")
    x, y = r // NY, lax.rem(r, NY)
    if kind == "y":
        return y, NY, lambda pos: x * NY + pos
    if kind == "x":
        return x, n_red // NY, lambda pos: pos * NY + y
    return r, n_red, lambda pos: pos


def _half(ref, which):
    size = ref.shape[0] // 2
    return ref.at[pl.ds(which * size, size)]


def _exchange_kernel(jobs, n_in, n_out, n_red, *refs):
    ins, outs = refs[:n_in], refs[n_in:n_in + n_out]
    relays = refs[n_in + n_out:n_in + n_out + len(jobs)]
    send_sem, recv_sem, local_sem = refs[n_in + n_out + len(jobs):]
    row = lax.axis_index("blk")

    barrier = pltpu.get_barrier_semaphore()
    count = 0
    for kind in sorted(set(job[0] for job in jobs)):
        me, n, red_of = _group(kind, n_red)
        for o in range(1, n):
            pl.semaphore_signal(
                barrier, inc=1, device_id=(row, red_of(lax.rem(me + o, n))), device_id_type=MESH
            )
            count += 1
    pl.semaphore_wait(barrier, count)

    def copy(j, role, src, dst, pos):
        _, _, red_of = _group(jobs[j][0], n_red)
        return pltpu.make_async_remote_copy(
            src_ref=src,
            dst_ref=dst,
            send_sem=send_sem.at[j, role],
            recv_sem=recv_sem.at[j, role],
            device_id=(row, red_of(pos)),
            device_id_type=MESH,
        )

    started = []
    for j, (kind, si, src_view, di, dst_view) in enumerate(jobs):
        me, n, _ = _group(kind, n_red)
        right, left, far = lax.rem(me + 1, n), lax.rem(me + n - 1, n), lax.rem(me + 2, n)
        sends = [
            copy(j, 0, src_view(ins[si], right), dst_view(outs[di], me), right),
            copy(j, 1, src_view(ins[si], left), dst_view(outs[di], me), left),
            copy(j, 2, _half(src_view(ins[si], far), 0), relays[j].at[0], right),
            copy(j, 3, _half(src_view(ins[si], far), 1), relays[j].at[1], left),
        ]
        for c in sends:
            c.start()
        started.append(sends)
    for j, (kind, si, src_view, di, dst_view) in enumerate(jobs):
        me, n, _ = _group(kind, n_red)
        local = pltpu.make_async_copy(
            src_view(ins[si], me), dst_view(outs[di], me), local_sem.at[j]
        )
        local.start()
        local.wait()
    for j, (kind, si, src_view, di, dst_view) in enumerate(jobs):
        me, n, _ = _group(kind, n_red)
        right, left = lax.rem(me + 1, n), lax.rem(me + n - 1, n)
        to_right = copy(j, 4, relays[j].at[0], _half(dst_view(outs[di], left), 0), right)
        to_left = copy(j, 5, relays[j].at[1], _half(dst_view(outs[di], right), 1), left)
        copy(j, 2, relays[j].at[0], relays[j].at[0], right).wait_recv()
        to_right.start()
        copy(j, 3, relays[j].at[1], relays[j].at[1], left).wait_recv()
        to_left.start()
        started[j] += [to_right, to_left]
    for j, (kind, si, src_view, di, dst_view) in enumerate(jobs):
        me, n, _ = _group(kind, n_red)
        right, left, far = lax.rem(me + 1, n), lax.rem(me + n - 1, n), lax.rem(me + 2, n)
        for c in started[j]:
            c.wait_send()
        copy(j, 0, src_view(ins[si], me), dst_view(outs[di], left), left).wait_recv()
        copy(j, 1, src_view(ins[si], me), dst_view(outs[di], right), right).wait_recv()
        copy(j, 4, relays[j].at[0], _half(dst_view(outs[di], far), 0), left).wait_recv()
        copy(j, 5, relays[j].at[1], _half(dst_view(outs[di], far), 1), right).wait_recv()


def _exchange(jobs, srcs, out_shapes, units, n_red, collective_id):
    nbytes = sum(s.size * s.dtype.itemsize for s in srcs)
    relay_shapes = [
        pltpu.VMEM((2, unit[0] // 2) + tuple(unit[1:]), srcs[job[1]].dtype)
        for job, unit in zip(jobs, units)
    ]
    return pl.pallas_call(
        functools.partial(_exchange_kernel, tuple(jobs), len(srcs), len(out_shapes), n_red),
        out_shape=tuple(jax.ShapeDtypeStruct(s, d) for s, d in out_shapes),
        in_specs=[pl.BlockSpec(memory_space=pl.ANY)] * len(srcs),
        out_specs=tuple(pl.BlockSpec(memory_space=pl.ANY) for _ in out_shapes),
        scratch_shapes=relay_shapes + [
            pltpu.SemaphoreType.DMA((len(jobs), 6)),
            pltpu.SemaphoreType.DMA((len(jobs), 6)),
            pltpu.SemaphoreType.DMA((len(jobs),)),
        ],
        compiler_params=pltpu.CompilerParams(collective_id=collective_id, has_side_effects=True),
        cost_estimate=pl.CostEstimate(flops=0, bytes_accessed=4 * nbytes, transcendentals=0),
    )(*srcs)


def _group_size(kind, n_red):
    return {"y": NY, "x": n_red // NY}.get(kind, n_red)


def _whole(ref, pos):
    return ref


def _slot(ref, pos):
    return ref.at[pos]


def shards(amplitudes, ladder_ints, cycle_ints, occ_energy, vir_energy, slab_index):
    slab_rows, occ_local, vir_local, virt_width = amplitudes.shape
    n_red = lax.axis_size("red")
    n_blk = lax.axis_size("blk")
    occ_all = occ_local * n_blk
    occ_red = occ_all // n_red
    n_x = n_red // NY

    swapped = jnp.transpose(amplitudes, (0, 2, 1, 3)).reshape(
        slab_rows * vir_local, occ_local * virt_width
    )
    width = swapped.shape[1]
    part = swapped.shape[0] // 2
    bf = swapped.dtype
    near_a, near_b = _exchange(
        [
            ("y", 0, lambda ref, pos: ref.at[pl.ds(0, part)], 0, _slot),
            ("x", 0, lambda ref, pos: ref.at[pl.ds(part, part)], 1, _slot),
        ],
        [swapped],
        [((NY, part, width), bf), ((n_x, part, width), bf)],
        [(part, width), (part, width)],
        n_red,
        0,
    )
    (gathered,) = _exchange(
        [
            ("x", 0, _whole, 0, lambda ref, slot: ref.at[slot, :, pl.ds(0, part)]),
            ("y", 1, _whole, 0, lambda ref, slot: ref.at[:, slot, pl.ds(part, part)]),
        ],
        [near_a, near_b],
        [((n_x, NY, 2 * part, width), bf)],
        [(NY, part, width), (n_x, part, width)],
        n_red,
        3,
    )
    operand = gathered.reshape(n_red * slab_rows * vir_local, occ_local * virt_width)
    product = jnp.dot(operand, cycle_ints, preferred_element_type=jnp.float32)
    product = product.reshape(n_red, slab_rows * vir_local, cycle_ints.shape[1])
    cycle_own = lax.psum_scatter(product, "blk", scatter_dimension=0, tiled=True)[0]
    cycle_own = jnp.transpose(
        cycle_own.reshape(slab_rows, vir_local, occ_red, virt_width), (0, 2, 1, 3)
    )

    rows = slab_rows * occ_local
    flat = amplitudes.reshape(rows, vir_local * virt_width)
    shard_piece = lax.all_gather(flat, "blk", axis=0, tiled=False)
    product = jnp.dot(
        shard_piece.reshape(n_blk * rows, -1), ladder_ints, preferred_element_type=jnp.float32
    )
    cols = ladder_ints.shape[1]
    product = product.reshape(n_x, NY, rows, cols)
    half = rows // 2
    first_a, first_b = _exchange(
        [
            ("y", 0, lambda ref, pos: ref.at[:, pos, pl.ds(0, half)], 0, _slot),
            ("x", 0, lambda ref, pos: ref.at[pos, :, pl.ds(half, half)], 1, _slot),
        ],
        [product],
        [((NY, n_x, half, cols), jnp.float32), ((n_x, NY, half, cols), jnp.float32)],
        [(n_x, half, cols), (NY, half, cols)],
        n_red,
        1,
    )
    second_a, second_b = _exchange(
        [("x", 0, _slot, 0, _slot), ("y", 1, _slot, 1, _slot)],
        [jnp.sum(first_a, axis=0), jnp.sum(first_b, axis=0)],
        [((n_x, half, cols), jnp.float32), ((NY, half, cols), jnp.float32)],
        [(half, cols), (half, cols)],
        n_red,
        2,
    )
    ladder_own = jnp.concatenate([jnp.sum(second_a, axis=0), jnp.sum(second_b, axis=0)], axis=0)
    ladder_own = ladder_own.reshape(slab_rows, occ_red, -1, virt_width)

    vir_block = cycle_own.shape[2]
    orbital_ids = jnp.arange(occ_energy.shape[0], dtype=jnp.int32)
    chosen = slab_index[:, None] == orbital_ids[None, :]
    slab_energy = jnp.sum(jnp.where(chosen, occ_energy[None, :], jnp.float32(0.0)), axis=1)
    pair_energy = lax.dynamic_slice_in_dim(occ_energy, lax.axis_index("red") * occ_red, occ_red)
    first_virtual = lax.dynamic_slice_in_dim(
        vir_energy, lax.axis_index("blk") * vir_block, vir_block
    )
    denominator = (
        first_virtual[None, None, :, None]
        + vir_energy[None, None, None, :]
        - slab_energy[:, None, None, None]
        - pair_energy[None, :, None, None]
    )
    return (ladder_own + cycle_own) / denominator


def solution(mesh):
    placed = (P(None, "blk", "red", None), P("red", "blk"), P("blk", "red"), P(), P(), P())
    return jax.shard_map(
        shards, mesh=mesh, in_specs=placed, out_specs=P(None, "red", "blk", None), check_vma=False
    )
```

```python
import functools

import jax
import jax.numpy as jnp
from jax import lax
from jax.experimental import pallas as pl
from jax.experimental.pallas import tpu as pltpu
from jax.sharding import PartitionSpec as P

MESH = pl.DeviceIdType.MESH
PIECES = 2


NY = 4


def _group(kind, n_red):
    r = lax.axis_index("red")
    x, y = r // NY, lax.rem(r, NY)
    if kind == "y":
        return y, NY, lambda pos: x * NY + pos
    if kind == "x":
        return x, n_red // NY, lambda pos: pos * NY + y
    return r, n_red, lambda pos: pos


def _exchange_kernel(jobs, n_in, n_out, n_red, *refs):
    ins, outs = refs[:n_in], refs[n_in:n_in + n_out]
    send_sem, recv_sem, local_sem = refs[n_in + n_out:]
    row = lax.axis_index("blk")

    barrier = pltpu.get_barrier_semaphore()
    count = 0
    for kind in sorted(set(job[0] for job in jobs)):
        me, n, red_of = _group(kind, n_red)
        for o in range(1, n):
            pl.semaphore_signal(
                barrier, inc=1, device_id=(row, red_of(lax.rem(me + o, n))), device_id_type=MESH
            )
            count += 1
    pl.semaphore_wait(barrier, count)

    def remote(j, pos, slot, piece=None):
        kind, si, src_view, di, dst_view = jobs[j]
        _, _, red_of = _group(kind, n_red)
        src, dst = src_view(ins[si], pos), dst_view(outs[di], slot)
        if piece is not None:
            size = src.shape[0] // PIECES
            src, dst = src.at[pl.ds(piece * size, size)], dst.at[pl.ds(piece * size, size)]
        return pltpu.make_async_remote_copy(
            src_ref=src,
            dst_ref=dst,
            send_sem=send_sem.at[j, pos],
            recv_sem=recv_sem.at[j, slot],
            device_id=(row, red_of(pos)),
            device_id_type=MESH,
        )

    for piece in range(PIECES):
        for j, job in enumerate(jobs):
            me, n, _ = _group(job[0], n_red)
            for o in range(1, n):
                remote(j, lax.rem(me + o, n), me, piece).start()
    for j, (kind, si, src_view, di, dst_view) in enumerate(jobs):
        me, n, _ = _group(kind, n_red)
        local = pltpu.make_async_copy(
            src_view(ins[si], me), dst_view(outs[di], me), local_sem.at[j]
        )
        local.start()
        local.wait()
    for j, job in enumerate(jobs):
        me, n, _ = _group(job[0], n_red)
        for o in range(1, n):
            g = lax.rem(me + o, n)
            remote(j, g, g).wait()


def _exchange(jobs, srcs, out_shapes, n_red, collective_id):
    nbytes = sum(s.size * s.dtype.itemsize for s in srcs)
    nmax = max(_group_size(job[0], n_red) for job in jobs)
    return pl.pallas_call(
        functools.partial(_exchange_kernel, tuple(jobs), len(srcs), len(out_shapes), n_red),
        out_shape=tuple(jax.ShapeDtypeStruct(s, d) for s, d in out_shapes),
        in_specs=[pl.BlockSpec(memory_space=pl.ANY)] * len(srcs),
        out_specs=tuple(pl.BlockSpec(memory_space=pl.ANY) for _ in out_shapes),
        scratch_shapes=[
            pltpu.SemaphoreType.DMA((len(jobs), nmax)),
            pltpu.SemaphoreType.DMA((len(jobs), nmax)),
            pltpu.SemaphoreType.DMA((len(jobs),)),
        ],
        compiler_params=pltpu.CompilerParams(collective_id=collective_id, has_side_effects=True),
        cost_estimate=pl.CostEstimate(flops=0, bytes_accessed=4 * nbytes, transcendentals=0),
    )(*srcs)


def _group_size(kind, n_red):
    return {"y": NY, "x": n_red // NY}.get(kind, n_red)


def _whole(ref, pos):
    return ref


def _slot(ref, pos):
    return ref.at[pos]


def shards(amplitudes, ladder_ints, cycle_ints, occ_energy, vir_energy, slab_index):
    slab_rows, occ_local, vir_local, virt_width = amplitudes.shape
    n_red = lax.axis_size("red")
    n_blk = lax.axis_size("blk")
    occ_all = occ_local * n_blk
    occ_red = occ_all // n_red
    n_x = n_red // NY

    swapped = jnp.transpose(amplitudes, (0, 2, 1, 3)).reshape(
        slab_rows * vir_local, occ_local * virt_width
    )
    width = swapped.shape[1]
    part = swapped.shape[0] // 2
    bf = swapped.dtype
    near_a, near_b = _exchange(
        [
            ("y", 0, lambda ref, pos: ref.at[pl.ds(0, part)], 0, _slot),
            ("x", 0, lambda ref, pos: ref.at[pl.ds(part, part)], 1, _slot),
        ],
        [swapped],
        [((NY, part, width), bf), ((n_x, part, width), bf)],
        n_red,
        0,
    )
    (gathered,) = _exchange(
        [
            ("x", 0, _whole, 0, lambda ref, slot: ref.at[slot, :, pl.ds(0, part)]),
            ("y", 1, _whole, 0, lambda ref, slot: ref.at[:, slot, pl.ds(part, part)]),
        ],
        [near_a, near_b],
        [((n_x, NY, 2 * part, width), bf)],
        n_red,
        3,
    )
    operand = gathered.reshape(n_red * slab_rows * vir_local, occ_local * virt_width)
    product = jnp.dot(operand, cycle_ints, preferred_element_type=jnp.float32)
    product = product.reshape(n_red, slab_rows * vir_local, cycle_ints.shape[1])
    cycle_own = lax.psum_scatter(product, "blk", scatter_dimension=0, tiled=True)[0]
    cycle_own = jnp.transpose(
        cycle_own.reshape(slab_rows, vir_local, occ_red, virt_width), (0, 2, 1, 3)
    )

    rows = slab_rows * occ_local
    flat = amplitudes.reshape(rows, vir_local * virt_width)
    shard_piece = lax.all_gather(flat, "blk", axis=0, tiled=False)
    product = jnp.dot(
        shard_piece.reshape(n_blk * rows, -1), ladder_ints, preferred_element_type=jnp.float32
    )
    cols = ladder_ints.shape[1]
    product = product.reshape(n_x, NY, rows, cols)
    half = rows // 2
    first_a, first_b = _exchange(
        [
            ("y", 0, lambda ref, pos: ref.at[:, pos, pl.ds(0, half)], 0, _slot),
            ("x", 0, lambda ref, pos: ref.at[pos, :, pl.ds(half, half)], 1, _slot),
        ],
        [product],
        [((NY, n_x, half, cols), jnp.float32), ((n_x, NY, half, cols), jnp.float32)],
        n_red,
        1,
    )
    second_a, second_b = _exchange(
        [("x", 0, _slot, 0, _slot), ("y", 1, _slot, 1, _slot)],
        [jnp.sum(first_a, axis=0), jnp.sum(first_b, axis=0)],
        [((n_x, half, cols), jnp.float32), ((NY, half, cols), jnp.float32)],
        n_red,
        2,
    )
    ladder_own = jnp.concatenate([jnp.sum(second_a, axis=0), jnp.sum(second_b, axis=0)], axis=0)
    ladder_own = ladder_own.reshape(slab_rows, occ_red, -1, virt_width)

    vir_block = cycle_own.shape[2]
    orbital_ids = jnp.arange(occ_energy.shape[0], dtype=jnp.int32)
    chosen = slab_index[:, None] == orbital_ids[None, :]
    slab_energy = jnp.sum(jnp.where(chosen, occ_energy[None, :], jnp.float32(0.0)), axis=1)
    pair_energy = lax.dynamic_slice_in_dim(occ_energy, lax.axis_index("red") * occ_red, occ_red)
    first_virtual = lax.dynamic_slice_in_dim(
        vir_energy, lax.axis_index("blk") * vir_block, vir_block
    )
    denominator = (
        first_virtual[None, None, :, None]
        + vir_energy[None, None, None, :]
        - slab_energy[:, None, None, None]
        - pair_energy[None, :, None, None]
    )
    return (ladder_own + cycle_own) / denominator


def solution(mesh):
    placed = (P(None, "blk", "red", None), P("red", "blk"), P("blk", "red"), P(), P(), P())
    return jax.shard_map(
        shards, mesh=mesh, in_specs=placed, out_specs=P(None, "red", "blk", None), check_vma=False
    )
```

```python
import functools

import jax
import jax.numpy as jnp
from jax import lax
from jax.experimental import pallas as pl
from jax.experimental.pallas import tpu as pltpu
from jax.sharding import PartitionSpec as P

MESH = pl.DeviceIdType.MESH
PIECES = 1


NY = 4


def _group(kind, n_red):
    r = lax.axis_index("red")
    x, y = r // NY, lax.rem(r, NY)
    if kind == "y":
        return y, NY, lambda pos: x * NY + pos
    if kind == "x":
        return x, n_red // NY, lambda pos: pos * NY + y
    return r, n_red, lambda pos: pos


def _exchange_kernel(jobs, n_in, n_out, n_red, *refs):
    ins, outs = refs[:n_in], refs[n_in:n_in + n_out]
    send_sem, recv_sem, local_sem = refs[n_in + n_out:]
    row = lax.axis_index("blk")

    barrier = pltpu.get_barrier_semaphore()
    count = 0
    for kind in sorted(set(job[0] for job in jobs)):
        me, n, red_of = _group(kind, n_red)
        for o in range(1, n):
            pl.semaphore_signal(
                barrier, inc=1, device_id=(row, red_of(lax.rem(me + o, n))), device_id_type=MESH
            )
            count += 1
    pl.semaphore_wait(barrier, count)

    def remote(j, pos, slot, piece=None):
        kind, si, src_view, di, dst_view = jobs[j]
        _, _, red_of = _group(kind, n_red)
        src, dst = src_view(ins[si], pos), dst_view(outs[di], slot)
        if piece is not None:
            size = src.shape[0] // PIECES
            src, dst = src.at[pl.ds(piece * size, size)], dst.at[pl.ds(piece * size, size)]
        return pltpu.make_async_remote_copy(
            src_ref=src,
            dst_ref=dst,
            send_sem=send_sem.at[j, pos],
            recv_sem=recv_sem.at[j, slot],
            device_id=(row, red_of(pos)),
            device_id_type=MESH,
        )

    for piece in range(PIECES):
        for j, job in enumerate(jobs):
            me, n, _ = _group(job[0], n_red)
            for o in range(1, n):
                remote(j, lax.rem(me + o, n), me, piece).start()
    for j, (kind, si, src_view, di, dst_view) in enumerate(jobs):
        me, n, _ = _group(kind, n_red)
        local = pltpu.make_async_copy(
            src_view(ins[si], me), dst_view(outs[di], me), local_sem.at[j]
        )
        local.start()
        local.wait()
    for j, job in enumerate(jobs):
        me, n, _ = _group(job[0], n_red)
        for o in range(1, n):
            g = lax.rem(me + o, n)
            remote(j, g, g).wait()


def _gather_kernel(n_red, src_ref, out_ref, send_sem, recv_sem, local_sem):
    row = lax.axis_index("blk")
    ym, ny, red_y = _group("y", n_red)
    xm, nx, red_x = _group("x", n_red)
    part = src_ref.shape[0] // 2
    first, second = pl.ds(0, part), pl.ds(part, part)

    barrier = pltpu.get_barrier_semaphore()
    for o in range(1, ny):
        pl.semaphore_signal(barrier, inc=1, device_id=(row, red_y(lax.rem(ym + o, ny))), device_id_type=MESH)
    for o in range(1, nx):
        pl.semaphore_signal(barrier, inc=1, device_id=(row, red_x(lax.rem(xm + o, nx))), device_id_type=MESH)
    pl.semaphore_wait(barrier, ny - 1 + nx - 1)

    def copy(src, dst, stage, pos, dev):
        return pltpu.make_async_remote_copy(
            src_ref=src,
            dst_ref=dst,
            send_sem=send_sem.at[stage, pos],
            recv_sem=recv_sem.at[stage, pos],
            device_id=(row, dev),
            device_id_type=MESH,
        )

    sent = []
    for o in range(1, ny):
        g = lax.rem(ym + o, ny)
        c = pltpu.make_async_remote_copy(
            src_ref=src_ref.at[first], dst_ref=out_ref.at[xm, ym, first],
            send_sem=send_sem.at[0, g], recv_sem=recv_sem.at[0, ym],
            device_id=(row, red_y(g)), device_id_type=MESH,
        )
        c.start()
        sent.append(c)
    for o in range(1, nx):
        g = lax.rem(xm + o, nx)
        c = pltpu.make_async_remote_copy(
            src_ref=src_ref.at[second], dst_ref=out_ref.at[xm, ym, second],
            send_sem=send_sem.at[1, g], recv_sem=recv_sem.at[1, xm],
            device_id=(row, red_x(g)), device_id_type=MESH,
        )
        c.start()
        sent.append(c)
    own = [
        pltpu.make_async_copy(src_ref.at[first], out_ref.at[xm, ym, first], local_sem.at[0]),
        pltpu.make_async_copy(src_ref.at[second], out_ref.at[xm, ym, second], local_sem.at[1]),
    ]
    for c in own:
        c.start()
    for c in own:
        c.wait()

    for o in range(1, ny):
        g = lax.rem(ym + o, ny)
        copy(src_ref.at[first], out_ref.at[xm, g, first], 0, g, red_y(g)).wait_recv()
    for o in range(1, nx):
        g = lax.rem(xm + o, nx)
        c = pltpu.make_async_remote_copy(
            src_ref=out_ref.at[xm, :, first], dst_ref=out_ref.at[xm, :, first],
            send_sem=send_sem.at[2, g], recv_sem=recv_sem.at[2, xm],
            device_id=(row, red_x(g)), device_id_type=MESH,
        )
        c.start()
        sent.append(c)
    for o in range(1, nx):
        g = lax.rem(xm + o, nx)
        copy(src_ref.at[second], out_ref.at[g, ym, second], 1, g, red_x(g)).wait_recv()
    for o in range(1, ny):
        g = lax.rem(ym + o, ny)
        c = pltpu.make_async_remote_copy(
            src_ref=out_ref.at[:, ym, second], dst_ref=out_ref.at[:, ym, second],
            send_sem=send_sem.at[3, g], recv_sem=recv_sem.at[3, ym],
            device_id=(row, red_y(g)), device_id_type=MESH,
        )
        c.start()
        sent.append(c)

    for c in sent:
        c.wait_send()
    for o in range(1, nx):
        g = lax.rem(xm + o, nx)
        copy(out_ref.at[g, :, first], out_ref.at[g, :, first], 2, g, red_x(g)).wait_recv()
    for o in range(1, ny):
        g = lax.rem(ym + o, ny)
        copy(out_ref.at[:, g, second], out_ref.at[:, g, second], 3, g, red_y(g)).wait_recv()


def _gather(block, n_red, collective_id):
    n_x = n_red // NY
    nbytes = block.size * block.dtype.itemsize
    return pl.pallas_call(
        functools.partial(_gather_kernel, n_red),
        out_shape=jax.ShapeDtypeStruct((n_x, NY) + block.shape, block.dtype),
        in_specs=[pl.BlockSpec(memory_space=pl.ANY)],
        out_specs=pl.BlockSpec(memory_space=pl.ANY),
        scratch_shapes=[
            pltpu.SemaphoreType.DMA((4, max(n_x, NY))),
            pltpu.SemaphoreType.DMA((4, max(n_x, NY))),
            pltpu.SemaphoreType.DMA((2,)),
        ],
        compiler_params=pltpu.CompilerParams(collective_id=collective_id, has_side_effects=True),
        cost_estimate=pl.CostEstimate(flops=0, bytes_accessed=2 * n_red * nbytes, transcendentals=0),
    )(block)


def _exchange(jobs, srcs, out_shapes, n_red, collective_id):
    nbytes = sum(s.size * s.dtype.itemsize for s in srcs)
    nmax = max(_group_size(job[0], n_red) for job in jobs)
    return pl.pallas_call(
        functools.partial(_exchange_kernel, tuple(jobs), len(srcs), len(out_shapes), n_red),
        out_shape=tuple(jax.ShapeDtypeStruct(s, d) for s, d in out_shapes),
        in_specs=[pl.BlockSpec(memory_space=pl.ANY)] * len(srcs),
        out_specs=tuple(pl.BlockSpec(memory_space=pl.ANY) for _ in out_shapes),
        scratch_shapes=[
            pltpu.SemaphoreType.DMA((len(jobs), nmax)),
            pltpu.SemaphoreType.DMA((len(jobs), nmax)),
            pltpu.SemaphoreType.DMA((len(jobs),)),
        ],
        compiler_params=pltpu.CompilerParams(collective_id=collective_id, has_side_effects=True),
        cost_estimate=pl.CostEstimate(flops=0, bytes_accessed=4 * nbytes, transcendentals=0),
    )(*srcs)


def _group_size(kind, n_red):
    return {"y": NY, "x": n_red // NY}.get(kind, n_red)


def _whole(ref, pos):
    return ref


def _slot(ref, pos):
    return ref.at[pos]


def shards(amplitudes, ladder_ints, cycle_ints, occ_energy, vir_energy, slab_index):
    slab_rows, occ_local, vir_local, virt_width = amplitudes.shape
    n_red = lax.axis_size("red")
    n_blk = lax.axis_size("blk")
    occ_all = occ_local * n_blk
    occ_red = occ_all // n_red
    n_x = n_red // NY

    swapped = jnp.transpose(amplitudes, (0, 2, 1, 3)).reshape(
        slab_rows * vir_local, occ_local * virt_width
    )
    gathered = _gather(swapped, n_red, 0)
    operand = gathered.reshape(n_red * slab_rows * vir_local, occ_local * virt_width)
    product = jnp.dot(operand, cycle_ints, preferred_element_type=jnp.float32)
    product = product.reshape(n_red, slab_rows * vir_local, cycle_ints.shape[1])
    cycle_own = lax.psum_scatter(product, "blk", scatter_dimension=0, tiled=True)[0]
    cycle_own = jnp.transpose(
        cycle_own.reshape(slab_rows, vir_local, occ_red, virt_width), (0, 2, 1, 3)
    )

    rows = slab_rows * occ_local
    flat = amplitudes.reshape(rows, vir_local * virt_width)
    shard_piece = lax.all_gather(flat, "blk", axis=0, tiled=False)
    product = jnp.dot(
        shard_piece.reshape(n_blk * rows, -1), ladder_ints, preferred_element_type=jnp.float32
    )
    cols = ladder_ints.shape[1]
    product = product.reshape(n_x, NY, rows, cols)
    half = rows // 2
    first_a, first_b = _exchange(
        [
            ("y", 0, lambda ref, pos: ref.at[:, pos, pl.ds(0, half)], 0, _slot),
            ("x", 0, lambda ref, pos: ref.at[pos, :, pl.ds(half, half)], 1, _slot),
        ],
        [product],
        [((NY, n_x, half, cols), jnp.float32), ((n_x, NY, half, cols), jnp.float32)],
        n_red,
        1,
    )
    second_a, second_b = _exchange(
        [("x", 0, _slot, 0, _slot), ("y", 1, _slot, 1, _slot)],
        [jnp.sum(first_a, axis=0), jnp.sum(first_b, axis=0)],
        [((n_x, half, cols), jnp.float32), ((NY, half, cols), jnp.float32)],
        n_red,
        2,
    )
    ladder_own = jnp.concatenate([jnp.sum(second_a, axis=0), jnp.sum(second_b, axis=0)], axis=0)
    ladder_own = ladder_own.reshape(slab_rows, occ_red, -1, virt_width)

    vir_block = cycle_own.shape[2]
    orbital_ids = jnp.arange(occ_energy.shape[0], dtype=jnp.int32)
    chosen = slab_index[:, None] == orbital_ids[None, :]
    slab_energy = jnp.sum(jnp.where(chosen, occ_energy[None, :], jnp.float32(0.0)), axis=1)
    pair_energy = lax.dynamic_slice_in_dim(occ_energy, lax.axis_index("red") * occ_red, occ_red)
    first_virtual = lax.dynamic_slice_in_dim(
        vir_energy, lax.axis_index("blk") * vir_block, vir_block
    )
    denominator = (
        first_virtual[None, None, :, None]
        + vir_energy[None, None, None, :]
        - slab_energy[:, None, None, None]
        - pair_energy[None, :, None, None]
    )
    return (ladder_own + cycle_own) / denominator


def solution(mesh):
    placed = (P(None, "blk", "red", None), P("red", "blk"), P("blk", "red"), P(), P(), P())
    return jax.shard_map(
        shards, mesh=mesh, in_specs=placed, out_specs=P(None, "red", "blk", None), check_vma=False
    )
```

```python
import functools

import jax
import jax.numpy as jnp
from jax import lax
from jax.experimental import pallas as pl
from jax.experimental.pallas import tpu as pltpu
from jax.sharding import PartitionSpec as P

MESH = pl.DeviceIdType.MESH
PIECES = 1


NY = 4


def _group(kind, n_red):
    r = lax.axis_index("red")
    x, y = r // NY, lax.rem(r, NY)
    if kind == "y":
        return y, NY, lambda pos: x * NY + pos
    if kind == "x":
        return x, n_red // NY, lambda pos: pos * NY + y
    return r, n_red, lambda pos: pos


def _exchange_kernel(jobs, n_in, n_out, n_red, *refs):
    ins, outs = refs[:n_in], refs[n_in:n_in + n_out]
    send_sem, recv_sem, local_sem = refs[n_in + n_out:]
    row = lax.axis_index("blk")

    barrier = pltpu.get_barrier_semaphore()
    count = 0
    for kind in sorted(set(job[0] for job in jobs)):
        me, n, red_of = _group(kind, n_red)
        for o in range(1, n):
            pl.semaphore_signal(
                barrier, inc=1, device_id=(row, red_of(lax.rem(me + o, n))), device_id_type=MESH
            )
            count += 1
    pl.semaphore_wait(barrier, count)

    def remote(j, pos, slot, piece=None):
        kind, si, src_view, di, dst_view = jobs[j]
        _, _, red_of = _group(kind, n_red)
        src, dst = src_view(ins[si], pos), dst_view(outs[di], slot)
        if piece is not None:
            size = src.shape[0] // PIECES
            src, dst = src.at[pl.ds(piece * size, size)], dst.at[pl.ds(piece * size, size)]
        return pltpu.make_async_remote_copy(
            src_ref=src,
            dst_ref=dst,
            send_sem=send_sem.at[j, pos],
            recv_sem=recv_sem.at[j, slot],
            device_id=(row, red_of(pos)),
            device_id_type=MESH,
        )

    for piece in range(PIECES):
        for j, job in enumerate(jobs):
            me, n, _ = _group(job[0], n_red)
            for o in range(1, n):
                remote(j, lax.rem(me + o, n), me, piece).start()
    for j, (kind, si, src_view, di, dst_view) in enumerate(jobs):
        me, n, _ = _group(kind, n_red)
        local = pltpu.make_async_copy(
            src_view(ins[si], me), dst_view(outs[di], me), local_sem.at[j]
        )
        local.start()
        local.wait()
    for j, job in enumerate(jobs):
        me, n, _ = _group(job[0], n_red)
        for o in range(1, n):
            g = lax.rem(me + o, n)
            remote(j, g, g).wait()


def _gather_kernel(n_red, src_ref, out_ref, send_sem, recv_sem, local_sem):
    row = lax.axis_index("blk")
    ym, ny, red_y = _group("y", n_red)
    xm, nx, red_x = _group("x", n_red)
    part = src_ref.shape[0] // 2
    first, second = pl.ds(0, part), pl.ds(part, part)

    barrier = pltpu.get_barrier_semaphore()
    for o in range(1, ny):
        pl.semaphore_signal(barrier, inc=1, device_id=(row, red_y(lax.rem(ym + o, ny))), device_id_type=MESH)
    for o in range(1, nx):
        pl.semaphore_signal(barrier, inc=1, device_id=(row, red_x(lax.rem(xm + o, nx))), device_id_type=MESH)
    pl.semaphore_wait(barrier, ny - 1 + nx - 1)

    def copy(src, dst, stage, pos, dev):
        return pltpu.make_async_remote_copy(
            src_ref=src,
            dst_ref=dst,
            send_sem=send_sem.at[stage, pos],
            recv_sem=recv_sem.at[stage, pos],
            device_id=(row, dev),
            device_id_type=MESH,
        )

    sent = []
    for o in range(1, ny):
        g = lax.rem(ym + o, ny)
        c = pltpu.make_async_remote_copy(
            src_ref=src_ref.at[first], dst_ref=out_ref.at[xm, ym, first],
            send_sem=send_sem.at[0, g], recv_sem=recv_sem.at[0, ym],
            device_id=(row, red_y(g)), device_id_type=MESH,
        )
        c.start()
        sent.append(c)
    for o in range(1, nx):
        g = lax.rem(xm + o, nx)
        c = pltpu.make_async_remote_copy(
            src_ref=src_ref.at[second], dst_ref=out_ref.at[xm, ym, second],
            send_sem=send_sem.at[1, g], recv_sem=recv_sem.at[1, xm],
            device_id=(row, red_x(g)), device_id_type=MESH,
        )
        c.start()
        sent.append(c)
    own = [
        pltpu.make_async_copy(src_ref.at[first], out_ref.at[xm, ym, first], local_sem.at[0]),
        pltpu.make_async_copy(src_ref.at[second], out_ref.at[xm, ym, second], local_sem.at[1]),
    ]
    for c in own:
        c.start()
    for c in own:
        c.wait()

    for o in range(1, ny):
        g = lax.rem(ym + o, ny)
        copy(src_ref.at[first], out_ref.at[xm, g, first], 0, g, red_y(g)).wait_recv()
    for o in range(1, nx):
        g = lax.rem(xm + o, nx)
        c = pltpu.make_async_remote_copy(
            src_ref=out_ref.at[xm, :, first], dst_ref=out_ref.at[xm, :, first],
            send_sem=send_sem.at[2, g], recv_sem=recv_sem.at[2, xm],
            device_id=(row, red_x(g)), device_id_type=MESH,
        )
        c.start()
        sent.append(c)
    for o in range(1, nx):
        g = lax.rem(xm + o, nx)
        copy(src_ref.at[second], out_ref.at[g, ym, second], 1, g, red_x(g)).wait_recv()
    for o in range(1, ny):
        g = lax.rem(ym + o, ny)
        c = pltpu.make_async_remote_copy(
            src_ref=out_ref.at[:, ym, second], dst_ref=out_ref.at[:, ym, second],
            send_sem=send_sem.at[3, g], recv_sem=recv_sem.at[3, ym],
            device_id=(row, red_y(g)), device_id_type=MESH,
        )
        c.start()
        sent.append(c)

    for c in sent:
        c.wait_send()
    for o in range(1, nx):
        g = lax.rem(xm + o, nx)
        copy(out_ref.at[g, :, first], out_ref.at[g, :, first], 2, g, red_x(g)).wait_recv()
    for o in range(1, ny):
        g = lax.rem(ym + o, ny)
        copy(out_ref.at[:, g, second], out_ref.at[:, g, second], 3, g, red_y(g)).wait_recv()


def _gather(block, n_red, collective_id):
    n_x = n_red // NY
    nbytes = block.size * block.dtype.itemsize
    return pl.pallas_call(
        functools.partial(_gather_kernel, n_red),
        out_shape=jax.ShapeDtypeStruct((n_x, NY) + block.shape, block.dtype),
        in_specs=[pl.BlockSpec(memory_space=pl.ANY)],
        out_specs=pl.BlockSpec(memory_space=pl.ANY),
        scratch_shapes=[
            pltpu.SemaphoreType.DMA((4, max(n_x, NY))),
            pltpu.SemaphoreType.DMA((4, max(n_x, NY))),
            pltpu.SemaphoreType.DMA((2,)),
        ],
        compiler_params=pltpu.CompilerParams(collective_id=collective_id, has_side_effects=True),
        cost_estimate=pl.CostEstimate(flops=0, bytes_accessed=2 * n_red * nbytes, transcendentals=0),
    )(block)


def _reduce_kernel(n_red, prod_ref, out_ref, ra, rb, sa, sb, qa, qb, send1, recv1, send2, recv2, local_sem):
    row = lax.axis_index("blk")
    ym, ny, red_y = _group("y", n_red)
    xm, nx, red_x = _group("x", n_red)
    half = ra.shape[2]
    first, second = pl.ds(0, half), pl.ds(half, half)

    barrier = pltpu.get_barrier_semaphore()
    for o in range(1, ny):
        pl.semaphore_signal(barrier, inc=1, device_id=(row, red_y(lax.rem(ym + o, ny))), device_id_type=MESH)
    for o in range(1, nx):
        pl.semaphore_signal(barrier, inc=1, device_id=(row, red_x(lax.rem(xm + o, nx))), device_id_type=MESH)
    pl.semaphore_wait(barrier, ny - 1 + nx - 1)

    def copy(src, dst, send, recv, dev):
        return pltpu.make_async_remote_copy(
            src_ref=src, dst_ref=dst, send_sem=send, recv_sem=recv,
            device_id=(row, dev), device_id_type=MESH,
        )

    sent = []
    for o in range(1, ny):
        g = lax.rem(ym + o, ny)
        c = copy(prod_ref.at[:, g, first], ra.at[ym], send1.at[0, g], recv1.at[0, ym], red_y(g))
        c.start()
        sent.append(c)
    for o in range(1, nx):
        g = lax.rem(xm + o, nx)
        c = copy(prod_ref.at[g, :, second], rb.at[xm], send1.at[1, g], recv1.at[1, xm], red_x(g))
        c.start()
        sent.append(c)
    own_a = pltpu.make_async_copy(prod_ref.at[:, ym, first], ra.at[ym], local_sem.at[0])
    own_b = pltpu.make_async_copy(prod_ref.at[xm, :, second], rb.at[xm], local_sem.at[1])
    own_a.start()
    own_b.start()

    own_a.wait()
    for o in range(1, ny):
        g = lax.rem(ym + o, ny)
        copy(prod_ref.at[:, g, first], ra.at[g], send1.at[0, g], recv1.at[0, g], red_y(g)).wait_recv()
    for k in range(nx):
        sa[k] = ra[0, k] + ra[1, k] + ra[2, k] + ra[3, k]
    for o in range(1, nx):
        g = lax.rem(xm + o, nx)
        c = copy(sa.at[g], qa.at[xm], send2.at[0, g], recv2.at[0, xm], red_x(g))
        c.start()
        sent.append(c)

    own_b.wait()
    for o in range(1, nx):
        g = lax.rem(xm + o, nx)
        copy(prod_ref.at[g, :, second], rb.at[g], send1.at[1, g], recv1.at[1, g], red_x(g)).wait_recv()
    for k in range(ny):
        sb[k] = rb[0, k] + rb[1, k] + rb[2, k] + rb[3, k]
    for o in range(1, ny):
        g = lax.rem(ym + o, ny)
        c = copy(sb.at[g], qb.at[ym], send2.at[1, g], recv2.at[1, ym], red_y(g))
        c.start()
        sent.append(c)

    for c in sent:
        c.wait_send()
    total_a = sa[xm]
    for o in range(1, nx):
        g = lax.rem(xm + o, nx)
        copy(sa.at[g], qa.at[g], send2.at[0, g], recv2.at[0, g], red_x(g)).wait_recv()
        total_a = total_a + qa[g]
    total_b = sb[ym]
    for o in range(1, ny):
        g = lax.rem(ym + o, ny)
        copy(sb.at[g], qb.at[g], send2.at[1, g], recv2.at[1, g], red_y(g)).wait_recv()
        total_b = total_b + qb[g]
    out_ref[first] = total_a
    out_ref[second] = total_b


def _reduce(prod, n_red, collective_id):
    n_x, n_y, rows, cols = prod.shape
    half = rows // 2
    f32 = jnp.float32
    return pl.pallas_call(
        functools.partial(_reduce_kernel, n_red),
        out_shape=jax.ShapeDtypeStruct((rows, cols), f32),
        in_specs=[pl.BlockSpec(memory_space=pl.ANY)],
        out_specs=pl.BlockSpec(memory_space=pltpu.VMEM),
        scratch_shapes=[
            pltpu.VMEM((n_y, n_x, half, cols), f32),
            pltpu.VMEM((n_x, n_y, half, cols), f32),
            pltpu.VMEM((n_x, half, cols), f32),
            pltpu.VMEM((n_y, half, cols), f32),
            pltpu.VMEM((n_x, half, cols), f32),
            pltpu.VMEM((n_y, half, cols), f32),
            pltpu.SemaphoreType.DMA((2, max(n_x, n_y))),
            pltpu.SemaphoreType.DMA((2, max(n_x, n_y))),
            pltpu.SemaphoreType.DMA((2, max(n_x, n_y))),
            pltpu.SemaphoreType.DMA((2, max(n_x, n_y))),
            pltpu.SemaphoreType.DMA((2,)),
        ],
        compiler_params=pltpu.CompilerParams(collective_id=collective_id, has_side_effects=True),
        cost_estimate=pl.CostEstimate(
            flops=prod.size, bytes_accessed=2 * prod.size * 4, transcendentals=0
        ),
    )(prod)


def _exchange(jobs, srcs, out_shapes, n_red, collective_id):
    nbytes = sum(s.size * s.dtype.itemsize for s in srcs)
    nmax = max(_group_size(job[0], n_red) for job in jobs)
    return pl.pallas_call(
        functools.partial(_exchange_kernel, tuple(jobs), len(srcs), len(out_shapes), n_red),
        out_shape=tuple(jax.ShapeDtypeStruct(s, d) for s, d in out_shapes),
        in_specs=[pl.BlockSpec(memory_space=pl.ANY)] * len(srcs),
        out_specs=tuple(pl.BlockSpec(memory_space=pl.ANY) for _ in out_shapes),
        scratch_shapes=[
            pltpu.SemaphoreType.DMA((len(jobs), nmax)),
            pltpu.SemaphoreType.DMA((len(jobs), nmax)),
            pltpu.SemaphoreType.DMA((len(jobs),)),
        ],
        compiler_params=pltpu.CompilerParams(collective_id=collective_id, has_side_effects=True),
        cost_estimate=pl.CostEstimate(flops=0, bytes_accessed=4 * nbytes, transcendentals=0),
    )(*srcs)


def _group_size(kind, n_red):
    return {"y": NY, "x": n_red // NY}.get(kind, n_red)


def _whole(ref, pos):
    return ref


def _slot(ref, pos):
    return ref.at[pos]


def shards(amplitudes, ladder_ints, cycle_ints, occ_energy, vir_energy, slab_index):
    slab_rows, occ_local, vir_local, virt_width = amplitudes.shape
    n_red = lax.axis_size("red")
    n_blk = lax.axis_size("blk")
    occ_all = occ_local * n_blk
    occ_red = occ_all // n_red
    n_x = n_red // NY

    swapped = jnp.transpose(amplitudes, (0, 2, 1, 3)).reshape(
        slab_rows * vir_local, occ_local * virt_width
    )
    gathered = _gather(swapped, n_red, 0)
    operand = gathered.reshape(n_red * slab_rows * vir_local, occ_local * virt_width)
    product = jnp.dot(operand, cycle_ints, preferred_element_type=jnp.float32)
    product = product.reshape(n_red, slab_rows * vir_local, cycle_ints.shape[1])
    cycle_own = lax.psum_scatter(product, "blk", scatter_dimension=0, tiled=True)[0]
    cycle_own = jnp.transpose(
        cycle_own.reshape(slab_rows, vir_local, occ_red, virt_width), (0, 2, 1, 3)
    )

    rows = slab_rows * occ_local
    flat = amplitudes.reshape(rows, vir_local * virt_width)
    shard_piece = lax.all_gather(flat, "blk", axis=0, tiled=False)
    product = jnp.dot(
        shard_piece.reshape(n_blk * rows, -1), ladder_ints, preferred_element_type=jnp.float32
    )
    cols = ladder_ints.shape[1]
    product = product.reshape(n_x, NY, rows, cols)
    ladder_own = _reduce(product, n_red, 1)
    ladder_own = ladder_own.reshape(slab_rows, occ_red, -1, virt_width)

    vir_block = cycle_own.shape[2]
    orbital_ids = jnp.arange(occ_energy.shape[0], dtype=jnp.int32)
    chosen = slab_index[:, None] == orbital_ids[None, :]
    slab_energy = jnp.sum(jnp.where(chosen, occ_energy[None, :], jnp.float32(0.0)), axis=1)
    pair_energy = lax.dynamic_slice_in_dim(occ_energy, lax.axis_index("red") * occ_red, occ_red)
    first_virtual = lax.dynamic_slice_in_dim(
        vir_energy, lax.axis_index("blk") * vir_block, vir_block
    )
    denominator = (
        first_virtual[None, None, :, None]
        + vir_energy[None, None, None, :]
        - slab_energy[:, None, None, None]
        - pair_energy[None, :, None, None]
    )
    return (ladder_own + cycle_own) / denominator


def solution(mesh):
    placed = (P(None, "blk", "red", None), P("red", "blk"), P("blk", "red"), P(), P(), P())
    return jax.shard_map(
        shards, mesh=mesh, in_specs=placed, out_specs=P(None, "red", "blk", None), check_vma=False
    )
```

```python
import functools

import jax
import jax.numpy as jnp
from jax import lax
from jax.experimental import pallas as pl
from jax.experimental.pallas import tpu as pltpu
from jax.sharding import Mesh, PartitionSpec as P

MESH = pl.DeviceIdType.MESH
PIECES = 1


NY = 4
CORES = 2


def _row():
    return lax.axis_index("z"), lax.axis_index("core")


def _group(kind, n_red):
    r = lax.axis_index("red")
    x, y = r // NY, lax.rem(r, NY)
    if kind == "y":
        return y, NY, lambda pos: x * NY + pos
    if kind == "x":
        return x, n_red // NY, lambda pos: pos * NY + y
    return r, n_red, lambda pos: pos


def _exchange_kernel(jobs, n_in, n_out, n_red, *refs):
    ins, outs = refs[:n_in], refs[n_in:n_in + n_out]
    send_sem, recv_sem, local_sem = refs[n_in + n_out:]
    row = _row()

    barrier = pltpu.get_barrier_semaphore()
    count = 0
    for kind in sorted(set(job[0] for job in jobs)):
        me, n, red_of = _group(kind, n_red)
        for o in range(1, n):
            pl.semaphore_signal(
                barrier, inc=1, device_id=(*row, red_of(lax.rem(me + o, n))), device_id_type=MESH
            )
            count += 1
    pl.semaphore_wait(barrier, count)

    def remote(j, pos, slot, piece=None):
        kind, si, src_view, di, dst_view = jobs[j]
        _, _, red_of = _group(kind, n_red)
        src, dst = src_view(ins[si], pos), dst_view(outs[di], slot)
        if piece is not None:
            size = src.shape[0] // PIECES
            src, dst = src.at[pl.ds(piece * size, size)], dst.at[pl.ds(piece * size, size)]
        return pltpu.make_async_remote_copy(
            src_ref=src,
            dst_ref=dst,
            send_sem=send_sem.at[j, pos],
            recv_sem=recv_sem.at[j, slot],
            device_id=(*row, red_of(pos)),
            device_id_type=MESH,
        )

    for piece in range(PIECES):
        for j, job in enumerate(jobs):
            me, n, _ = _group(job[0], n_red)
            for o in range(1, n):
                remote(j, lax.rem(me + o, n), me, piece).start()
    for j, (kind, si, src_view, di, dst_view) in enumerate(jobs):
        me, n, _ = _group(kind, n_red)
        local = pltpu.make_async_copy(
            src_view(ins[si], me), dst_view(outs[di], me), local_sem.at[j]
        )
        local.start()
        local.wait()
    for j, job in enumerate(jobs):
        me, n, _ = _group(job[0], n_red)
        for o in range(1, n):
            g = lax.rem(me + o, n)
            remote(j, g, g).wait()


def _gather_kernel(n_red, src_ref, out_ref, send_sem, recv_sem, local_sem):
    row = _row()
    ym, ny, red_y = _group("y", n_red)
    xm, nx, red_x = _group("x", n_red)
    part = src_ref.shape[0] // 2
    first, second = pl.ds(0, part), pl.ds(part, part)

    barrier = pltpu.get_barrier_semaphore()
    for o in range(1, ny):
        pl.semaphore_signal(barrier, inc=1, device_id=(*row, red_y(lax.rem(ym + o, ny))), device_id_type=MESH)
    for o in range(1, nx):
        pl.semaphore_signal(barrier, inc=1, device_id=(*row, red_x(lax.rem(xm + o, nx))), device_id_type=MESH)
    pl.semaphore_wait(barrier, ny - 1 + nx - 1)

    def copy(src, dst, stage, pos, dev):
        return pltpu.make_async_remote_copy(
            src_ref=src,
            dst_ref=dst,
            send_sem=send_sem.at[stage, pos],
            recv_sem=recv_sem.at[stage, pos],
            device_id=(*row, dev),
            device_id_type=MESH,
        )

    sent = []
    for o in range(1, ny):
        g = lax.rem(ym + o, ny)
        c = pltpu.make_async_remote_copy(
            src_ref=src_ref.at[first], dst_ref=out_ref.at[xm, ym, first],
            send_sem=send_sem.at[0, g], recv_sem=recv_sem.at[0, ym],
            device_id=(*row, red_y(g)), device_id_type=MESH,
        )
        c.start()
        sent.append(c)
    for o in range(1, nx):
        g = lax.rem(xm + o, nx)
        c = pltpu.make_async_remote_copy(
            src_ref=src_ref.at[second], dst_ref=out_ref.at[xm, ym, second],
            send_sem=send_sem.at[1, g], recv_sem=recv_sem.at[1, xm],
            device_id=(*row, red_x(g)), device_id_type=MESH,
        )
        c.start()
        sent.append(c)
    own = [
        pltpu.make_async_copy(src_ref.at[first], out_ref.at[xm, ym, first], local_sem.at[0]),
        pltpu.make_async_copy(src_ref.at[second], out_ref.at[xm, ym, second], local_sem.at[1]),
    ]
    for c in own:
        c.start()
    for c in own:
        c.wait()

    for o in range(1, ny):
        g = lax.rem(ym + o, ny)
        copy(src_ref.at[first], out_ref.at[xm, g, first], 0, g, red_y(g)).wait_recv()
    for o in range(1, nx):
        g = lax.rem(xm + o, nx)
        c = pltpu.make_async_remote_copy(
            src_ref=out_ref.at[xm, :, first], dst_ref=out_ref.at[xm, :, first],
            send_sem=send_sem.at[2, g], recv_sem=recv_sem.at[2, xm],
            device_id=(*row, red_x(g)), device_id_type=MESH,
        )
        c.start()
        sent.append(c)
    for o in range(1, nx):
        g = lax.rem(xm + o, nx)
        copy(src_ref.at[second], out_ref.at[g, ym, second], 1, g, red_x(g)).wait_recv()
    for o in range(1, ny):
        g = lax.rem(ym + o, ny)
        c = pltpu.make_async_remote_copy(
            src_ref=out_ref.at[:, ym, second], dst_ref=out_ref.at[:, ym, second],
            send_sem=send_sem.at[3, g], recv_sem=recv_sem.at[3, ym],
            device_id=(*row, red_y(g)), device_id_type=MESH,
        )
        c.start()
        sent.append(c)

    for c in sent:
        c.wait_send()
    for o in range(1, nx):
        g = lax.rem(xm + o, nx)
        copy(out_ref.at[g, :, first], out_ref.at[g, :, first], 2, g, red_x(g)).wait_recv()
    for o in range(1, ny):
        g = lax.rem(ym + o, ny)
        copy(out_ref.at[:, g, second], out_ref.at[:, g, second], 3, g, red_y(g)).wait_recv()


def _gather(block, n_red, collective_id):
    n_x = n_red // NY
    nbytes = block.size * block.dtype.itemsize
    return pl.pallas_call(
        functools.partial(_gather_kernel, n_red),
        out_shape=jax.ShapeDtypeStruct((n_x, NY) + block.shape, block.dtype),
        in_specs=[pl.BlockSpec(memory_space=pl.ANY)],
        out_specs=pl.BlockSpec(memory_space=pl.ANY),
        scratch_shapes=[
            pltpu.SemaphoreType.DMA((4, max(n_x, NY))),
            pltpu.SemaphoreType.DMA((4, max(n_x, NY))),
            pltpu.SemaphoreType.DMA((2,)),
        ],
        compiler_params=pltpu.CompilerParams(collective_id=collective_id, has_side_effects=True),
        cost_estimate=pl.CostEstimate(flops=0, bytes_accessed=2 * n_red * nbytes, transcendentals=0),
    )(block)


def _reduce_kernel(n_red, prod_ref, out_ref, ra, rb, sa, sb, qa, qb, send1, recv1, send2, recv2, local_sem):
    row = _row()
    ym, ny, red_y = _group("y", n_red)
    xm, nx, red_x = _group("x", n_red)
    half = ra.shape[2]
    first, second = pl.ds(0, half), pl.ds(half, half)

    barrier = pltpu.get_barrier_semaphore()
    for o in range(1, ny):
        pl.semaphore_signal(barrier, inc=1, device_id=(*row, red_y(lax.rem(ym + o, ny))), device_id_type=MESH)
    for o in range(1, nx):
        pl.semaphore_signal(barrier, inc=1, device_id=(*row, red_x(lax.rem(xm + o, nx))), device_id_type=MESH)
    pl.semaphore_wait(barrier, ny - 1 + nx - 1)

    def copy(src, dst, send, recv, dev):
        return pltpu.make_async_remote_copy(
            src_ref=src, dst_ref=dst, send_sem=send, recv_sem=recv,
            device_id=(*row, dev), device_id_type=MESH,
        )

    sent = []
    for o in range(1, ny):
        g = lax.rem(ym + o, ny)
        c = copy(prod_ref.at[:, g, first], ra.at[ym], send1.at[0, g], recv1.at[0, ym], red_y(g))
        c.start()
        sent.append(c)
    for o in range(1, nx):
        g = lax.rem(xm + o, nx)
        c = copy(prod_ref.at[g, :, second], rb.at[xm], send1.at[1, g], recv1.at[1, xm], red_x(g))
        c.start()
        sent.append(c)
    own_a = pltpu.make_async_copy(prod_ref.at[:, ym, first], ra.at[ym], local_sem.at[0])
    own_b = pltpu.make_async_copy(prod_ref.at[xm, :, second], rb.at[xm], local_sem.at[1])
    own_a.start()
    own_b.start()

    own_a.wait()
    for o in range(1, ny):
        g = lax.rem(ym + o, ny)
        copy(prod_ref.at[:, g, first], ra.at[g], send1.at[0, g], recv1.at[0, g], red_y(g)).wait_recv()
    for k in range(nx):
        sa[k] = ra[0, k] + ra[1, k] + ra[2, k] + ra[3, k]
    for o in range(1, nx):
        g = lax.rem(xm + o, nx)
        c = copy(sa.at[g], qa.at[xm], send2.at[0, g], recv2.at[0, xm], red_x(g))
        c.start()
        sent.append(c)

    own_b.wait()
    for o in range(1, nx):
        g = lax.rem(xm + o, nx)
        copy(prod_ref.at[g, :, second], rb.at[g], send1.at[1, g], recv1.at[1, g], red_x(g)).wait_recv()
    for k in range(ny):
        sb[k] = rb[0, k] + rb[1, k] + rb[2, k] + rb[3, k]
    for o in range(1, ny):
        g = lax.rem(ym + o, ny)
        c = copy(sb.at[g], qb.at[ym], send2.at[1, g], recv2.at[1, ym], red_y(g))
        c.start()
        sent.append(c)

    for c in sent:
        c.wait_send()
    total_a = sa[xm]
    for o in range(1, nx):
        g = lax.rem(xm + o, nx)
        copy(sa.at[g], qa.at[g], send2.at[0, g], recv2.at[0, g], red_x(g)).wait_recv()
        total_a = total_a + qa[g]
    total_b = sb[ym]
    for o in range(1, ny):
        g = lax.rem(ym + o, ny)
        copy(sb.at[g], qb.at[g], send2.at[1, g], recv2.at[1, g], red_y(g)).wait_recv()
        total_b = total_b + qb[g]
    out_ref[first] = total_a
    out_ref[second] = total_b


def _reduce(prod, n_red, collective_id):
    n_x, n_y, rows, cols = prod.shape
    half = rows // 2
    f32 = jnp.float32
    return pl.pallas_call(
        functools.partial(_reduce_kernel, n_red),
        out_shape=jax.ShapeDtypeStruct((rows, cols), f32),
        in_specs=[pl.BlockSpec(memory_space=pl.ANY)],
        out_specs=pl.BlockSpec(memory_space=pltpu.VMEM),
        scratch_shapes=[
            pltpu.VMEM((n_y, n_x, half, cols), f32),
            pltpu.VMEM((n_x, n_y, half, cols), f32),
            pltpu.VMEM((n_x, half, cols), f32),
            pltpu.VMEM((n_y, half, cols), f32),
            pltpu.VMEM((n_x, half, cols), f32),
            pltpu.VMEM((n_y, half, cols), f32),
            pltpu.SemaphoreType.DMA((2, max(n_x, n_y))),
            pltpu.SemaphoreType.DMA((2, max(n_x, n_y))),
            pltpu.SemaphoreType.DMA((2, max(n_x, n_y))),
            pltpu.SemaphoreType.DMA((2, max(n_x, n_y))),
            pltpu.SemaphoreType.DMA((2,)),
        ],
        compiler_params=pltpu.CompilerParams(collective_id=collective_id, has_side_effects=True),
        cost_estimate=pl.CostEstimate(
            flops=prod.size, bytes_accessed=2 * prod.size * 4, transcendentals=0
        ),
    )(prod)


def _exchange(jobs, srcs, out_shapes, n_red, collective_id):
    nbytes = sum(s.size * s.dtype.itemsize for s in srcs)
    nmax = max(_group_size(job[0], n_red) for job in jobs)
    return pl.pallas_call(
        functools.partial(_exchange_kernel, tuple(jobs), len(srcs), len(out_shapes), n_red),
        out_shape=tuple(jax.ShapeDtypeStruct(s, d) for s, d in out_shapes),
        in_specs=[pl.BlockSpec(memory_space=pl.ANY)] * len(srcs),
        out_specs=tuple(pl.BlockSpec(memory_space=pl.ANY) for _ in out_shapes),
        scratch_shapes=[
            pltpu.SemaphoreType.DMA((len(jobs), nmax)),
            pltpu.SemaphoreType.DMA((len(jobs), nmax)),
            pltpu.SemaphoreType.DMA((len(jobs),)),
        ],
        compiler_params=pltpu.CompilerParams(collective_id=collective_id, has_side_effects=True),
        cost_estimate=pl.CostEstimate(flops=0, bytes_accessed=4 * nbytes, transcendentals=0),
    )(*srcs)


def _group_size(kind, n_red):
    return {"y": NY, "x": n_red // NY}.get(kind, n_red)


def _whole(ref, pos):
    return ref


def _slot(ref, pos):
    return ref.at[pos]


def shards(amplitudes, ladder_ints, cycle_ints, occ_energy, vir_energy, slab_index):
    slab_rows, occ_local, vir_local, virt_width = amplitudes.shape
    n_red = lax.axis_size("red")
    n_blk = lax.axis_size("z") * lax.axis_size("core")
    occ_all = occ_local * n_blk
    occ_red = occ_all // n_red
    n_x = n_red // NY

    swapped = jnp.transpose(amplitudes, (0, 2, 1, 3)).reshape(
        slab_rows * vir_local, occ_local * virt_width
    )
    gathered = _gather(swapped, n_red, 0)
    operand = gathered.reshape(n_red * slab_rows * vir_local, occ_local * virt_width)
    product = jnp.dot(operand, cycle_ints, preferred_element_type=jnp.float32)
    product = product.reshape(n_blk // CORES, CORES, slab_rows * vir_local, cycle_ints.shape[1])
    core = lax.axis_index("core")
    theirs = lax.dynamic_index_in_dim(product, CORES - 1 - core, axis=1, keepdims=False)
    mine = lax.dynamic_index_in_dim(product, core, axis=1, keepdims=False)
    product = mine + lax.ppermute(theirs, "core", [(0, 1), (1, 0)])
    cycle_own = lax.psum_scatter(product, "z", scatter_dimension=0, tiled=True)[0]
    cycle_own = jnp.transpose(
        cycle_own.reshape(slab_rows, vir_local, occ_red, virt_width), (0, 2, 1, 3)
    )

    rows = slab_rows * occ_local
    flat = amplitudes.reshape(rows, vir_local * virt_width)
    shard_piece = lax.all_gather(flat, "z", axis=0, tiled=False)
    shard_piece = lax.all_gather(shard_piece, "core", axis=1, tiled=False)
    product = jnp.dot(
        shard_piece.reshape(n_blk * rows, -1), ladder_ints, preferred_element_type=jnp.float32
    )
    cols = ladder_ints.shape[1]
    product = product.reshape(n_x, NY, rows, cols)
    ladder_own = _reduce(product, n_red, 1)
    ladder_own = ladder_own.reshape(slab_rows, occ_red, -1, virt_width)

    vir_block = cycle_own.shape[2]
    orbital_ids = jnp.arange(occ_energy.shape[0], dtype=jnp.int32)
    chosen = slab_index[:, None] == orbital_ids[None, :]
    slab_energy = jnp.sum(jnp.where(chosen, occ_energy[None, :], jnp.float32(0.0)), axis=1)
    pair_energy = lax.dynamic_slice_in_dim(occ_energy, lax.axis_index("red") * occ_red, occ_red)
    first_virtual = lax.dynamic_slice_in_dim(
        vir_energy, (lax.axis_index("z") * CORES + lax.axis_index("core")) * vir_block, vir_block
    )
    denominator = (
        first_virtual[None, None, :, None]
        + vir_energy[None, None, None, :]
        - slab_energy[:, None, None, None]
        - pair_energy[None, :, None, None]
    )
    return (ladder_own + cycle_own) / denominator


def solution(mesh):
    blk = ("z", "core")
    split = Mesh(
        mesh.devices.reshape(mesh.shape["blk"] // CORES, CORES, mesh.shape["red"]),
        ("z", "core", "red"),
    )
    placed = (P(None, blk, "red", None), P("red", blk), P(blk, "red"), P(), P(), P())
    return jax.shard_map(
        shards, mesh=split, in_specs=placed, out_specs=P(None, "red", blk, None), check_vma=False
    )
```

```python
import functools

import jax
import jax.numpy as jnp
from jax import lax
from jax.experimental import pallas as pl
from jax.experimental.pallas import tpu as pltpu
from jax.sharding import Mesh, PartitionSpec as P

MESH = pl.DeviceIdType.MESH
PIECES = 1


NY = 4
CORES = 2


def _row():
    return lax.axis_index("z"), lax.axis_index("core")


def _group(kind, n_red):
    r = lax.axis_index("red")
    x, y = r // NY, lax.rem(r, NY)
    if kind == "y":
        return y, NY, lambda pos: x * NY + pos
    if kind == "x":
        return x, n_red // NY, lambda pos: pos * NY + y
    return r, n_red, lambda pos: pos


def _exchange_kernel(jobs, n_in, n_out, n_red, *refs):
    ins, outs = refs[:n_in], refs[n_in:n_in + n_out]
    send_sem, recv_sem, local_sem = refs[n_in + n_out:]
    row = _row()

    barrier = pltpu.get_barrier_semaphore()
    count = 0
    for kind in sorted(set(job[0] for job in jobs)):
        me, n, red_of = _group(kind, n_red)
        for o in range(1, n):
            pl.semaphore_signal(
                barrier, inc=1, device_id=(*row, red_of(lax.rem(me + o, n))), device_id_type=MESH
            )
            count += 1
    pl.semaphore_wait(barrier, count)

    def remote(j, pos, slot, piece=None):
        kind, si, src_view, di, dst_view = jobs[j]
        _, _, red_of = _group(kind, n_red)
        src, dst = src_view(ins[si], pos), dst_view(outs[di], slot)
        if piece is not None:
            size = src.shape[0] // PIECES
            src, dst = src.at[pl.ds(piece * size, size)], dst.at[pl.ds(piece * size, size)]
        return pltpu.make_async_remote_copy(
            src_ref=src,
            dst_ref=dst,
            send_sem=send_sem.at[j, pos],
            recv_sem=recv_sem.at[j, slot],
            device_id=(*row, red_of(pos)),
            device_id_type=MESH,
        )

    for piece in range(PIECES):
        for j, job in enumerate(jobs):
            me, n, _ = _group(job[0], n_red)
            for o in range(1, n):
                remote(j, lax.rem(me + o, n), me, piece).start()
    for j, (kind, si, src_view, di, dst_view) in enumerate(jobs):
        me, n, _ = _group(kind, n_red)
        local = pltpu.make_async_copy(
            src_view(ins[si], me), dst_view(outs[di], me), local_sem.at[j]
        )
        local.start()
        local.wait()
    for j, job in enumerate(jobs):
        me, n, _ = _group(job[0], n_red)
        for o in range(1, n):
            g = lax.rem(me + o, n)
            remote(j, g, g).wait()


def _gather_kernel(n_red, src_ref, out_ref, send_sem, recv_sem, local_sem):
    row = _row()
    ym, ny, red_y = _group("y", n_red)
    xm, nx, red_x = _group("x", n_red)
    part = src_ref.shape[0] // 2
    first, second = pl.ds(0, part), pl.ds(part, part)

    barrier = pltpu.get_barrier_semaphore()
    for o in range(1, ny):
        pl.semaphore_signal(barrier, inc=1, device_id=(*row, red_y(lax.rem(ym + o, ny))), device_id_type=MESH)
    for o in range(1, nx):
        pl.semaphore_signal(barrier, inc=1, device_id=(*row, red_x(lax.rem(xm + o, nx))), device_id_type=MESH)
    pl.semaphore_wait(barrier, ny - 1 + nx - 1)

    def copy(src, dst, stage, pos, dev):
        return pltpu.make_async_remote_copy(
            src_ref=src,
            dst_ref=dst,
            send_sem=send_sem.at[stage, pos],
            recv_sem=recv_sem.at[stage, pos],
            device_id=(*row, dev),
            device_id_type=MESH,
        )

    sent = []
    for o in range(1, ny):
        g = lax.rem(ym + o, ny)
        c = pltpu.make_async_remote_copy(
            src_ref=src_ref.at[first], dst_ref=out_ref.at[xm, ym, first],
            send_sem=send_sem.at[0, g], recv_sem=recv_sem.at[0, ym],
            device_id=(*row, red_y(g)), device_id_type=MESH,
        )
        c.start()
        sent.append(c)
    for o in range(1, nx):
        g = lax.rem(xm + o, nx)
        c = pltpu.make_async_remote_copy(
            src_ref=src_ref.at[second], dst_ref=out_ref.at[xm, ym, second],
            send_sem=send_sem.at[1, g], recv_sem=recv_sem.at[1, xm],
            device_id=(*row, red_x(g)), device_id_type=MESH,
        )
        c.start()
        sent.append(c)
    own = [
        pltpu.make_async_copy(src_ref.at[first], out_ref.at[xm, ym, first], local_sem.at[0]),
        pltpu.make_async_copy(src_ref.at[second], out_ref.at[xm, ym, second], local_sem.at[1]),
    ]
    for c in own:
        c.start()
    for c in own:
        c.wait()

    for o in range(1, ny):
        g = lax.rem(ym + o, ny)
        copy(src_ref.at[first], out_ref.at[xm, g, first], 0, g, red_y(g)).wait_recv()
    for o in range(1, nx):
        g = lax.rem(xm + o, nx)
        c = pltpu.make_async_remote_copy(
            src_ref=out_ref.at[xm, :, first], dst_ref=out_ref.at[xm, :, first],
            send_sem=send_sem.at[2, g], recv_sem=recv_sem.at[2, xm],
            device_id=(*row, red_x(g)), device_id_type=MESH,
        )
        c.start()
        sent.append(c)
    for o in range(1, nx):
        g = lax.rem(xm + o, nx)
        copy(src_ref.at[second], out_ref.at[g, ym, second], 1, g, red_x(g)).wait_recv()
    for o in range(1, ny):
        g = lax.rem(ym + o, ny)
        c = pltpu.make_async_remote_copy(
            src_ref=out_ref.at[:, ym, second], dst_ref=out_ref.at[:, ym, second],
            send_sem=send_sem.at[3, g], recv_sem=recv_sem.at[3, ym],
            device_id=(*row, red_y(g)), device_id_type=MESH,
        )
        c.start()
        sent.append(c)

    for c in sent:
        c.wait_send()
    for o in range(1, nx):
        g = lax.rem(xm + o, nx)
        copy(out_ref.at[g, :, first], out_ref.at[g, :, first], 2, g, red_x(g)).wait_recv()
    for o in range(1, ny):
        g = lax.rem(ym + o, ny)
        copy(out_ref.at[:, g, second], out_ref.at[:, g, second], 3, g, red_y(g)).wait_recv()


def _gather(block, n_red, collective_id):
    n_x = n_red // NY
    nbytes = block.size * block.dtype.itemsize
    return pl.pallas_call(
        functools.partial(_gather_kernel, n_red),
        out_shape=jax.ShapeDtypeStruct((n_x, NY) + block.shape, block.dtype),
        in_specs=[pl.BlockSpec(memory_space=pl.ANY)],
        out_specs=pl.BlockSpec(memory_space=pl.ANY),
        scratch_shapes=[
            pltpu.SemaphoreType.DMA((4, max(n_x, NY))),
            pltpu.SemaphoreType.DMA((4, max(n_x, NY))),
            pltpu.SemaphoreType.DMA((2,)),
        ],
        compiler_params=pltpu.CompilerParams(collective_id=collective_id, has_side_effects=True),
        cost_estimate=pl.CostEstimate(flops=0, bytes_accessed=2 * n_red * nbytes, transcendentals=0),
    )(block)


def _reduce_kernel(n_red, prod_ref, out_ref, ra, rb, sa, sb, qa, qb, send1, recv1, send2, recv2, local_sem):
    row = _row()
    ym, ny, red_y = _group("y", n_red)
    xm, nx, red_x = _group("x", n_red)
    half = ra.shape[2]
    first, second = pl.ds(0, half), pl.ds(half, half)

    barrier = pltpu.get_barrier_semaphore()
    for o in range(1, ny):
        pl.semaphore_signal(barrier, inc=1, device_id=(*row, red_y(lax.rem(ym + o, ny))), device_id_type=MESH)
    for o in range(1, nx):
        pl.semaphore_signal(barrier, inc=1, device_id=(*row, red_x(lax.rem(xm + o, nx))), device_id_type=MESH)
    pl.semaphore_wait(barrier, ny - 1 + nx - 1)

    def copy(src, dst, send, recv, dev):
        return pltpu.make_async_remote_copy(
            src_ref=src, dst_ref=dst, send_sem=send, recv_sem=recv,
            device_id=(*row, dev), device_id_type=MESH,
        )

    sent = []
    for o in range(1, ny):
        g = lax.rem(ym + o, ny)
        c = copy(prod_ref.at[:, g, first], ra.at[ym], send1.at[0, g], recv1.at[0, ym], red_y(g))
        c.start()
        sent.append(c)
    for o in range(1, nx):
        g = lax.rem(xm + o, nx)
        c = copy(prod_ref.at[g, :, second], rb.at[xm], send1.at[1, g], recv1.at[1, xm], red_x(g))
        c.start()
        sent.append(c)
    own_a = pltpu.make_async_copy(prod_ref.at[:, ym, first], ra.at[ym], local_sem.at[0])
    own_b = pltpu.make_async_copy(prod_ref.at[xm, :, second], rb.at[xm], local_sem.at[1])
    own_a.start()
    own_b.start()

    own_a.wait()
    for o in range(1, ny):
        g = lax.rem(ym + o, ny)
        copy(prod_ref.at[:, g, first], ra.at[g], send1.at[0, g], recv1.at[0, g], red_y(g)).wait_recv()
    for k in range(nx):
        sa[k] = ra[0, k] + ra[1, k] + ra[2, k] + ra[3, k]
    for o in range(1, nx):
        g = lax.rem(xm + o, nx)
        c = copy(sa.at[g], qa.at[xm], send2.at[0, g], recv2.at[0, xm], red_x(g))
        c.start()
        sent.append(c)

    own_b.wait()
    for o in range(1, nx):
        g = lax.rem(xm + o, nx)
        copy(prod_ref.at[g, :, second], rb.at[g], send1.at[1, g], recv1.at[1, g], red_x(g)).wait_recv()
    for k in range(ny):
        sb[k] = rb[0, k] + rb[1, k] + rb[2, k] + rb[3, k]
    for o in range(1, ny):
        g = lax.rem(ym + o, ny)
        c = copy(sb.at[g], qb.at[ym], send2.at[1, g], recv2.at[1, ym], red_y(g))
        c.start()
        sent.append(c)

    for c in sent:
        c.wait_send()
    total_a = sa[xm]
    for o in range(1, nx):
        g = lax.rem(xm + o, nx)
        copy(sa.at[g], qa.at[g], send2.at[0, g], recv2.at[0, g], red_x(g)).wait_recv()
        total_a = total_a + qa[g]
    total_b = sb[ym]
    for o in range(1, ny):
        g = lax.rem(ym + o, ny)
        copy(sb.at[g], qb.at[g], send2.at[1, g], recv2.at[1, g], red_y(g)).wait_recv()
        total_b = total_b + qb[g]
    out_ref[first] = total_a
    out_ref[second] = total_b


def _reduce(prod, n_red, collective_id):
    n_x, n_y, rows, cols = prod.shape
    half = rows // 2
    f32 = jnp.float32
    return pl.pallas_call(
        functools.partial(_reduce_kernel, n_red),
        out_shape=jax.ShapeDtypeStruct((rows, cols), f32),
        in_specs=[pl.BlockSpec(memory_space=pl.ANY)],
        out_specs=pl.BlockSpec(memory_space=pltpu.VMEM),
        scratch_shapes=[
            pltpu.VMEM((n_y, n_x, half, cols), f32),
            pltpu.VMEM((n_x, n_y, half, cols), f32),
            pltpu.VMEM((n_x, half, cols), f32),
            pltpu.VMEM((n_y, half, cols), f32),
            pltpu.VMEM((n_x, half, cols), f32),
            pltpu.VMEM((n_y, half, cols), f32),
            pltpu.SemaphoreType.DMA((2, max(n_x, n_y))),
            pltpu.SemaphoreType.DMA((2, max(n_x, n_y))),
            pltpu.SemaphoreType.DMA((2, max(n_x, n_y))),
            pltpu.SemaphoreType.DMA((2, max(n_x, n_y))),
            pltpu.SemaphoreType.DMA((2,)),
        ],
        compiler_params=pltpu.CompilerParams(collective_id=collective_id, has_side_effects=True),
        cost_estimate=pl.CostEstimate(
            flops=prod.size, bytes_accessed=2 * prod.size * 4, transcendentals=0
        ),
    )(prod)


def _core_reduce_kernel(prod_ref, out_ref, theirs, mine, send_sem, recv_sem, local_sem):
    z, core = _row()
    red = lax.axis_index("red")
    other = CORES - 1 - core
    barrier = pltpu.get_barrier_semaphore()
    pl.semaphore_signal(barrier, inc=1, device_id=(z, other, red), device_id_type=MESH)
    pl.semaphore_wait(barrier, 1)
    send = pltpu.make_async_remote_copy(
        src_ref=prod_ref.at[:, other], dst_ref=theirs, send_sem=send_sem, recv_sem=recv_sem,
        device_id=(z, other, red), device_id_type=MESH,
    )
    send.start()
    own = pltpu.make_async_copy(prod_ref.at[:, core], mine, local_sem)
    own.start()
    own.wait()
    send.wait()
    for k in range(out_ref.shape[0]):
        out_ref[k] = mine[k] + theirs[k]


def _core_reduce(prod, collective_id):
    n_z, _, rows, cols = prod.shape
    f32 = jnp.float32
    return pl.pallas_call(
        _core_reduce_kernel,
        out_shape=jax.ShapeDtypeStruct((n_z, rows, cols), f32),
        in_specs=[pl.BlockSpec(memory_space=pl.ANY)],
        out_specs=pl.BlockSpec(memory_space=pltpu.VMEM),
        scratch_shapes=[
            pltpu.VMEM((n_z, rows, cols), f32),
            pltpu.VMEM((n_z, rows, cols), f32),
            pltpu.SemaphoreType.DMA,
            pltpu.SemaphoreType.DMA,
            pltpu.SemaphoreType.DMA,
        ],
        compiler_params=pltpu.CompilerParams(collective_id=collective_id, has_side_effects=True),
        cost_estimate=pl.CostEstimate(
            flops=prod.size // 2, bytes_accessed=prod.size * 4, transcendentals=0
        ),
    )(prod)


def _exchange(jobs, srcs, out_shapes, n_red, collective_id):
    nbytes = sum(s.size * s.dtype.itemsize for s in srcs)
    nmax = max(_group_size(job[0], n_red) for job in jobs)
    return pl.pallas_call(
        functools.partial(_exchange_kernel, tuple(jobs), len(srcs), len(out_shapes), n_red),
        out_shape=tuple(jax.ShapeDtypeStruct(s, d) for s, d in out_shapes),
        in_specs=[pl.BlockSpec(memory_space=pl.ANY)] * len(srcs),
        out_specs=tuple(pl.BlockSpec(memory_space=pl.ANY) for _ in out_shapes),
        scratch_shapes=[
            pltpu.SemaphoreType.DMA((len(jobs), nmax)),
            pltpu.SemaphoreType.DMA((len(jobs), nmax)),
            pltpu.SemaphoreType.DMA((len(jobs),)),
        ],
        compiler_params=pltpu.CompilerParams(collective_id=collective_id, has_side_effects=True),
        cost_estimate=pl.CostEstimate(flops=0, bytes_accessed=4 * nbytes, transcendentals=0),
    )(*srcs)


def _group_size(kind, n_red):
    return {"y": NY, "x": n_red // NY}.get(kind, n_red)


def _whole(ref, pos):
    return ref


def _slot(ref, pos):
    return ref.at[pos]


def shards(amplitudes, ladder_ints, cycle_ints, occ_energy, vir_energy, slab_index):
    slab_rows, occ_local, vir_local, virt_width = amplitudes.shape
    n_red = lax.axis_size("red")
    n_blk = lax.axis_size("z") * lax.axis_size("core")
    occ_all = occ_local * n_blk
    occ_red = occ_all // n_red
    n_x = n_red // NY

    swapped = jnp.transpose(amplitudes, (0, 2, 1, 3)).reshape(
        slab_rows * vir_local, occ_local * virt_width
    )
    gathered = _gather(swapped, n_red, 0)
    operand = gathered.reshape(n_red * slab_rows * vir_local, occ_local * virt_width)
    product = jnp.dot(operand, cycle_ints, preferred_element_type=jnp.float32)
    product = product.reshape(n_blk // CORES, CORES, slab_rows * vir_local, cycle_ints.shape[1])
    product = _core_reduce(product, 4)
    cycle_own = lax.psum_scatter(product, "z", scatter_dimension=0, tiled=True)[0]
    cycle_own = jnp.transpose(
        cycle_own.reshape(slab_rows, vir_local, occ_red, virt_width), (0, 2, 1, 3)
    )

    rows = slab_rows * occ_local
    flat = amplitudes.reshape(rows, vir_local * virt_width)
    shard_piece = lax.all_gather(flat, ("z", "core"), axis=0, tiled=False)
    product = jnp.dot(
        shard_piece.reshape(n_blk * rows, -1), ladder_ints, preferred_element_type=jnp.float32
    )
    cols = ladder_ints.shape[1]
    product = product.reshape(n_x, NY, rows, cols)
    ladder_own = _reduce(product, n_red, 1)
    ladder_own = ladder_own.reshape(slab_rows, occ_red, -1, virt_width)

    vir_block = cycle_own.shape[2]
    orbital_ids = jnp.arange(occ_energy.shape[0], dtype=jnp.int32)
    chosen = slab_index[:, None] == orbital_ids[None, :]
    slab_energy = jnp.sum(jnp.where(chosen, occ_energy[None, :], jnp.float32(0.0)), axis=1)
    pair_energy = lax.dynamic_slice_in_dim(occ_energy, lax.axis_index("red") * occ_red, occ_red)
    first_virtual = lax.dynamic_slice_in_dim(
        vir_energy, (lax.axis_index("z") * CORES + lax.axis_index("core")) * vir_block, vir_block
    )
    denominator = (
        first_virtual[None, None, :, None]
        + vir_energy[None, None, None, :]
        - slab_energy[:, None, None, None]
        - pair_energy[None, :, None, None]
    )
    return (ladder_own + cycle_own) / denominator


def solution(mesh):
    blk = ("z", "core")
    split = Mesh(
        mesh.devices.reshape(mesh.shape["blk"] // CORES, CORES, mesh.shape["red"]),
        ("z", "core", "red"),
    )
    placed = (P(None, blk, "red", None), P("red", blk), P(blk, "red"), P(), P(), P())
    return jax.shard_map(
        shards, mesh=split, in_specs=placed, out_specs=P(None, "red", blk, None), check_vma=False
    )
```

```python
import functools

import jax
import jax.numpy as jnp
from jax import lax
from jax.experimental import pallas as pl
from jax.experimental.pallas import tpu as pltpu
from jax.sharding import Mesh, PartitionSpec as P

MESH = pl.DeviceIdType.MESH
PIECES = 1


NY = 4
CORES = 2


def _row():
    return lax.axis_index("z"), lax.axis_index("core")


def _group(kind, n_red):
    r = lax.axis_index("red")
    x, y = r // NY, lax.rem(r, NY)
    if kind == "y":
        return y, NY, lambda pos: x * NY + pos
    if kind == "x":
        return x, n_red // NY, lambda pos: pos * NY + y
    return r, n_red, lambda pos: pos


def _exchange_kernel(jobs, n_in, n_out, n_red, *refs):
    ins, outs = refs[:n_in], refs[n_in:n_in + n_out]
    send_sem, recv_sem, local_sem = refs[n_in + n_out:]
    row = _row()

    barrier = pltpu.get_barrier_semaphore()
    count = 0
    for kind in sorted(set(job[0] for job in jobs)):
        me, n, red_of = _group(kind, n_red)
        for o in range(1, n):
            pl.semaphore_signal(
                barrier, inc=1, device_id=(*row, red_of(lax.rem(me + o, n))), device_id_type=MESH
            )
            count += 1
    pl.semaphore_wait(barrier, count)

    def remote(j, pos, slot, piece=None):
        kind, si, src_view, di, dst_view = jobs[j]
        _, _, red_of = _group(kind, n_red)
        src, dst = src_view(ins[si], pos), dst_view(outs[di], slot)
        if piece is not None:
            size = src.shape[0] // PIECES
            src, dst = src.at[pl.ds(piece * size, size)], dst.at[pl.ds(piece * size, size)]
        return pltpu.make_async_remote_copy(
            src_ref=src,
            dst_ref=dst,
            send_sem=send_sem.at[j, pos],
            recv_sem=recv_sem.at[j, slot],
            device_id=(*row, red_of(pos)),
            device_id_type=MESH,
        )

    for piece in range(PIECES):
        for j, job in enumerate(jobs):
            me, n, _ = _group(job[0], n_red)
            for o in range(1, n):
                remote(j, lax.rem(me + o, n), me, piece).start()
    for j, (kind, si, src_view, di, dst_view) in enumerate(jobs):
        me, n, _ = _group(kind, n_red)
        local = pltpu.make_async_copy(
            src_view(ins[si], me), dst_view(outs[di], me), local_sem.at[j]
        )
        local.start()
        local.wait()
    for j, job in enumerate(jobs):
        me, n, _ = _group(job[0], n_red)
        for o in range(1, n):
            g = lax.rem(me + o, n)
            remote(j, g, g).wait()


def _gather_kernel(n_red, src_ref, out_ref, send_sem, recv_sem, local_sem):
    row = _row()
    ym, ny, red_y = _group("y", n_red)
    xm, nx, red_x = _group("x", n_red)
    part = src_ref.shape[0] // 2
    first, second = pl.ds(0, part), pl.ds(part, part)

    barrier = pltpu.get_barrier_semaphore()
    for o in range(1, ny):
        pl.semaphore_signal(barrier, inc=1, device_id=(*row, red_y(lax.rem(ym + o, ny))), device_id_type=MESH)
    for o in range(1, nx):
        pl.semaphore_signal(barrier, inc=1, device_id=(*row, red_x(lax.rem(xm + o, nx))), device_id_type=MESH)
    pl.semaphore_wait(barrier, ny - 1 + nx - 1)

    def copy(src, dst, stage, pos, dev):
        return pltpu.make_async_remote_copy(
            src_ref=src,
            dst_ref=dst,
            send_sem=send_sem.at[stage, pos],
            recv_sem=recv_sem.at[stage, pos],
            device_id=(*row, dev),
            device_id_type=MESH,
        )

    sent = []
    for o in range(1, ny):
        g = lax.rem(ym + o, ny)
        c = pltpu.make_async_remote_copy(
            src_ref=src_ref.at[first], dst_ref=out_ref.at[xm, ym, first],
            send_sem=send_sem.at[0, g], recv_sem=recv_sem.at[0, ym],
            device_id=(*row, red_y(g)), device_id_type=MESH,
        )
        c.start()
        sent.append(c)
    for o in range(1, nx):
        g = lax.rem(xm + o, nx)
        c = pltpu.make_async_remote_copy(
            src_ref=src_ref.at[second], dst_ref=out_ref.at[xm, ym, second],
            send_sem=send_sem.at[1, g], recv_sem=recv_sem.at[1, xm],
            device_id=(*row, red_x(g)), device_id_type=MESH,
        )
        c.start()
        sent.append(c)
    own = [
        pltpu.make_async_copy(src_ref.at[first], out_ref.at[xm, ym, first], local_sem.at[0]),
        pltpu.make_async_copy(src_ref.at[second], out_ref.at[xm, ym, second], local_sem.at[1]),
    ]
    for c in own:
        c.start()
    for c in own:
        c.wait()

    for o in range(1, ny):
        g = lax.rem(ym + o, ny)
        copy(src_ref.at[first], out_ref.at[xm, g, first], 0, g, red_y(g)).wait_recv()
    for o in range(1, nx):
        g = lax.rem(xm + o, nx)
        c = pltpu.make_async_remote_copy(
            src_ref=out_ref.at[xm, :, first], dst_ref=out_ref.at[xm, :, first],
            send_sem=send_sem.at[2, g], recv_sem=recv_sem.at[2, xm],
            device_id=(*row, red_x(g)), device_id_type=MESH,
        )
        c.start()
        sent.append(c)
    for o in range(1, nx):
        g = lax.rem(xm + o, nx)
        copy(src_ref.at[second], out_ref.at[g, ym, second], 1, g, red_x(g)).wait_recv()
    for o in range(1, ny):
        g = lax.rem(ym + o, ny)
        c = pltpu.make_async_remote_copy(
            src_ref=out_ref.at[:, ym, second], dst_ref=out_ref.at[:, ym, second],
            send_sem=send_sem.at[3, g], recv_sem=recv_sem.at[3, ym],
            device_id=(*row, red_y(g)), device_id_type=MESH,
        )
        c.start()
        sent.append(c)

    for c in sent:
        c.wait_send()
    for o in range(1, nx):
        g = lax.rem(xm + o, nx)
        copy(out_ref.at[g, :, first], out_ref.at[g, :, first], 2, g, red_x(g)).wait_recv()
    for o in range(1, ny):
        g = lax.rem(ym + o, ny)
        copy(out_ref.at[:, g, second], out_ref.at[:, g, second], 3, g, red_y(g)).wait_recv()


def _gather(block, n_red, collective_id):
    n_x = n_red // NY
    nbytes = block.size * block.dtype.itemsize
    return pl.pallas_call(
        functools.partial(_gather_kernel, n_red),
        out_shape=jax.ShapeDtypeStruct((n_x, NY) + block.shape, block.dtype),
        in_specs=[pl.BlockSpec(memory_space=pl.ANY)],
        out_specs=pl.BlockSpec(memory_space=pl.ANY),
        scratch_shapes=[
            pltpu.SemaphoreType.DMA((4, max(n_x, NY))),
            pltpu.SemaphoreType.DMA((4, max(n_x, NY))),
            pltpu.SemaphoreType.DMA((2,)),
        ],
        compiler_params=pltpu.CompilerParams(collective_id=collective_id, has_side_effects=True),
        cost_estimate=pl.CostEstimate(flops=0, bytes_accessed=2 * n_red * nbytes, transcendentals=0),
    )(block)


def _reduce_kernel(n_red, amp_ref, ints_ref, out_ref, ra, rb, pa, pb, sa, sb, qa, qb, send1, recv1, send2, recv2):
    row = _row()
    ym, ny, red_y = _group("y", n_red)
    xm, nx, red_x = _group("x", n_red)
    half = ra.shape[2]
    first, second = pl.ds(0, half), pl.ds(half, half)

    barrier = pltpu.get_barrier_semaphore()
    for o in range(1, ny):
        pl.semaphore_signal(barrier, inc=1, device_id=(*row, red_y(lax.rem(ym + o, ny))), device_id_type=MESH)
    for o in range(1, nx):
        pl.semaphore_signal(barrier, inc=1, device_id=(*row, red_x(lax.rem(xm + o, nx))), device_id_type=MESH)
    pl.semaphore_wait(barrier, ny - 1 + nx - 1)

    def copy(src, dst, send, recv, dev):
        return pltpu.make_async_remote_copy(
            src_ref=src, dst_ref=dst, send_sem=send, recv_sem=recv,
            device_id=(*row, dev), device_id_type=MESH,
        )

    width = ints_ref.shape[1]

    def block(lhs):
        slots = lhs.shape[0]
        flat = lhs.reshape(slots * half, lhs.shape[2])
        product = jnp.dot(flat, ints_ref[...], preferred_element_type=jnp.float32)
        return product.reshape(slots, half, width)

    sent = []
    for o in range(1, max(nx, ny)):
        if o < ny:
            g = lax.rem(ym + o, ny)
            pa[g] = block(amp_ref[:, g, first])
            c = copy(pa.at[g], ra.at[ym], send1.at[0, g], recv1.at[0, ym], red_y(g))
            c.start()
            sent.append(c)
        if o < nx:
            g = lax.rem(xm + o, nx)
            pb[g] = block(amp_ref[g, :, second])
            c = copy(pb.at[g], rb.at[xm], send1.at[1, g], recv1.at[1, xm], red_x(g))
            c.start()
            sent.append(c)
    ra[ym] = block(amp_ref[:, ym, first])
    rb[xm] = block(amp_ref[xm, :, second])

    for o in range(1, ny):
        g = lax.rem(ym + o, ny)
        copy(pa.at[g], ra.at[g], send1.at[0, g], recv1.at[0, g], red_y(g)).wait_recv()
    for k in range(nx):
        sa[k] = ra[0, k] + ra[1, k] + ra[2, k] + ra[3, k]
    for o in range(1, nx):
        g = lax.rem(xm + o, nx)
        c = copy(sa.at[g], qa.at[xm], send2.at[0, g], recv2.at[0, xm], red_x(g))
        c.start()
        sent.append(c)

    for o in range(1, nx):
        g = lax.rem(xm + o, nx)
        copy(pb.at[g], rb.at[g], send1.at[1, g], recv1.at[1, g], red_x(g)).wait_recv()
    for k in range(ny):
        sb[k] = rb[0, k] + rb[1, k] + rb[2, k] + rb[3, k]
    for o in range(1, ny):
        g = lax.rem(ym + o, ny)
        c = copy(sb.at[g], qb.at[ym], send2.at[1, g], recv2.at[1, ym], red_y(g))
        c.start()
        sent.append(c)

    for c in sent:
        c.wait_send()
    total_a = sa[xm]
    for o in range(1, nx):
        g = lax.rem(xm + o, nx)
        copy(sa.at[g], qa.at[g], send2.at[0, g], recv2.at[0, g], red_x(g)).wait_recv()
        total_a = total_a + qa[g]
    total_b = sb[ym]
    for o in range(1, ny):
        g = lax.rem(ym + o, ny)
        copy(sb.at[g], qb.at[g], send2.at[1, g], recv2.at[1, g], red_y(g)).wait_recv()
        total_b = total_b + qb[g]
    out_ref[first] = total_a
    out_ref[second] = total_b


def _reduce(amp, ints, n_red, collective_id):
    n_x, n_y, rows, _ = amp.shape
    cols = ints.shape[1]
    half = rows // 2
    f32 = jnp.float32
    return pl.pallas_call(
        functools.partial(_reduce_kernel, n_red),
        out_shape=jax.ShapeDtypeStruct((rows, cols), f32),
        in_specs=[pl.BlockSpec(memory_space=pltpu.VMEM)] * 2,
        out_specs=pl.BlockSpec(memory_space=pltpu.VMEM),
        scratch_shapes=[
            pltpu.VMEM((n_y, n_x, half, cols), f32),
            pltpu.VMEM((n_x, n_y, half, cols), f32),
            pltpu.VMEM((n_y, n_x, half, cols), f32),
            pltpu.VMEM((n_x, n_y, half, cols), f32),
            pltpu.VMEM((n_x, half, cols), f32),
            pltpu.VMEM((n_y, half, cols), f32),
            pltpu.VMEM((n_x, half, cols), f32),
            pltpu.VMEM((n_y, half, cols), f32),
            pltpu.SemaphoreType.DMA((2, max(n_x, n_y))),
            pltpu.SemaphoreType.DMA((2, max(n_x, n_y))),
            pltpu.SemaphoreType.DMA((2, max(n_x, n_y))),
            pltpu.SemaphoreType.DMA((2, max(n_x, n_y))),
        ],
        compiler_params=pltpu.CompilerParams(
            collective_id=collective_id, has_side_effects=True, vmem_limit_bytes=60 * 1024 * 1024
        ),
        cost_estimate=pl.CostEstimate(
            flops=2 * amp.size * cols, bytes_accessed=amp.size * 2 + ints.size * 2 + rows * cols * 4,
            transcendentals=0,
        ),
    )(amp, ints)


def _core_reduce_kernel(prod_ref, out_ref, theirs, mine, send_sem, recv_sem, local_sem):
    z, core = _row()
    red = lax.axis_index("red")
    other = CORES - 1 - core
    barrier = pltpu.get_barrier_semaphore()
    pl.semaphore_signal(barrier, inc=1, device_id=(z, other, red), device_id_type=MESH)
    pl.semaphore_wait(barrier, 1)
    send = pltpu.make_async_remote_copy(
        src_ref=prod_ref.at[:, other], dst_ref=theirs, send_sem=send_sem, recv_sem=recv_sem,
        device_id=(z, other, red), device_id_type=MESH,
    )
    send.start()
    own = pltpu.make_async_copy(prod_ref.at[:, core], mine, local_sem)
    own.start()
    own.wait()
    send.wait()
    for k in range(out_ref.shape[0]):
        out_ref[k] = mine[k] + theirs[k]


def _core_reduce(prod, collective_id):
    n_z, _, rows, cols = prod.shape
    f32 = jnp.float32
    return pl.pallas_call(
        _core_reduce_kernel,
        out_shape=jax.ShapeDtypeStruct((n_z, rows, cols), f32),
        in_specs=[pl.BlockSpec(memory_space=pl.ANY)],
        out_specs=pl.BlockSpec(memory_space=pltpu.VMEM),
        scratch_shapes=[
            pltpu.VMEM((n_z, rows, cols), f32),
            pltpu.VMEM((n_z, rows, cols), f32),
            pltpu.SemaphoreType.DMA,
            pltpu.SemaphoreType.DMA,
            pltpu.SemaphoreType.DMA,
        ],
        compiler_params=pltpu.CompilerParams(collective_id=collective_id, has_side_effects=True),
        cost_estimate=pl.CostEstimate(
            flops=prod.size // 2, bytes_accessed=prod.size * 4, transcendentals=0
        ),
    )(prod)


def _exchange(jobs, srcs, out_shapes, n_red, collective_id):
    nbytes = sum(s.size * s.dtype.itemsize for s in srcs)
    nmax = max(_group_size(job[0], n_red) for job in jobs)
    return pl.pallas_call(
        functools.partial(_exchange_kernel, tuple(jobs), len(srcs), len(out_shapes), n_red),
        out_shape=tuple(jax.ShapeDtypeStruct(s, d) for s, d in out_shapes),
        in_specs=[pl.BlockSpec(memory_space=pl.ANY)] * len(srcs),
        out_specs=tuple(pl.BlockSpec(memory_space=pl.ANY) for _ in out_shapes),
        scratch_shapes=[
            pltpu.SemaphoreType.DMA((len(jobs), nmax)),
            pltpu.SemaphoreType.DMA((len(jobs), nmax)),
            pltpu.SemaphoreType.DMA((len(jobs),)),
        ],
        compiler_params=pltpu.CompilerParams(collective_id=collective_id, has_side_effects=True),
        cost_estimate=pl.CostEstimate(flops=0, bytes_accessed=4 * nbytes, transcendentals=0),
    )(*srcs)


def _group_size(kind, n_red):
    return {"y": NY, "x": n_red // NY}.get(kind, n_red)


def _whole(ref, pos):
    return ref


def _slot(ref, pos):
    return ref.at[pos]


def shards(amplitudes, ladder_ints, cycle_ints, occ_energy, vir_energy, slab_index):
    slab_rows, occ_local, vir_local, virt_width = amplitudes.shape
    n_red = lax.axis_size("red")
    n_blk = lax.axis_size("z") * lax.axis_size("core")
    occ_all = occ_local * n_blk
    occ_red = occ_all // n_red
    n_x = n_red // NY

    swapped = jnp.transpose(amplitudes, (0, 2, 1, 3)).reshape(
        slab_rows * vir_local, occ_local * virt_width
    )
    gathered = _gather(swapped, n_red, 0)
    operand = gathered.reshape(n_red * slab_rows * vir_local, occ_local * virt_width)
    product = jnp.dot(operand, cycle_ints, preferred_element_type=jnp.float32)
    product = product.reshape(n_blk // CORES, CORES, slab_rows * vir_local, cycle_ints.shape[1])
    product = _core_reduce(product, 4)
    cycle_own = lax.psum_scatter(product, "z", scatter_dimension=0, tiled=True)[0]
    cycle_own = jnp.transpose(
        cycle_own.reshape(slab_rows, vir_local, occ_red, virt_width), (0, 2, 1, 3)
    )

    rows = slab_rows * occ_local
    flat = amplitudes.reshape(rows, vir_local * virt_width)
    shard_piece = lax.all_gather(flat, ("z", "core"), axis=0, tiled=False)
    ladder_own = _reduce(shard_piece.reshape(n_x, NY, rows, -1), ladder_ints, n_red, 1)
    ladder_own = ladder_own.reshape(slab_rows, occ_red, -1, virt_width)

    vir_block = cycle_own.shape[2]
    orbital_ids = jnp.arange(occ_energy.shape[0], dtype=jnp.int32)
    chosen = slab_index[:, None] == orbital_ids[None, :]
    slab_energy = jnp.sum(jnp.where(chosen, occ_energy[None, :], jnp.float32(0.0)), axis=1)
    pair_energy = lax.dynamic_slice_in_dim(occ_energy, lax.axis_index("red") * occ_red, occ_red)
    first_virtual = lax.dynamic_slice_in_dim(
        vir_energy, (lax.axis_index("z") * CORES + lax.axis_index("core")) * vir_block, vir_block
    )
    denominator = (
        first_virtual[None, None, :, None]
        + vir_energy[None, None, None, :]
        - slab_energy[:, None, None, None]
        - pair_energy[None, :, None, None]
    )
    return (ladder_own + cycle_own) / denominator


def solution(mesh):
    blk = ("z", "core")
    split = Mesh(
        mesh.devices.reshape(mesh.shape["blk"] // CORES, CORES, mesh.shape["red"]),
        ("z", "core", "red"),
    )
    placed = (P(None, blk, "red", None), P("red", blk), P(blk, "red"), P(), P(), P())
    return jax.shard_map(
        shards, mesh=split, in_specs=placed, out_specs=P(None, "red", blk, None), check_vma=False
    )
```

```python
import functools

import jax
import jax.numpy as jnp
from jax import lax
from jax.experimental import pallas as pl
from jax.experimental.pallas import tpu as pltpu
from jax.sharding import Mesh, PartitionSpec as P

MESH = pl.DeviceIdType.MESH
PIECES = 1


NY = 4
CORES = 2


def _row():
    return lax.axis_index("z"), lax.axis_index("core")


def _group(kind, n_red):
    r = lax.axis_index("red")
    x, y = r // NY, lax.rem(r, NY)
    if kind == "y":
        return y, NY, lambda pos: x * NY + pos
    if kind == "x":
        return x, n_red // NY, lambda pos: pos * NY + y
    return r, n_red, lambda pos: pos


def _exchange_kernel(jobs, n_in, n_out, n_red, *refs):
    ins, outs = refs[:n_in], refs[n_in:n_in + n_out]
    send_sem, recv_sem, local_sem = refs[n_in + n_out:]
    row = _row()

    barrier = pltpu.get_barrier_semaphore()
    count = 0
    for kind in sorted(set(job[0] for job in jobs)):
        me, n, red_of = _group(kind, n_red)
        for o in range(1, n):
            pl.semaphore_signal(
                barrier, inc=1, device_id=(*row, red_of(lax.rem(me + o, n))), device_id_type=MESH
            )
            count += 1
    pl.semaphore_wait(barrier, count)

    def remote(j, pos, slot, piece=None):
        kind, si, src_view, di, dst_view = jobs[j]
        _, _, red_of = _group(kind, n_red)
        src, dst = src_view(ins[si], pos), dst_view(outs[di], slot)
        if piece is not None:
            size = src.shape[0] // PIECES
            src, dst = src.at[pl.ds(piece * size, size)], dst.at[pl.ds(piece * size, size)]
        return pltpu.make_async_remote_copy(
            src_ref=src,
            dst_ref=dst,
            send_sem=send_sem.at[j, pos],
            recv_sem=recv_sem.at[j, slot],
            device_id=(*row, red_of(pos)),
            device_id_type=MESH,
        )

    for piece in range(PIECES):
        for j, job in enumerate(jobs):
            me, n, _ = _group(job[0], n_red)
            for o in range(1, n):
                remote(j, lax.rem(me + o, n), me, piece).start()
    for j, (kind, si, src_view, di, dst_view) in enumerate(jobs):
        me, n, _ = _group(kind, n_red)
        local = pltpu.make_async_copy(
            src_view(ins[si], me), dst_view(outs[di], me), local_sem.at[j]
        )
        local.start()
        local.wait()
    for j, job in enumerate(jobs):
        me, n, _ = _group(job[0], n_red)
        for o in range(1, n):
            g = lax.rem(me + o, n)
            remote(j, g, g).wait()


def _gather_kernel(n_red, src_ref, out_ref, send_sem, recv_sem, local_sem):
    row = _row()
    ym, ny, red_y = _group("y", n_red)
    xm, nx, red_x = _group("x", n_red)
    part = src_ref.shape[0] // 2
    first, second = pl.ds(0, part), pl.ds(part, part)

    barrier = pltpu.get_barrier_semaphore()
    for o in range(1, ny):
        pl.semaphore_signal(barrier, inc=1, device_id=(*row, red_y(lax.rem(ym + o, ny))), device_id_type=MESH)
    for o in range(1, nx):
        pl.semaphore_signal(barrier, inc=1, device_id=(*row, red_x(lax.rem(xm + o, nx))), device_id_type=MESH)
    pl.semaphore_wait(barrier, ny - 1 + nx - 1)

    def copy(src, dst, stage, pos, dev):
        return pltpu.make_async_remote_copy(
            src_ref=src,
            dst_ref=dst,
            send_sem=send_sem.at[stage, pos],
            recv_sem=recv_sem.at[stage, pos],
            device_id=(*row, dev),
            device_id_type=MESH,
        )

    sent = []
    for o in range(1, ny):
        g = lax.rem(ym + o, ny)
        c = pltpu.make_async_remote_copy(
            src_ref=src_ref.at[first], dst_ref=out_ref.at[xm, ym, first],
            send_sem=send_sem.at[0, g], recv_sem=recv_sem.at[0, ym],
            device_id=(*row, red_y(g)), device_id_type=MESH,
        )
        c.start()
        sent.append(c)
    for o in range(1, nx):
        g = lax.rem(xm + o, nx)
        c = pltpu.make_async_remote_copy(
            src_ref=src_ref.at[second], dst_ref=out_ref.at[xm, ym, second],
            send_sem=send_sem.at[1, g], recv_sem=recv_sem.at[1, xm],
            device_id=(*row, red_x(g)), device_id_type=MESH,
        )
        c.start()
        sent.append(c)
    own = [
        pltpu.make_async_copy(src_ref.at[first], out_ref.at[xm, ym, first], local_sem.at[0]),
        pltpu.make_async_copy(src_ref.at[second], out_ref.at[xm, ym, second], local_sem.at[1]),
    ]
    for c in own:
        c.start()
    for c in own:
        c.wait()

    for o in range(1, ny):
        g = lax.rem(ym + o, ny)
        copy(src_ref.at[first], out_ref.at[xm, g, first], 0, g, red_y(g)).wait_recv()
    for o in range(1, nx):
        g = lax.rem(xm + o, nx)
        c = pltpu.make_async_remote_copy(
            src_ref=out_ref.at[xm, :, first], dst_ref=out_ref.at[xm, :, first],
            send_sem=send_sem.at[2, g], recv_sem=recv_sem.at[2, xm],
            device_id=(*row, red_x(g)), device_id_type=MESH,
        )
        c.start()
        sent.append(c)
    for o in range(1, nx):
        g = lax.rem(xm + o, nx)
        copy(src_ref.at[second], out_ref.at[g, ym, second], 1, g, red_x(g)).wait_recv()
    for o in range(1, ny):
        g = lax.rem(ym + o, ny)
        c = pltpu.make_async_remote_copy(
            src_ref=out_ref.at[:, ym, second], dst_ref=out_ref.at[:, ym, second],
            send_sem=send_sem.at[3, g], recv_sem=recv_sem.at[3, ym],
            device_id=(*row, red_y(g)), device_id_type=MESH,
        )
        c.start()
        sent.append(c)

    for c in sent:
        c.wait_send()
    for o in range(1, nx):
        g = lax.rem(xm + o, nx)
        copy(out_ref.at[g, :, first], out_ref.at[g, :, first], 2, g, red_x(g)).wait_recv()
    for o in range(1, ny):
        g = lax.rem(ym + o, ny)
        copy(out_ref.at[:, g, second], out_ref.at[:, g, second], 3, g, red_y(g)).wait_recv()


def _gather(block, n_red, collective_id):
    n_x = n_red // NY
    nbytes = block.size * block.dtype.itemsize
    return pl.pallas_call(
        functools.partial(_gather_kernel, n_red),
        out_shape=jax.ShapeDtypeStruct((n_x, NY) + block.shape, block.dtype),
        in_specs=[pl.BlockSpec(memory_space=pl.ANY)],
        out_specs=pl.BlockSpec(memory_space=pl.ANY),
        scratch_shapes=[
            pltpu.SemaphoreType.DMA((4, max(n_x, NY))),
            pltpu.SemaphoreType.DMA((4, max(n_x, NY))),
            pltpu.SemaphoreType.DMA((2,)),
        ],
        compiler_params=pltpu.CompilerParams(collective_id=collective_id, has_side_effects=True),
        cost_estimate=pl.CostEstimate(flops=0, bytes_accessed=2 * n_red * nbytes, transcendentals=0),
    )(block)


def _reduce_kernel(n_red, amp_ref, ints_ref, out_ref, ra, rb, pa, pb, sa, sb, qa, qb, send1, recv1, send2, recv2):
    row = _row()
    ym, ny, red_y = _group("y", n_red)
    xm, nx, red_x = _group("x", n_red)
    half = ra.shape[2]
    first, second = pl.ds(0, half), pl.ds(half, half)

    barrier = pltpu.get_barrier_semaphore()
    for o in range(1, ny):
        pl.semaphore_signal(barrier, inc=1, device_id=(*row, red_y(lax.rem(ym + o, ny))), device_id_type=MESH)
    for o in range(1, nx):
        pl.semaphore_signal(barrier, inc=1, device_id=(*row, red_x(lax.rem(xm + o, nx))), device_id_type=MESH)
    pl.semaphore_wait(barrier, ny - 1 + nx - 1)

    def copy(src, dst, send, recv, dev):
        return pltpu.make_async_remote_copy(
            src_ref=src, dst_ref=dst, send_sem=send, recv_sem=recv,
            device_id=(*row, dev), device_id_type=MESH,
        )

    width = ints_ref.shape[1]

    def block(lhs):
        slots = lhs.shape[0]
        flat = lhs.reshape(slots * half, lhs.shape[2])
        product = jnp.dot(flat, ints_ref[...], preferred_element_type=jnp.float32)
        return product.reshape(slots, half, width)

    sent = []
    for o in range(1, max(nx, ny)):
        if o < ny:
            g = lax.rem(ym + o, ny)
            pa[g] = block(amp_ref[:, g, first])
            c = copy(pa.at[g], ra.at[ym], send1.at[0, g], recv1.at[0, ym], red_y(g))
            c.start()
            sent.append(c)
        if o < nx:
            g = lax.rem(xm + o, nx)
            pb[g] = block(amp_ref[g, :, second])
            c = copy(pb.at[g], rb.at[xm], send1.at[1, g], recv1.at[1, xm], red_x(g))
            c.start()
            sent.append(c)
    ra[ym] = block(amp_ref[:, ym, first])
    rb[xm] = block(amp_ref[xm, :, second])

    for o in range(1, ny):
        g = lax.rem(ym + o, ny)
        copy(pa.at[g], ra.at[g], send1.at[0, g], recv1.at[0, g], red_y(g)).wait_recv()
    for k in range(nx):
        sa[k] = ra[0, k] + ra[1, k] + ra[2, k] + ra[3, k]
    for o in range(1, nx):
        g = lax.rem(xm + o, nx)
        c = copy(sa.at[g], qa.at[xm], send2.at[0, g], recv2.at[0, xm], red_x(g))
        c.start()
        sent.append(c)

    for o in range(1, nx):
        g = lax.rem(xm + o, nx)
        copy(pb.at[g], rb.at[g], send1.at[1, g], recv1.at[1, g], red_x(g)).wait_recv()
    for k in range(ny):
        sb[k] = rb[0, k] + rb[1, k] + rb[2, k] + rb[3, k]
    for o in range(1, ny):
        g = lax.rem(ym + o, ny)
        c = copy(sb.at[g], qb.at[ym], send2.at[1, g], recv2.at[1, ym], red_y(g))
        c.start()
        sent.append(c)

    for c in sent:
        c.wait_send()
    total_a = sa[xm]
    for o in range(1, nx):
        g = lax.rem(xm + o, nx)
        copy(sa.at[g], qa.at[g], send2.at[0, g], recv2.at[0, g], red_x(g)).wait_recv()
        total_a = total_a + qa[g]
    total_b = sb[ym]
    for o in range(1, ny):
        g = lax.rem(ym + o, ny)
        copy(sb.at[g], qb.at[g], send2.at[1, g], recv2.at[1, g], red_y(g)).wait_recv()
        total_b = total_b + qb[g]
    out_ref[first] = total_a
    out_ref[second] = total_b


def _reduce(amp, ints, n_red, collective_id):
    n_x, n_y, rows, _ = amp.shape
    cols = ints.shape[1]
    half = rows // 2
    f32 = jnp.float32
    return pl.pallas_call(
        functools.partial(_reduce_kernel, n_red),
        out_shape=jax.ShapeDtypeStruct((rows, cols), f32),
        in_specs=[pl.BlockSpec(memory_space=pltpu.VMEM)] * 2,
        out_specs=pl.BlockSpec(memory_space=pltpu.VMEM),
        scratch_shapes=[
            pltpu.VMEM((n_y, n_x, half, cols), f32),
            pltpu.VMEM((n_x, n_y, half, cols), f32),
            pltpu.VMEM((n_y, n_x, half, cols), f32),
            pltpu.VMEM((n_x, n_y, half, cols), f32),
            pltpu.VMEM((n_x, half, cols), f32),
            pltpu.VMEM((n_y, half, cols), f32),
            pltpu.VMEM((n_x, half, cols), f32),
            pltpu.VMEM((n_y, half, cols), f32),
            pltpu.SemaphoreType.DMA((2, max(n_x, n_y))),
            pltpu.SemaphoreType.DMA((2, max(n_x, n_y))),
            pltpu.SemaphoreType.DMA((2, max(n_x, n_y))),
            pltpu.SemaphoreType.DMA((2, max(n_x, n_y))),
        ],
        compiler_params=pltpu.CompilerParams(
            collective_id=collective_id, has_side_effects=True, vmem_limit_bytes=60 * 1024 * 1024
        ),
        cost_estimate=pl.CostEstimate(
            flops=2 * amp.size * cols, bytes_accessed=amp.size * 2 + ints.size * 2 + rows * cols * 4,
            transcendentals=0,
        ),
    )(amp, ints)


def _core_reduce_kernel(amp_ref, ints_ref, out_ref, mine_sent, theirs, send_sem, recv_sem):
    z, core = _row()
    red = lax.axis_index("red")
    other = CORES - 1 - core
    n_z, _, rows, _ = amp_ref.shape
    width = ints_ref.shape[1]
    step = n_z // 2
    barrier = pltpu.get_barrier_semaphore()
    pl.semaphore_signal(barrier, inc=1, device_id=(z, other, red), device_id_type=MESH)
    pl.semaphore_wait(barrier, 1)

    def block(k, which):
        lhs = amp_ref[pl.ds(k * step, step), which]
        product = jnp.dot(
            lhs.reshape(step * rows, lhs.shape[2]), ints_ref[...], preferred_element_type=jnp.float32
        )
        return product.reshape(step, rows, width)

    sends = []
    for k in range(2):
        mine_sent[pl.ds(k * step, step)] = block(k, other)
        c = pltpu.make_async_remote_copy(
            src_ref=mine_sent.at[pl.ds(k * step, step)], dst_ref=theirs.at[pl.ds(k * step, step)],
            send_sem=send_sem.at[k], recv_sem=recv_sem.at[k],
            device_id=(z, other, red), device_id_type=MESH,
        )
        c.start()
        sends.append(c)
    for k in range(2):
        out_ref[pl.ds(k * step, step)] = block(k, core)
    for k, c in enumerate(sends):
        c.wait()
        for i in range(k * step, (k + 1) * step):
            out_ref[i] = out_ref[i] + theirs[i]


def _core_reduce(amp, ints, collective_id):
    n_z, _, rows, _ = amp.shape
    cols = ints.shape[1]
    f32 = jnp.float32
    return pl.pallas_call(
        _core_reduce_kernel,
        out_shape=jax.ShapeDtypeStruct((n_z, rows, cols), f32),
        in_specs=[pl.BlockSpec(memory_space=pltpu.VMEM)] * 2,
        out_specs=pl.BlockSpec(memory_space=pltpu.VMEM),
        scratch_shapes=[
            pltpu.VMEM((n_z, rows, cols), f32),
            pltpu.VMEM((n_z, rows, cols), f32),
            pltpu.SemaphoreType.DMA((2,)),
            pltpu.SemaphoreType.DMA((2,)),
        ],
        compiler_params=pltpu.CompilerParams(
            collective_id=collective_id, has_side_effects=True, vmem_limit_bytes=60 * 1024 * 1024
        ),
        cost_estimate=pl.CostEstimate(
            flops=2 * amp.size * cols, bytes_accessed=amp.size * 2 + ints.size * 2 + n_z * rows * cols * 4,
            transcendentals=0,
        ),
    )(amp, ints)


def _exchange(jobs, srcs, out_shapes, n_red, collective_id):
    nbytes = sum(s.size * s.dtype.itemsize for s in srcs)
    nmax = max(_group_size(job[0], n_red) for job in jobs)
    return pl.pallas_call(
        functools.partial(_exchange_kernel, tuple(jobs), len(srcs), len(out_shapes), n_red),
        out_shape=tuple(jax.ShapeDtypeStruct(s, d) for s, d in out_shapes),
        in_specs=[pl.BlockSpec(memory_space=pl.ANY)] * len(srcs),
        out_specs=tuple(pl.BlockSpec(memory_space=pl.ANY) for _ in out_shapes),
        scratch_shapes=[
            pltpu.SemaphoreType.DMA((len(jobs), nmax)),
            pltpu.SemaphoreType.DMA((len(jobs), nmax)),
            pltpu.SemaphoreType.DMA((len(jobs),)),
        ],
        compiler_params=pltpu.CompilerParams(collective_id=collective_id, has_side_effects=True),
        cost_estimate=pl.CostEstimate(flops=0, bytes_accessed=4 * nbytes, transcendentals=0),
    )(*srcs)


def _group_size(kind, n_red):
    return {"y": NY, "x": n_red // NY}.get(kind, n_red)


def _whole(ref, pos):
    return ref


def _slot(ref, pos):
    return ref.at[pos]


def shards(amplitudes, ladder_ints, cycle_ints, occ_energy, vir_energy, slab_index):
    slab_rows, occ_local, vir_local, virt_width = amplitudes.shape
    n_red = lax.axis_size("red")
    n_blk = lax.axis_size("z") * lax.axis_size("core")
    occ_all = occ_local * n_blk
    occ_red = occ_all // n_red
    n_x = n_red // NY

    swapped = jnp.transpose(amplitudes, (0, 2, 1, 3)).reshape(
        slab_rows * vir_local, occ_local * virt_width
    )
    gathered = _gather(swapped, n_red, 0)
    operand = gathered.reshape(n_blk // CORES, CORES, slab_rows * vir_local, occ_local * virt_width)
    product = _core_reduce(operand, cycle_ints, 4)
    cycle_own = lax.psum_scatter(product, "z", scatter_dimension=0, tiled=True)[0]
    cycle_own = jnp.transpose(
        cycle_own.reshape(slab_rows, vir_local, occ_red, virt_width), (0, 2, 1, 3)
    )

    rows = slab_rows * occ_local
    flat = amplitudes.reshape(rows, vir_local * virt_width)
    shard_piece = lax.all_gather(flat, ("z", "core"), axis=0, tiled=False)
    ladder_own = _reduce(shard_piece.reshape(n_x, NY, rows, -1), ladder_ints, n_red, 1)
    ladder_own = ladder_own.reshape(slab_rows, occ_red, -1, virt_width)

    vir_block = cycle_own.shape[2]
    orbital_ids = jnp.arange(occ_energy.shape[0], dtype=jnp.int32)
    chosen = slab_index[:, None] == orbital_ids[None, :]
    slab_energy = jnp.sum(jnp.where(chosen, occ_energy[None, :], jnp.float32(0.0)), axis=1)
    pair_energy = lax.dynamic_slice_in_dim(occ_energy, lax.axis_index("red") * occ_red, occ_red)
    first_virtual = lax.dynamic_slice_in_dim(
        vir_energy, (lax.axis_index("z") * CORES + lax.axis_index("core")) * vir_block, vir_block
    )
    denominator = (
        first_virtual[None, None, :, None]
        + vir_energy[None, None, None, :]
        - slab_energy[:, None, None, None]
        - pair_energy[None, :, None, None]
    )
    return (ladder_own + cycle_own) / denominator


def solution(mesh):
    blk = ("z", "core")
    split = Mesh(
        mesh.devices.reshape(mesh.shape["blk"] // CORES, CORES, mesh.shape["red"]),
        ("z", "core", "red"),
    )
    placed = (P(None, blk, "red", None), P("red", blk), P(blk, "red"), P(), P(), P())
    return jax.shard_map(
        shards, mesh=split, in_specs=placed, out_specs=P(None, "red", blk, None), check_vma=False
    )
```

```python
import functools

import jax
import jax.numpy as jnp
from jax import lax
from jax.experimental import pallas as pl
from jax.experimental.pallas import tpu as pltpu
from jax.sharding import Mesh, PartitionSpec as P

MESH = pl.DeviceIdType.MESH
PIECES = 1


NY = 4
CORES = 2


def _row():
    return lax.axis_index("z"), lax.axis_index("core")


def _group(kind, n_red):
    r = lax.axis_index("red")
    x, y = r // NY, lax.rem(r, NY)
    if kind == "y":
        return y, NY, lambda pos: x * NY + pos
    if kind == "x":
        return x, n_red // NY, lambda pos: pos * NY + y
    return r, n_red, lambda pos: pos


def _exchange_kernel(jobs, n_in, n_out, n_red, *refs):
    ins, outs = refs[:n_in], refs[n_in:n_in + n_out]
    send_sem, recv_sem, local_sem = refs[n_in + n_out:]
    row = _row()

    barrier = pltpu.get_barrier_semaphore()
    count = 0
    for kind in sorted(set(job[0] for job in jobs)):
        me, n, red_of = _group(kind, n_red)
        for o in range(1, n):
            pl.semaphore_signal(
                barrier, inc=1, device_id=(*row, red_of(lax.rem(me + o, n))), device_id_type=MESH
            )
            count += 1
    pl.semaphore_wait(barrier, count)

    def remote(j, pos, slot, piece=None):
        kind, si, src_view, di, dst_view = jobs[j]
        _, _, red_of = _group(kind, n_red)
        src, dst = src_view(ins[si], pos), dst_view(outs[di], slot)
        if piece is not None:
            size = src.shape[0] // PIECES
            src, dst = src.at[pl.ds(piece * size, size)], dst.at[pl.ds(piece * size, size)]
        return pltpu.make_async_remote_copy(
            src_ref=src,
            dst_ref=dst,
            send_sem=send_sem.at[j, pos],
            recv_sem=recv_sem.at[j, slot],
            device_id=(*row, red_of(pos)),
            device_id_type=MESH,
        )

    for piece in range(PIECES):
        for j, job in enumerate(jobs):
            me, n, _ = _group(job[0], n_red)
            for o in range(1, n):
                remote(j, lax.rem(me + o, n), me, piece).start()
    for j, (kind, si, src_view, di, dst_view) in enumerate(jobs):
        me, n, _ = _group(kind, n_red)
        local = pltpu.make_async_copy(
            src_view(ins[si], me), dst_view(outs[di], me), local_sem.at[j]
        )
        local.start()
        local.wait()
    for j, job in enumerate(jobs):
        me, n, _ = _group(job[0], n_red)
        for o in range(1, n):
            g = lax.rem(me + o, n)
            remote(j, g, g).wait()


def _gather_kernel(n_red, src_ref, out_ref, send_sem, recv_sem, local_sem):
    row = _row()
    ym, ny, red_y = _group("y", n_red)
    xm, nx, red_x = _group("x", n_red)
    part = src_ref.shape[0] // 2
    first, second = pl.ds(0, part), pl.ds(part, part)

    barrier = pltpu.get_barrier_semaphore()
    for o in range(1, ny):
        pl.semaphore_signal(barrier, inc=1, device_id=(*row, red_y(lax.rem(ym + o, ny))), device_id_type=MESH)
    for o in range(1, nx):
        pl.semaphore_signal(barrier, inc=1, device_id=(*row, red_x(lax.rem(xm + o, nx))), device_id_type=MESH)
    pl.semaphore_wait(barrier, ny - 1 + nx - 1)

    def copy(src, dst, stage, pos, dev):
        return pltpu.make_async_remote_copy(
            src_ref=src,
            dst_ref=dst,
            send_sem=send_sem.at[stage, pos],
            recv_sem=recv_sem.at[stage, pos],
            device_id=(*row, dev),
            device_id_type=MESH,
        )

    sent = []
    for o in range(1, ny):
        g = lax.rem(ym + o, ny)
        c = pltpu.make_async_remote_copy(
            src_ref=src_ref.at[first], dst_ref=out_ref.at[xm, ym, first],
            send_sem=send_sem.at[0, g], recv_sem=recv_sem.at[0, ym],
            device_id=(*row, red_y(g)), device_id_type=MESH,
        )
        c.start()
        sent.append(c)
    for o in range(1, nx):
        g = lax.rem(xm + o, nx)
        c = pltpu.make_async_remote_copy(
            src_ref=src_ref.at[second], dst_ref=out_ref.at[xm, ym, second],
            send_sem=send_sem.at[1, g], recv_sem=recv_sem.at[1, xm],
            device_id=(*row, red_x(g)), device_id_type=MESH,
        )
        c.start()
        sent.append(c)
    own = [
        pltpu.make_async_copy(src_ref.at[first], out_ref.at[xm, ym, first], local_sem.at[0]),
        pltpu.make_async_copy(src_ref.at[second], out_ref.at[xm, ym, second], local_sem.at[1]),
    ]
    for c in own:
        c.start()
    for c in own:
        c.wait()

    for o in range(1, ny):
        g = lax.rem(ym + o, ny)
        copy(src_ref.at[first], out_ref.at[xm, g, first], 0, g, red_y(g)).wait_recv()
    for o in range(1, nx):
        g = lax.rem(xm + o, nx)
        c = pltpu.make_async_remote_copy(
            src_ref=out_ref.at[xm, :, first], dst_ref=out_ref.at[xm, :, first],
            send_sem=send_sem.at[2, g], recv_sem=recv_sem.at[2, xm],
            device_id=(*row, red_x(g)), device_id_type=MESH,
        )
        c.start()
        sent.append(c)
    for o in range(1, nx):
        g = lax.rem(xm + o, nx)
        copy(src_ref.at[second], out_ref.at[g, ym, second], 1, g, red_x(g)).wait_recv()
    for o in range(1, ny):
        g = lax.rem(ym + o, ny)
        c = pltpu.make_async_remote_copy(
            src_ref=out_ref.at[:, ym, second], dst_ref=out_ref.at[:, ym, second],
            send_sem=send_sem.at[3, g], recv_sem=recv_sem.at[3, ym],
            device_id=(*row, red_y(g)), device_id_type=MESH,
        )
        c.start()
        sent.append(c)

    for c in sent:
        c.wait_send()
    for o in range(1, nx):
        g = lax.rem(xm + o, nx)
        copy(out_ref.at[g, :, first], out_ref.at[g, :, first], 2, g, red_x(g)).wait_recv()
    for o in range(1, ny):
        g = lax.rem(ym + o, ny)
        copy(out_ref.at[:, g, second], out_ref.at[:, g, second], 3, g, red_y(g)).wait_recv()


def _gather(block, n_red, collective_id):
    n_x = n_red // NY
    nbytes = block.size * block.dtype.itemsize
    return pl.pallas_call(
        functools.partial(_gather_kernel, n_red),
        out_shape=jax.ShapeDtypeStruct((n_x, NY) + block.shape, block.dtype),
        in_specs=[pl.BlockSpec(memory_space=pl.ANY)],
        out_specs=pl.BlockSpec(memory_space=pl.ANY),
        scratch_shapes=[
            pltpu.SemaphoreType.DMA((4, max(n_x, NY))),
            pltpu.SemaphoreType.DMA((4, max(n_x, NY))),
            pltpu.SemaphoreType.DMA((2,)),
        ],
        compiler_params=pltpu.CompilerParams(collective_id=collective_id, has_side_effects=True),
        cost_estimate=pl.CostEstimate(flops=0, bytes_accessed=2 * n_red * nbytes, transcendentals=0),
    )(block)


def _reduce_kernel(n_red, amp_ref, ints_ref, out_ref, ra, rb, pa, pb, sa, sb, qa, qb, send1, recv1, send2, recv2):
    row = _row()
    ym, ny, red_y = _group("y", n_red)
    xm, nx, red_x = _group("x", n_red)
    half = ra.shape[2]
    first, second = pl.ds(0, half), pl.ds(half, half)

    barrier = pltpu.get_barrier_semaphore()
    for o in range(1, ny):
        pl.semaphore_signal(barrier, inc=1, device_id=(*row, red_y(lax.rem(ym + o, ny))), device_id_type=MESH)
    for o in range(1, nx):
        pl.semaphore_signal(barrier, inc=1, device_id=(*row, red_x(lax.rem(xm + o, nx))), device_id_type=MESH)
    pl.semaphore_wait(barrier, ny - 1 + nx - 1)

    def copy(src, dst, send, recv, dev):
        return pltpu.make_async_remote_copy(
            src_ref=src, dst_ref=dst, send_sem=send, recv_sem=recv,
            device_id=(*row, dev), device_id_type=MESH,
        )

    width = ints_ref.shape[1]

    def block(lhs):
        slots = lhs.shape[0]
        flat = lhs.reshape(slots * half, lhs.shape[2])
        product = jnp.dot(flat, ints_ref[...], preferred_element_type=jnp.float32)
        return product.reshape(slots, half, width)

    sent = []
    for o in range(1, max(nx, ny)):
        if o < ny:
            g = lax.rem(ym + o, ny)
            pa[g] = block(amp_ref[:, g, first])
            c = copy(pa.at[g], ra.at[ym], send1.at[0, g], recv1.at[0, ym], red_y(g))
            c.start()
            sent.append(c)
        if o < nx:
            g = lax.rem(xm + o, nx)
            pb[g] = block(amp_ref[g, :, second])
            c = copy(pb.at[g], rb.at[xm], send1.at[1, g], recv1.at[1, xm], red_x(g))
            c.start()
            sent.append(c)
    ra[ym] = block(amp_ref[:, ym, first])
    rb[xm] = block(amp_ref[xm, :, second])

    for o in range(1, ny):
        g = lax.rem(ym + o, ny)
        copy(pa.at[g], ra.at[g], send1.at[0, g], recv1.at[0, g], red_y(g)).wait_recv()
    for o in range(1, nx):
        g = lax.rem(xm + o, nx)
        sa[g] = ra[0, g] + ra[1, g] + ra[2, g] + ra[3, g]
        c = copy(sa.at[g], qa.at[xm], send2.at[0, g], recv2.at[0, xm], red_x(g))
        c.start()
        sent.append(c)
    sa[xm] = ra[0, xm] + ra[1, xm] + ra[2, xm] + ra[3, xm]

    for o in range(1, nx):
        g = lax.rem(xm + o, nx)
        copy(pb.at[g], rb.at[g], send1.at[1, g], recv1.at[1, g], red_x(g)).wait_recv()
    for o in range(1, ny):
        g = lax.rem(ym + o, ny)
        sb[g] = rb[0, g] + rb[1, g] + rb[2, g] + rb[3, g]
        c = copy(sb.at[g], qb.at[ym], send2.at[1, g], recv2.at[1, ym], red_y(g))
        c.start()
        sent.append(c)
    sb[ym] = rb[0, ym] + rb[1, ym] + rb[2, ym] + rb[3, ym]

    for c in sent:
        c.wait_send()
    total_a = sa[xm]
    for o in range(1, nx):
        g = lax.rem(xm + o, nx)
        copy(sa.at[g], qa.at[g], send2.at[0, g], recv2.at[0, g], red_x(g)).wait_recv()
        total_a = total_a + qa[g]
    total_b = sb[ym]
    for o in range(1, ny):
        g = lax.rem(ym + o, ny)
        copy(sb.at[g], qb.at[g], send2.at[1, g], recv2.at[1, g], red_y(g)).wait_recv()
        total_b = total_b + qb[g]
    out_ref[first] = total_a
    out_ref[second] = total_b


def _reduce(amp, ints, n_red, collective_id):
    n_x, n_y, rows, _ = amp.shape
    cols = ints.shape[1]
    half = rows // 2
    f32 = jnp.float32
    return pl.pallas_call(
        functools.partial(_reduce_kernel, n_red),
        out_shape=jax.ShapeDtypeStruct((rows, cols), f32),
        in_specs=[pl.BlockSpec(memory_space=pltpu.VMEM)] * 2,
        out_specs=pl.BlockSpec(memory_space=pltpu.VMEM),
        scratch_shapes=[
            pltpu.VMEM((n_y, n_x, half, cols), f32),
            pltpu.VMEM((n_x, n_y, half, cols), f32),
            pltpu.VMEM((n_y, n_x, half, cols), f32),
            pltpu.VMEM((n_x, n_y, half, cols), f32),
            pltpu.VMEM((n_x, half, cols), f32),
            pltpu.VMEM((n_y, half, cols), f32),
            pltpu.VMEM((n_x, half, cols), f32),
            pltpu.VMEM((n_y, half, cols), f32),
            pltpu.SemaphoreType.DMA((2, max(n_x, n_y))),
            pltpu.SemaphoreType.DMA((2, max(n_x, n_y))),
            pltpu.SemaphoreType.DMA((2, max(n_x, n_y))),
            pltpu.SemaphoreType.DMA((2, max(n_x, n_y))),
        ],
        compiler_params=pltpu.CompilerParams(
            collective_id=collective_id, has_side_effects=True, vmem_limit_bytes=60 * 1024 * 1024
        ),
        cost_estimate=pl.CostEstimate(
            flops=2 * amp.size * cols, bytes_accessed=amp.size * 2 + ints.size * 2 + rows * cols * 4,
            transcendentals=0,
        ),
    )(amp, ints)


def _core_reduce_kernel(amp_ref, ints_ref, out_ref, mine_sent, theirs, send_sem, recv_sem):
    z, core = _row()
    red = lax.axis_index("red")
    other = CORES - 1 - core
    n_z, _, rows, _ = amp_ref.shape
    width = ints_ref.shape[1]
    step = n_z // 2
    barrier = pltpu.get_barrier_semaphore()
    pl.semaphore_signal(barrier, inc=1, device_id=(z, other, red), device_id_type=MESH)
    pl.semaphore_wait(barrier, 1)

    def block(k, which):
        lhs = amp_ref[pl.ds(k * step, step), which]
        product = jnp.dot(
            lhs.reshape(step * rows, lhs.shape[2]), ints_ref[...], preferred_element_type=jnp.float32
        )
        return product.reshape(step, rows, width)

    sends = []
    for k in range(2):
        mine_sent[pl.ds(k * step, step)] = block(k, other)
        c = pltpu.make_async_remote_copy(
            src_ref=mine_sent.at[pl.ds(k * step, step)], dst_ref=theirs.at[pl.ds(k * step, step)],
            send_sem=send_sem.at[k], recv_sem=recv_sem.at[k],
            device_id=(z, other, red), device_id_type=MESH,
        )
        c.start()
        sends.append(c)
    for k in range(2):
        out_ref[pl.ds(k * step, step)] = block(k, core)
    for k, c in enumerate(sends):
        c.wait()
        for i in range(k * step, (k + 1) * step):
            out_ref[i] = out_ref[i] + theirs[i]


def _core_reduce(amp, ints, collective_id):
    n_z, _, rows, _ = amp.shape
    cols = ints.shape[1]
    f32 = jnp.float32
    return pl.pallas_call(
        _core_reduce_kernel,
        out_shape=jax.ShapeDtypeStruct((n_z, rows, cols), f32),
        in_specs=[pl.BlockSpec(memory_space=pltpu.VMEM)] * 2,
        out_specs=pl.BlockSpec(memory_space=pltpu.VMEM),
        scratch_shapes=[
            pltpu.VMEM((n_z, rows, cols), f32),
            pltpu.VMEM((n_z, rows, cols), f32),
            pltpu.SemaphoreType.DMA((2,)),
            pltpu.SemaphoreType.DMA((2,)),
        ],
        compiler_params=pltpu.CompilerParams(
            collective_id=collective_id, has_side_effects=True, vmem_limit_bytes=60 * 1024 * 1024
        ),
        cost_estimate=pl.CostEstimate(
            flops=2 * amp.size * cols, bytes_accessed=amp.size * 2 + ints.size * 2 + n_z * rows * cols * 4,
            transcendentals=0,
        ),
    )(amp, ints)


def _exchange(jobs, srcs, out_shapes, n_red, collective_id):
    nbytes = sum(s.size * s.dtype.itemsize for s in srcs)
    nmax = max(_group_size(job[0], n_red) for job in jobs)
    return pl.pallas_call(
        functools.partial(_exchange_kernel, tuple(jobs), len(srcs), len(out_shapes), n_red),
        out_shape=tuple(jax.ShapeDtypeStruct(s, d) for s, d in out_shapes),
        in_specs=[pl.BlockSpec(memory_space=pl.ANY)] * len(srcs),
        out_specs=tuple(pl.BlockSpec(memory_space=pl.ANY) for _ in out_shapes),
        scratch_shapes=[
            pltpu.SemaphoreType.DMA((len(jobs), nmax)),
            pltpu.SemaphoreType.DMA((len(jobs), nmax)),
            pltpu.SemaphoreType.DMA((len(jobs),)),
        ],
        compiler_params=pltpu.CompilerParams(collective_id=collective_id, has_side_effects=True),
        cost_estimate=pl.CostEstimate(flops=0, bytes_accessed=4 * nbytes, transcendentals=0),
    )(*srcs)


def _group_size(kind, n_red):
    return {"y": NY, "x": n_red // NY}.get(kind, n_red)


def _whole(ref, pos):
    return ref


def _slot(ref, pos):
    return ref.at[pos]


def shards(amplitudes, ladder_ints, cycle_ints, occ_energy, vir_energy, slab_index):
    slab_rows, occ_local, vir_local, virt_width = amplitudes.shape
    n_red = lax.axis_size("red")
    n_blk = lax.axis_size("z") * lax.axis_size("core")
    occ_all = occ_local * n_blk
    occ_red = occ_all // n_red
    n_x = n_red // NY

    swapped = jnp.transpose(amplitudes, (0, 2, 1, 3)).reshape(
        slab_rows * vir_local, occ_local * virt_width
    )
    gathered = _gather(swapped, n_red, 0)
    gathered, amplitudes = lax.optimization_barrier((gathered, amplitudes))
    operand = gathered.reshape(n_blk // CORES, CORES, slab_rows * vir_local, occ_local * virt_width)
    product = _core_reduce(operand, cycle_ints, 4)
    cycle_own = lax.psum_scatter(product, "z", scatter_dimension=0, tiled=True)[0]
    cycle_own = jnp.transpose(
        cycle_own.reshape(slab_rows, vir_local, occ_red, virt_width), (0, 2, 1, 3)
    )

    rows = slab_rows * occ_local
    flat = amplitudes.reshape(rows, vir_local * virt_width)
    shard_piece = lax.all_gather(flat, ("z", "core"), axis=0, tiled=False)
    ladder_own = _reduce(shard_piece.reshape(n_x, NY, rows, -1), ladder_ints, n_red, 1)
    ladder_own = ladder_own.reshape(slab_rows, occ_red, -1, virt_width)

    vir_block = cycle_own.shape[2]
    orbital_ids = jnp.arange(occ_energy.shape[0], dtype=jnp.int32)
    chosen = slab_index[:, None] == orbital_ids[None, :]
    slab_energy = jnp.sum(jnp.where(chosen, occ_energy[None, :], jnp.float32(0.0)), axis=1)
    pair_energy = lax.dynamic_slice_in_dim(occ_energy, lax.axis_index("red") * occ_red, occ_red)
    first_virtual = lax.dynamic_slice_in_dim(
        vir_energy, (lax.axis_index("z") * CORES + lax.axis_index("core")) * vir_block, vir_block
    )
    denominator = (
        first_virtual[None, None, :, None]
        + vir_energy[None, None, None, :]
        - slab_energy[:, None, None, None]
        - pair_energy[None, :, None, None]
    )
    return (ladder_own + cycle_own) / denominator


def solution(mesh):
    blk = ("z", "core")
    split = Mesh(
        mesh.devices.reshape(mesh.shape["blk"] // CORES, CORES, mesh.shape["red"]),
        ("z", "core", "red"),
    )
    placed = (P(None, blk, "red", None), P("red", blk), P(blk, "red"), P(), P(), P())
    return jax.shard_map(
        shards, mesh=split, in_specs=placed, out_specs=P(None, "red", blk, None), check_vma=False
    )
```

```python
import functools

import jax
import jax.numpy as jnp
from jax import lax
from jax.experimental import pallas as pl
from jax.experimental.pallas import tpu as pltpu
from jax.sharding import Mesh, PartitionSpec as P

MESH = pl.DeviceIdType.MESH
PIECES = 1


NY = 4
CORES = 2


def _row():
    return lax.axis_index("z"), lax.axis_index("core")


def _group(kind, n_red):
    r = lax.axis_index("red")
    x, y = r // NY, lax.rem(r, NY)
    if kind == "y":
        return y, NY, lambda pos: x * NY + pos
    if kind == "x":
        return x, n_red // NY, lambda pos: pos * NY + y
    return r, n_red, lambda pos: pos


def _exchange_kernel(jobs, n_in, n_out, n_red, *refs):
    ins, outs = refs[:n_in], refs[n_in:n_in + n_out]
    send_sem, recv_sem, local_sem = refs[n_in + n_out:]
    row = _row()

    barrier = pltpu.get_barrier_semaphore()
    count = 0
    for kind in sorted(set(job[0] for job in jobs)):
        me, n, red_of = _group(kind, n_red)
        for o in range(1, n):
            pl.semaphore_signal(
                barrier, inc=1, device_id=(*row, red_of(lax.rem(me + o, n))), device_id_type=MESH
            )
            count += 1
    pl.semaphore_wait(barrier, count)

    def remote(j, pos, slot, piece=None):
        kind, si, src_view, di, dst_view = jobs[j]
        _, _, red_of = _group(kind, n_red)
        src, dst = src_view(ins[si], pos), dst_view(outs[di], slot)
        if piece is not None:
            size = src.shape[0] // PIECES
            src, dst = src.at[pl.ds(piece * size, size)], dst.at[pl.ds(piece * size, size)]
        return pltpu.make_async_remote_copy(
            src_ref=src,
            dst_ref=dst,
            send_sem=send_sem.at[j, pos],
            recv_sem=recv_sem.at[j, slot],
            device_id=(*row, red_of(pos)),
            device_id_type=MESH,
        )

    for piece in range(PIECES):
        for j, job in enumerate(jobs):
            me, n, _ = _group(job[0], n_red)
            for o in range(1, n):
                remote(j, lax.rem(me + o, n), me, piece).start()
    for j, (kind, si, src_view, di, dst_view) in enumerate(jobs):
        me, n, _ = _group(kind, n_red)
        local = pltpu.make_async_copy(
            src_view(ins[si], me), dst_view(outs[di], me), local_sem.at[j]
        )
        local.start()
        local.wait()
    for j, job in enumerate(jobs):
        me, n, _ = _group(job[0], n_red)
        for o in range(1, n):
            g = lax.rem(me + o, n)
            remote(j, g, g).wait()


def _gather_kernel(n_red, src_ref, out_ref, send_sem, recv_sem, local_sem):
    row = _row()
    ym, ny, red_y = _group("y", n_red)
    xm, nx, red_x = _group("x", n_red)
    part = src_ref.shape[0] // 2
    first, second = pl.ds(0, part), pl.ds(part, part)

    barrier = pltpu.get_barrier_semaphore()
    for o in range(1, ny):
        pl.semaphore_signal(barrier, inc=1, device_id=(*row, red_y(lax.rem(ym + o, ny))), device_id_type=MESH)
    for o in range(1, nx):
        pl.semaphore_signal(barrier, inc=1, device_id=(*row, red_x(lax.rem(xm + o, nx))), device_id_type=MESH)
    pl.semaphore_wait(barrier, ny - 1 + nx - 1)

    def copy(src, dst, stage, pos, dev):
        return pltpu.make_async_remote_copy(
            src_ref=src,
            dst_ref=dst,
            send_sem=send_sem.at[stage, pos],
            recv_sem=recv_sem.at[stage, pos],
            device_id=(*row, dev),
            device_id_type=MESH,
        )

    sent = []
    for o in range(1, ny):
        g = lax.rem(ym + o, ny)
        c = pltpu.make_async_remote_copy(
            src_ref=src_ref.at[first], dst_ref=out_ref.at[xm, ym, first],
            send_sem=send_sem.at[0, g], recv_sem=recv_sem.at[0, ym],
            device_id=(*row, red_y(g)), device_id_type=MESH,
        )
        c.start()
        sent.append(c)
    for o in range(1, nx):
        g = lax.rem(xm + o, nx)
        c = pltpu.make_async_remote_copy(
            src_ref=src_ref.at[second], dst_ref=out_ref.at[xm, ym, second],
            send_sem=send_sem.at[1, g], recv_sem=recv_sem.at[1, xm],
            device_id=(*row, red_x(g)), device_id_type=MESH,
        )
        c.start()
        sent.append(c)
    own = [
        pltpu.make_async_copy(src_ref.at[first], out_ref.at[xm, ym, first], local_sem.at[0]),
        pltpu.make_async_copy(src_ref.at[second], out_ref.at[xm, ym, second], local_sem.at[1]),
    ]
    for c in own:
        c.start()
    for c in own:
        c.wait()

    for o in range(1, ny):
        g = lax.rem(ym + o, ny)
        copy(src_ref.at[first], out_ref.at[xm, g, first], 0, g, red_y(g)).wait_recv()
    for o in range(1, nx):
        g = lax.rem(xm + o, nx)
        c = pltpu.make_async_remote_copy(
            src_ref=out_ref.at[xm, :, first], dst_ref=out_ref.at[xm, :, first],
            send_sem=send_sem.at[2, g], recv_sem=recv_sem.at[2, xm],
            device_id=(*row, red_x(g)), device_id_type=MESH,
        )
        c.start()
        sent.append(c)
    for o in range(1, nx):
        g = lax.rem(xm + o, nx)
        copy(src_ref.at[second], out_ref.at[g, ym, second], 1, g, red_x(g)).wait_recv()
    for o in range(1, ny):
        g = lax.rem(ym + o, ny)
        c = pltpu.make_async_remote_copy(
            src_ref=out_ref.at[:, ym, second], dst_ref=out_ref.at[:, ym, second],
            send_sem=send_sem.at[3, g], recv_sem=recv_sem.at[3, ym],
            device_id=(*row, red_y(g)), device_id_type=MESH,
        )
        c.start()
        sent.append(c)

    for c in sent:
        c.wait_send()
    for o in range(1, nx):
        g = lax.rem(xm + o, nx)
        copy(out_ref.at[g, :, first], out_ref.at[g, :, first], 2, g, red_x(g)).wait_recv()
    for o in range(1, ny):
        g = lax.rem(ym + o, ny)
        copy(out_ref.at[:, g, second], out_ref.at[:, g, second], 3, g, red_y(g)).wait_recv()


def _gather(block, n_red, collective_id):
    n_x = n_red // NY
    nbytes = block.size * block.dtype.itemsize
    return pl.pallas_call(
        functools.partial(_gather_kernel, n_red),
        out_shape=jax.ShapeDtypeStruct((n_x, NY) + block.shape, block.dtype),
        in_specs=[pl.BlockSpec(memory_space=pl.ANY)],
        out_specs=pl.BlockSpec(memory_space=pl.ANY),
        scratch_shapes=[
            pltpu.SemaphoreType.DMA((4, max(n_x, NY))),
            pltpu.SemaphoreType.DMA((4, max(n_x, NY))),
            pltpu.SemaphoreType.DMA((2,)),
        ],
        compiler_params=pltpu.CompilerParams(collective_id=collective_id, has_side_effects=True),
        cost_estimate=pl.CostEstimate(flops=0, bytes_accessed=2 * n_red * nbytes, transcendentals=0),
    )(block)


def _reduce_kernel(n_red, amp_ref, ints_ref, out_ref, ra, rb, pa, pb, sa, sb, qa, qb, send1, recv1, send2, recv2):
    row = _row()
    ym, ny, red_y = _group("y", n_red)
    xm, nx, red_x = _group("x", n_red)
    half = ra.shape[2]
    first, second = pl.ds(0, half), pl.ds(half, half)

    barrier = pltpu.get_barrier_semaphore()
    for o in range(1, ny):
        pl.semaphore_signal(barrier, inc=1, device_id=(*row, red_y(lax.rem(ym + o, ny))), device_id_type=MESH)
    for o in range(1, nx):
        pl.semaphore_signal(barrier, inc=1, device_id=(*row, red_x(lax.rem(xm + o, nx))), device_id_type=MESH)
    pl.semaphore_wait(barrier, ny - 1 + nx - 1)

    def copy(src, dst, send, recv, dev):
        return pltpu.make_async_remote_copy(
            src_ref=src, dst_ref=dst, send_sem=send, recv_sem=recv,
            device_id=(*row, dev), device_id_type=MESH,
        )

    width = ints_ref.shape[1]

    def block(lhs):
        slots = lhs.shape[0]
        flat = lhs.reshape(slots * half, lhs.shape[2])
        product = jnp.dot(flat, ints_ref[...], preferred_element_type=jnp.float32)
        return product.reshape(slots, half, width)

    sent = []
    for o in range(1, max(nx, ny)):
        if o < ny:
            g = lax.rem(ym + o, ny)
            pa[g] = block(amp_ref[:, g, first])
            c = copy(pa.at[g], ra.at[ym], send1.at[0, g], recv1.at[0, ym], red_y(g))
            c.start()
            sent.append(c)
        if o < nx:
            g = lax.rem(xm + o, nx)
            pb[g] = block(amp_ref[g, :, second])
            c = copy(pb.at[g], rb.at[xm], send1.at[1, g], recv1.at[1, xm], red_x(g))
            c.start()
            sent.append(c)
    ra[ym] = block(amp_ref[:, ym, first])
    rb[xm] = block(amp_ref[xm, :, second])

    for o in range(1, ny):
        g = lax.rem(ym + o, ny)
        copy(pa.at[g], ra.at[g], send1.at[0, g], recv1.at[0, g], red_y(g)).wait_recv()
    for o in range(1, nx):
        g = lax.rem(xm + o, nx)
        sa[g] = ra[0, g] + ra[1, g] + ra[2, g] + ra[3, g]
        c = copy(sa.at[g], qa.at[xm], send2.at[0, g], recv2.at[0, xm], red_x(g))
        c.start()
        sent.append(c)
    sa[xm] = ra[0, xm] + ra[1, xm] + ra[2, xm] + ra[3, xm]

    for o in range(1, nx):
        g = lax.rem(xm + o, nx)
        copy(pb.at[g], rb.at[g], send1.at[1, g], recv1.at[1, g], red_x(g)).wait_recv()
    for o in range(1, ny):
        g = lax.rem(ym + o, ny)
        sb[g] = rb[0, g] + rb[1, g] + rb[2, g] + rb[3, g]
        c = copy(sb.at[g], qb.at[ym], send2.at[1, g], recv2.at[1, ym], red_y(g))
        c.start()
        sent.append(c)
    sb[ym] = rb[0, ym] + rb[1, ym] + rb[2, ym] + rb[3, ym]

    for c in sent:
        c.wait_send()
    total_a = sa[xm]
    for o in range(1, nx):
        g = lax.rem(xm + o, nx)
        copy(sa.at[g], qa.at[g], send2.at[0, g], recv2.at[0, g], red_x(g)).wait_recv()
        total_a = total_a + qa[g]
    total_b = sb[ym]
    for o in range(1, ny):
        g = lax.rem(ym + o, ny)
        copy(sb.at[g], qb.at[g], send2.at[1, g], recv2.at[1, g], red_y(g)).wait_recv()
        total_b = total_b + qb[g]
    out_ref[first] = total_a
    out_ref[second] = total_b


def _reduce(amp, ints, n_red, collective_id):
    n_x, n_y, rows, _ = amp.shape
    cols = ints.shape[1]
    half = rows // 2
    f32 = jnp.float32
    return pl.pallas_call(
        functools.partial(_reduce_kernel, n_red),
        out_shape=jax.ShapeDtypeStruct((rows, cols), f32),
        in_specs=[pl.BlockSpec(memory_space=pltpu.VMEM)] * 2,
        out_specs=pl.BlockSpec(memory_space=pltpu.VMEM),
        scratch_shapes=[
            pltpu.VMEM((n_y, n_x, half, cols), f32),
            pltpu.VMEM((n_x, n_y, half, cols), f32),
            pltpu.VMEM((n_y, n_x, half, cols), f32),
            pltpu.VMEM((n_x, n_y, half, cols), f32),
            pltpu.VMEM((n_x, half, cols), f32),
            pltpu.VMEM((n_y, half, cols), f32),
            pltpu.VMEM((n_x, half, cols), f32),
            pltpu.VMEM((n_y, half, cols), f32),
            pltpu.SemaphoreType.DMA((2, max(n_x, n_y))),
            pltpu.SemaphoreType.DMA((2, max(n_x, n_y))),
            pltpu.SemaphoreType.DMA((2, max(n_x, n_y))),
            pltpu.SemaphoreType.DMA((2, max(n_x, n_y))),
        ],
        compiler_params=pltpu.CompilerParams(
            collective_id=collective_id, has_side_effects=True, vmem_limit_bytes=60 * 1024 * 1024
        ),
        cost_estimate=pl.CostEstimate(
            flops=2 * amp.size * cols, bytes_accessed=amp.size * 2 + ints.size * 2 + rows * cols * 4,
            transcendentals=0,
        ),
    )(amp, ints)


def _core_reduce_kernel(amp_ref, ints_ref, out_ref, mine_sent, theirs, send_sem, recv_sem):
    z, core = _row()
    red = lax.axis_index("red")
    other = CORES - 1 - core
    n_z, _, rows, _ = amp_ref.shape
    width = ints_ref.shape[1]
    step = n_z // 2
    barrier = pltpu.get_barrier_semaphore()
    pl.semaphore_signal(barrier, inc=1, device_id=(z, other, red), device_id_type=MESH)
    pl.semaphore_wait(barrier, 1)

    def block(k, which):
        lhs = amp_ref[pl.ds(k * step, step), which]
        product = jnp.dot(
            lhs.reshape(step * rows, lhs.shape[2]), ints_ref[...], preferred_element_type=jnp.float32
        )
        return product.reshape(step, rows, width)

    sends = []
    for k in range(2):
        mine_sent[pl.ds(k * step, step)] = block(k, other)
        c = pltpu.make_async_remote_copy(
            src_ref=mine_sent.at[pl.ds(k * step, step)], dst_ref=theirs.at[pl.ds(k * step, step)],
            send_sem=send_sem.at[k], recv_sem=recv_sem.at[k],
            device_id=(z, other, red), device_id_type=MESH,
        )
        c.start()
        sends.append(c)
    for k in range(2):
        out_ref[pl.ds(k * step, step)] = block(k, core)
    for k, c in enumerate(sends):
        c.wait()
        for i in range(k * step, (k + 1) * step):
            out_ref[i] = out_ref[i] + theirs[i]


def _core_reduce(amp, ints, collective_id):
    n_z, _, rows, _ = amp.shape
    cols = ints.shape[1]
    f32 = jnp.float32
    return pl.pallas_call(
        _core_reduce_kernel,
        out_shape=jax.ShapeDtypeStruct((n_z, rows, cols), f32),
        in_specs=[pl.BlockSpec(memory_space=pltpu.VMEM)] * 2,
        out_specs=pl.BlockSpec(memory_space=pltpu.VMEM),
        scratch_shapes=[
            pltpu.VMEM((n_z, rows, cols), f32),
            pltpu.VMEM((n_z, rows, cols), f32),
            pltpu.SemaphoreType.DMA((2,)),
            pltpu.SemaphoreType.DMA((2,)),
        ],
        compiler_params=pltpu.CompilerParams(
            collective_id=collective_id, has_side_effects=True, vmem_limit_bytes=60 * 1024 * 1024
        ),
        cost_estimate=pl.CostEstimate(
            flops=2 * amp.size * cols, bytes_accessed=amp.size * 2 + ints.size * 2 + n_z * rows * cols * 4,
            transcendentals=0,
        ),
    )(amp, ints)


def _exchange(jobs, srcs, out_shapes, n_red, collective_id):
    nbytes = sum(s.size * s.dtype.itemsize for s in srcs)
    nmax = max(_group_size(job[0], n_red) for job in jobs)
    return pl.pallas_call(
        functools.partial(_exchange_kernel, tuple(jobs), len(srcs), len(out_shapes), n_red),
        out_shape=tuple(jax.ShapeDtypeStruct(s, d) for s, d in out_shapes),
        in_specs=[pl.BlockSpec(memory_space=pl.ANY)] * len(srcs),
        out_specs=tuple(pl.BlockSpec(memory_space=pl.ANY) for _ in out_shapes),
        scratch_shapes=[
            pltpu.SemaphoreType.DMA((len(jobs), nmax)),
            pltpu.SemaphoreType.DMA((len(jobs), nmax)),
            pltpu.SemaphoreType.DMA((len(jobs),)),
        ],
        compiler_params=pltpu.CompilerParams(collective_id=collective_id, has_side_effects=True),
        cost_estimate=pl.CostEstimate(flops=0, bytes_accessed=4 * nbytes, transcendentals=0),
    )(*srcs)


def _group_size(kind, n_red):
    return {"y": NY, "x": n_red // NY}.get(kind, n_red)


def _whole(ref, pos):
    return ref


def _slot(ref, pos):
    return ref.at[pos]


def shards(amplitudes, ladder_ints, cycle_ints, occ_energy, vir_energy, slab_index):
    slab_rows, occ_local, vir_local, virt_width = amplitudes.shape
    n_red = lax.axis_size("red")
    n_blk = lax.axis_size("z") * lax.axis_size("core")
    occ_all = occ_local * n_blk
    occ_red = occ_all // n_red
    n_x = n_red // NY

    swapped = jnp.transpose(amplitudes, (0, 2, 1, 3)).reshape(
        slab_rows * vir_local, occ_local * virt_width
    )
    gathered = _gather(swapped, n_red, 0)
    operand = gathered.reshape(n_blk // CORES, CORES, slab_rows * vir_local, occ_local * virt_width)
    product = _core_reduce(operand, cycle_ints, 4)
    cycle_own = lax.psum_scatter(product, "z", scatter_dimension=0, tiled=True)[0]
    cycle_own = jnp.transpose(
        cycle_own.reshape(slab_rows, vir_local, occ_red, virt_width), (0, 2, 1, 3)
    )

    rows = slab_rows * occ_local
    flat = amplitudes.reshape(rows, vir_local * virt_width)
    shard_piece = lax.all_gather(flat, ("z", "core"), axis=0, tiled=False)
    ladder_own = _reduce(shard_piece.reshape(n_x, NY, rows, -1), ladder_ints, n_red, 1)
    ladder_own = ladder_own.reshape(slab_rows, occ_red, -1, virt_width)

    vir_block = cycle_own.shape[2]
    orbital_ids = jnp.arange(occ_energy.shape[0], dtype=jnp.int32)
    chosen = slab_index[:, None] == orbital_ids[None, :]
    slab_energy = jnp.sum(jnp.where(chosen, occ_energy[None, :], jnp.float32(0.0)), axis=1)
    pair_energy = lax.dynamic_slice_in_dim(occ_energy, lax.axis_index("red") * occ_red, occ_red)
    first_virtual = lax.dynamic_slice_in_dim(
        vir_energy, (lax.axis_index("z") * CORES + lax.axis_index("core")) * vir_block, vir_block
    )
    denominator = (
        first_virtual[None, None, :, None]
        + vir_energy[None, None, None, :]
        - slab_energy[:, None, None, None]
        - pair_energy[None, :, None, None]
    )
    return (ladder_own + cycle_own) / denominator


def solution(mesh):
    blk = ("z", "core")
    split = Mesh(
        mesh.devices.reshape(mesh.shape["blk"] // CORES, CORES, mesh.shape["red"]),
        ("z", "core", "red"),
    )
    placed = (P(None, blk, "red", None), P("red", blk), P(blk, "red"), P(), P(), P())
    return jax.shard_map(
        shards, mesh=split, in_specs=placed, out_specs=P(None, "red", blk, None), check_vma=False
    )
```

```python
import functools

import jax
import jax.numpy as jnp
from jax import lax
from jax.experimental import pallas as pl
from jax.experimental.pallas import tpu as pltpu
from jax.sharding import Mesh, PartitionSpec as P

MESH = pl.DeviceIdType.MESH
PIECES = 1


NY = 4
CORES = 2


def _row():
    return lax.axis_index("z"), lax.axis_index("core")


def _group(kind, n_red):
    r = lax.axis_index("red")
    x, y = r // NY, lax.rem(r, NY)
    if kind == "y":
        return y, NY, lambda pos: x * NY + pos
    if kind == "x":
        return x, n_red // NY, lambda pos: pos * NY + y
    return r, n_red, lambda pos: pos


def _exchange_kernel(jobs, n_in, n_out, n_red, *refs):
    ins, outs = refs[:n_in], refs[n_in:n_in + n_out]
    send_sem, recv_sem, local_sem = refs[n_in + n_out:]
    row = _row()

    barrier = pltpu.get_barrier_semaphore()
    count = 0
    for kind in sorted(set(job[0] for job in jobs)):
        me, n, red_of = _group(kind, n_red)
        for o in range(1, n):
            pl.semaphore_signal(
                barrier, inc=1, device_id=(*row, red_of(lax.rem(me + o, n))), device_id_type=MESH
            )
            count += 1
    pl.semaphore_wait(barrier, count)

    def remote(j, pos, slot, piece=None):
        kind, si, src_view, di, dst_view = jobs[j]
        _, _, red_of = _group(kind, n_red)
        src, dst = src_view(ins[si], pos), dst_view(outs[di], slot)
        if piece is not None:
            size = src.shape[0] // PIECES
            src, dst = src.at[pl.ds(piece * size, size)], dst.at[pl.ds(piece * size, size)]
        return pltpu.make_async_remote_copy(
            src_ref=src,
            dst_ref=dst,
            send_sem=send_sem.at[j, pos],
            recv_sem=recv_sem.at[j, slot],
            device_id=(*row, red_of(pos)),
            device_id_type=MESH,
        )

    for piece in range(PIECES):
        for j, job in enumerate(jobs):
            me, n, _ = _group(job[0], n_red)
            for o in range(1, n):
                remote(j, lax.rem(me + o, n), me, piece).start()
    for j, (kind, si, src_view, di, dst_view) in enumerate(jobs):
        me, n, _ = _group(kind, n_red)
        local = pltpu.make_async_copy(
            src_view(ins[si], me), dst_view(outs[di], me), local_sem.at[j]
        )
        local.start()
        local.wait()
    for j, job in enumerate(jobs):
        me, n, _ = _group(job[0], n_red)
        for o in range(1, n):
            g = lax.rem(me + o, n)
            remote(j, g, g).wait()


def _gather_kernel(n_red, src_ref, out_ref, send_sem, recv_sem, local_sem):
    row = _row()
    ym, ny, red_y = _group("y", n_red)
    xm, nx, red_x = _group("x", n_red)
    part = src_ref.shape[0] // 2
    first, second = pl.ds(0, part), pl.ds(part, part)

    barrier = pltpu.get_barrier_semaphore()
    for o in range(1, ny):
        pl.semaphore_signal(barrier, inc=1, device_id=(*row, red_y(lax.rem(ym + o, ny))), device_id_type=MESH)
    for o in range(1, nx):
        pl.semaphore_signal(barrier, inc=1, device_id=(*row, red_x(lax.rem(xm + o, nx))), device_id_type=MESH)
    pl.semaphore_wait(barrier, ny - 1 + nx - 1)

    def copy(src, dst, stage, pos, dev):
        return pltpu.make_async_remote_copy(
            src_ref=src,
            dst_ref=dst,
            send_sem=send_sem.at[stage, pos],
            recv_sem=recv_sem.at[stage, pos],
            device_id=(*row, dev),
            device_id_type=MESH,
        )

    sent = []
    for o in range(1, ny):
        g = lax.rem(ym + o, ny)
        c = pltpu.make_async_remote_copy(
            src_ref=src_ref.at[first], dst_ref=out_ref.at[xm, ym, first],
            send_sem=send_sem.at[0, g], recv_sem=recv_sem.at[0, ym],
            device_id=(*row, red_y(g)), device_id_type=MESH,
        )
        c.start()
        sent.append(c)
    for o in range(1, nx):
        g = lax.rem(xm + o, nx)
        c = pltpu.make_async_remote_copy(
            src_ref=src_ref.at[second], dst_ref=out_ref.at[xm, ym, second],
            send_sem=send_sem.at[1, g], recv_sem=recv_sem.at[1, xm],
            device_id=(*row, red_x(g)), device_id_type=MESH,
        )
        c.start()
        sent.append(c)
    own = [
        pltpu.make_async_copy(src_ref.at[first], out_ref.at[xm, ym, first], local_sem.at[0]),
        pltpu.make_async_copy(src_ref.at[second], out_ref.at[xm, ym, second], local_sem.at[1]),
    ]
    for c in own:
        c.start()
    for c in own:
        c.wait()

    for o in range(1, ny):
        g = lax.rem(ym + o, ny)
        copy(src_ref.at[first], out_ref.at[xm, g, first], 0, g, red_y(g)).wait_recv()
    for o in range(1, nx):
        g = lax.rem(xm + o, nx)
        c = pltpu.make_async_remote_copy(
            src_ref=out_ref.at[xm, :, first], dst_ref=out_ref.at[xm, :, first],
            send_sem=send_sem.at[2, g], recv_sem=recv_sem.at[2, xm],
            device_id=(*row, red_x(g)), device_id_type=MESH,
        )
        c.start()
        sent.append(c)
    for o in range(1, nx):
        g = lax.rem(xm + o, nx)
        copy(src_ref.at[second], out_ref.at[g, ym, second], 1, g, red_x(g)).wait_recv()
    for o in range(1, ny):
        g = lax.rem(ym + o, ny)
        c = pltpu.make_async_remote_copy(
            src_ref=out_ref.at[:, ym, second], dst_ref=out_ref.at[:, ym, second],
            send_sem=send_sem.at[3, g], recv_sem=recv_sem.at[3, ym],
            device_id=(*row, red_y(g)), device_id_type=MESH,
        )
        c.start()
        sent.append(c)

    for c in sent:
        c.wait_send()
    for o in range(1, nx):
        g = lax.rem(xm + o, nx)
        copy(out_ref.at[g, :, first], out_ref.at[g, :, first], 2, g, red_x(g)).wait_recv()
    for o in range(1, ny):
        g = lax.rem(ym + o, ny)
        copy(out_ref.at[:, g, second], out_ref.at[:, g, second], 3, g, red_y(g)).wait_recv()


def _gather(block, n_red, collective_id):
    n_x = n_red // NY
    nbytes = block.size * block.dtype.itemsize
    return pl.pallas_call(
        functools.partial(_gather_kernel, n_red),
        out_shape=jax.ShapeDtypeStruct((n_x, NY) + block.shape, block.dtype),
        in_specs=[pl.BlockSpec(memory_space=pl.ANY)],
        out_specs=pl.BlockSpec(memory_space=pl.ANY),
        scratch_shapes=[
            pltpu.SemaphoreType.DMA((4, max(n_x, NY))),
            pltpu.SemaphoreType.DMA((4, max(n_x, NY))),
            pltpu.SemaphoreType.DMA((2,)),
        ],
        compiler_params=pltpu.CompilerParams(collective_id=collective_id, has_side_effects=True),
        cost_estimate=pl.CostEstimate(flops=0, bytes_accessed=2 * n_red * nbytes, transcendentals=0),
    )(block)


def _reduce_kernel(n_red, amp_ref, ints_ref, out_ref, ra, rb, pa, pb, sa, sb, qa, qb, send1, recv1, send2, recv2):
    row = _row()
    ym, ny, red_y = _group("y", n_red)
    xm, nx, red_x = _group("x", n_red)
    half = ra.shape[2]
    first, second = pl.ds(0, half), pl.ds(half, half)

    barrier = pltpu.get_barrier_semaphore()
    for o in range(1, ny):
        pl.semaphore_signal(barrier, inc=1, device_id=(*row, red_y(lax.rem(ym + o, ny))), device_id_type=MESH)
    for o in range(1, nx):
        pl.semaphore_signal(barrier, inc=1, device_id=(*row, red_x(lax.rem(xm + o, nx))), device_id_type=MESH)

    def copy(src, dst, send, recv, dev):
        return pltpu.make_async_remote_copy(
            src_ref=src, dst_ref=dst, send_sem=send, recv_sem=recv,
            device_id=(*row, dev), device_id_type=MESH,
        )

    width = ints_ref.shape[1]

    def block(lhs):
        slots = lhs.shape[0]
        flat = lhs.reshape(slots * half, lhs.shape[2])
        product = jnp.dot(flat, ints_ref[...], preferred_element_type=jnp.float32)
        return product.reshape(slots, half, width)

    pa[lax.rem(ym + 1, ny)] = block(amp_ref[:, lax.rem(ym + 1, ny), first])
    pb[lax.rem(xm + 1, nx)] = block(amp_ref[lax.rem(xm + 1, nx), :, second])
    pl.semaphore_wait(barrier, ny - 1 + nx - 1)
    sent = []
    for o in range(1, max(nx, ny)):
        if o < ny:
            g = lax.rem(ym + o, ny)
            if o > 1:
                pa[g] = block(amp_ref[:, g, first])
            c = copy(pa.at[g], ra.at[ym], send1.at[0, g], recv1.at[0, ym], red_y(g))
            c.start()
            sent.append(c)
        if o < nx:
            g = lax.rem(xm + o, nx)
            if o > 1:
                pb[g] = block(amp_ref[g, :, second])
            c = copy(pb.at[g], rb.at[xm], send1.at[1, g], recv1.at[1, xm], red_x(g))
            c.start()
            sent.append(c)
    ra[ym] = block(amp_ref[:, ym, first])
    rb[xm] = block(amp_ref[xm, :, second])

    for o in range(1, ny):
        g = lax.rem(ym + o, ny)
        copy(pa.at[g], ra.at[g], send1.at[0, g], recv1.at[0, g], red_y(g)).wait_recv()
    for o in range(1, nx):
        g = lax.rem(xm + o, nx)
        sa[g] = ra[0, g] + ra[1, g] + ra[2, g] + ra[3, g]
        c = copy(sa.at[g], qa.at[xm], send2.at[0, g], recv2.at[0, xm], red_x(g))
        c.start()
        sent.append(c)
    sa[xm] = ra[0, xm] + ra[1, xm] + ra[2, xm] + ra[3, xm]

    for o in range(1, nx):
        g = lax.rem(xm + o, nx)
        copy(pb.at[g], rb.at[g], send1.at[1, g], recv1.at[1, g], red_x(g)).wait_recv()
    for o in range(1, ny):
        g = lax.rem(ym + o, ny)
        sb[g] = rb[0, g] + rb[1, g] + rb[2, g] + rb[3, g]
        c = copy(sb.at[g], qb.at[ym], send2.at[1, g], recv2.at[1, ym], red_y(g))
        c.start()
        sent.append(c)
    sb[ym] = rb[0, ym] + rb[1, ym] + rb[2, ym] + rb[3, ym]

    for c in sent:
        c.wait_send()
    total_a = sa[xm]
    for o in range(1, nx):
        g = lax.rem(xm + o, nx)
        copy(sa.at[g], qa.at[g], send2.at[0, g], recv2.at[0, g], red_x(g)).wait_recv()
        total_a = total_a + qa[g]
    total_b = sb[ym]
    for o in range(1, ny):
        g = lax.rem(ym + o, ny)
        copy(sb.at[g], qb.at[g], send2.at[1, g], recv2.at[1, g], red_y(g)).wait_recv()
        total_b = total_b + qb[g]
    out_ref[first] = total_a
    out_ref[second] = total_b


def _reduce(amp, ints, n_red, collective_id):
    n_x, n_y, rows, _ = amp.shape
    cols = ints.shape[1]
    half = rows // 2
    f32 = jnp.float32
    return pl.pallas_call(
        functools.partial(_reduce_kernel, n_red),
        out_shape=jax.ShapeDtypeStruct((rows, cols), f32),
        in_specs=[pl.BlockSpec(memory_space=pltpu.VMEM)] * 2,
        out_specs=pl.BlockSpec(memory_space=pltpu.VMEM),
        scratch_shapes=[
            pltpu.VMEM((n_y, n_x, half, cols), f32),
            pltpu.VMEM((n_x, n_y, half, cols), f32),
            pltpu.VMEM((n_y, n_x, half, cols), f32),
            pltpu.VMEM((n_x, n_y, half, cols), f32),
            pltpu.VMEM((n_x, half, cols), f32),
            pltpu.VMEM((n_y, half, cols), f32),
            pltpu.VMEM((n_x, half, cols), f32),
            pltpu.VMEM((n_y, half, cols), f32),
            pltpu.SemaphoreType.DMA((2, max(n_x, n_y))),
            pltpu.SemaphoreType.DMA((2, max(n_x, n_y))),
            pltpu.SemaphoreType.DMA((2, max(n_x, n_y))),
            pltpu.SemaphoreType.DMA((2, max(n_x, n_y))),
        ],
        compiler_params=pltpu.CompilerParams(
            collective_id=collective_id, has_side_effects=True, vmem_limit_bytes=60 * 1024 * 1024
        ),
        cost_estimate=pl.CostEstimate(
            flops=2 * amp.size * cols, bytes_accessed=amp.size * 2 + ints.size * 2 + rows * cols * 4,
            transcendentals=0,
        ),
    )(amp, ints)


def _core_reduce_kernel(amp_ref, ints_ref, out_ref, mine_sent, theirs, send_sem, recv_sem):
    z, core = _row()
    red = lax.axis_index("red")
    other = CORES - 1 - core
    n_z, _, rows, _ = amp_ref.shape
    width = ints_ref.shape[1]
    step = n_z // 2
    barrier = pltpu.get_barrier_semaphore()
    pl.semaphore_signal(barrier, inc=1, device_id=(z, other, red), device_id_type=MESH)

    def block(k, which):
        lhs = amp_ref[pl.ds(k * step, step), which]
        product = jnp.dot(
            lhs.reshape(step * rows, lhs.shape[2]), ints_ref[...], preferred_element_type=jnp.float32
        )
        return product.reshape(step, rows, width)

    sends = []
    for k in range(2):
        mine_sent[pl.ds(k * step, step)] = block(k, other)
        if k == 0:
            pl.semaphore_wait(barrier, 1)
        c = pltpu.make_async_remote_copy(
            src_ref=mine_sent.at[pl.ds(k * step, step)], dst_ref=theirs.at[pl.ds(k * step, step)],
            send_sem=send_sem.at[k], recv_sem=recv_sem.at[k],
            device_id=(z, other, red), device_id_type=MESH,
        )
        c.start()
        sends.append(c)
    for k in range(2):
        out_ref[pl.ds(k * step, step)] = block(k, core)
    for k, c in enumerate(sends):
        c.wait()
        for i in range(k * step, (k + 1) * step):
            out_ref[i] = out_ref[i] + theirs[i]


def _core_reduce(amp, ints, collective_id):
    n_z, _, rows, _ = amp.shape
    cols = ints.shape[1]
    f32 = jnp.float32
    return pl.pallas_call(
        _core_reduce_kernel,
        out_shape=jax.ShapeDtypeStruct((n_z, rows, cols), f32),
        in_specs=[pl.BlockSpec(memory_space=pltpu.VMEM)] * 2,
        out_specs=pl.BlockSpec(memory_space=pltpu.VMEM),
        scratch_shapes=[
            pltpu.VMEM((n_z, rows, cols), f32),
            pltpu.VMEM((n_z, rows, cols), f32),
            pltpu.SemaphoreType.DMA((2,)),
            pltpu.SemaphoreType.DMA((2,)),
        ],
        compiler_params=pltpu.CompilerParams(
            collective_id=collective_id, has_side_effects=True, vmem_limit_bytes=60 * 1024 * 1024
        ),
        cost_estimate=pl.CostEstimate(
            flops=2 * amp.size * cols, bytes_accessed=amp.size * 2 + ints.size * 2 + n_z * rows * cols * 4,
            transcendentals=0,
        ),
    )(amp, ints)


def _exchange(jobs, srcs, out_shapes, n_red, collective_id):
    nbytes = sum(s.size * s.dtype.itemsize for s in srcs)
    nmax = max(_group_size(job[0], n_red) for job in jobs)
    return pl.pallas_call(
        functools.partial(_exchange_kernel, tuple(jobs), len(srcs), len(out_shapes), n_red),
        out_shape=tuple(jax.ShapeDtypeStruct(s, d) for s, d in out_shapes),
        in_specs=[pl.BlockSpec(memory_space=pl.ANY)] * len(srcs),
        out_specs=tuple(pl.BlockSpec(memory_space=pl.ANY) for _ in out_shapes),
        scratch_shapes=[
            pltpu.SemaphoreType.DMA((len(jobs), nmax)),
            pltpu.SemaphoreType.DMA((len(jobs), nmax)),
            pltpu.SemaphoreType.DMA((len(jobs),)),
        ],
        compiler_params=pltpu.CompilerParams(collective_id=collective_id, has_side_effects=True),
        cost_estimate=pl.CostEstimate(flops=0, bytes_accessed=4 * nbytes, transcendentals=0),
    )(*srcs)


def _group_size(kind, n_red):
    return {"y": NY, "x": n_red // NY}.get(kind, n_red)


def _whole(ref, pos):
    return ref


def _slot(ref, pos):
    return ref.at[pos]


def shards(amplitudes, ladder_ints, cycle_ints, occ_energy, vir_energy, slab_index):
    slab_rows, occ_local, vir_local, virt_width = amplitudes.shape
    n_red = lax.axis_size("red")
    n_blk = lax.axis_size("z") * lax.axis_size("core")
    occ_all = occ_local * n_blk
    occ_red = occ_all // n_red
    n_x = n_red // NY

    swapped = jnp.transpose(amplitudes, (0, 2, 1, 3)).reshape(
        slab_rows * vir_local, occ_local * virt_width
    )
    gathered = _gather(swapped, n_red, 0)
    operand = gathered.reshape(n_blk // CORES, CORES, slab_rows * vir_local, occ_local * virt_width)
    product = _core_reduce(operand, cycle_ints, 4)
    cycle_own = lax.psum_scatter(product, "z", scatter_dimension=0, tiled=True)[0]
    cycle_own = jnp.transpose(
        cycle_own.reshape(slab_rows, vir_local, occ_red, virt_width), (0, 2, 1, 3)
    )

    rows = slab_rows * occ_local
    flat = amplitudes.reshape(rows, vir_local * virt_width)
    shard_piece = lax.all_gather(flat, ("z", "core"), axis=0, tiled=False)
    ladder_own = _reduce(shard_piece.reshape(n_x, NY, rows, -1), ladder_ints, n_red, 1)
    ladder_own = ladder_own.reshape(slab_rows, occ_red, -1, virt_width)

    vir_block = cycle_own.shape[2]
    orbital_ids = jnp.arange(occ_energy.shape[0], dtype=jnp.int32)
    chosen = slab_index[:, None] == orbital_ids[None, :]
    slab_energy = jnp.sum(jnp.where(chosen, occ_energy[None, :], jnp.float32(0.0)), axis=1)
    pair_energy = lax.dynamic_slice_in_dim(occ_energy, lax.axis_index("red") * occ_red, occ_red)
    first_virtual = lax.dynamic_slice_in_dim(
        vir_energy, (lax.axis_index("z") * CORES + lax.axis_index("core")) * vir_block, vir_block
    )
    denominator = (
        first_virtual[None, None, :, None]
        + vir_energy[None, None, None, :]
        - slab_energy[:, None, None, None]
        - pair_energy[None, :, None, None]
    )
    return (ladder_own + cycle_own) / denominator


def solution(mesh):
    blk = ("z", "core")
    split = Mesh(
        mesh.devices.reshape(mesh.shape["blk"] // CORES, CORES, mesh.shape["red"]),
        ("z", "core", "red"),
    )
    placed = (P(None, blk, "red", None), P("red", blk), P(blk, "red"), P(), P(), P())
    return jax.shard_map(
        shards, mesh=split, in_specs=placed, out_specs=P(None, "red", blk, None), check_vma=False
    )
```

```python
import functools

import jax
import jax.numpy as jnp
from jax import lax
from jax.experimental import pallas as pl
from jax.experimental.pallas import tpu as pltpu
from jax.sharding import Mesh, PartitionSpec as P

MESH = pl.DeviceIdType.MESH


NY = 4
CORES = 2


def _row():
    return lax.axis_index("z"), lax.axis_index("core")


def _group(kind, n_red):
    r = lax.axis_index("red")
    x, y = r // NY, lax.rem(r, NY)
    if kind == "y":
        return y, NY, lambda pos: x * NY + pos
    if kind == "x":
        return x, n_red // NY, lambda pos: pos * NY + y
    return r, n_red, lambda pos: pos


def _gather_kernel(n_red, src_ref, out_ref, send_sem, recv_sem, local_sem):
    row = _row()
    ym, ny, red_y = _group("y", n_red)
    xm, nx, red_x = _group("x", n_red)
    part = src_ref.shape[0] // 2
    first, second = pl.ds(0, part), pl.ds(part, part)

    barrier = pltpu.get_barrier_semaphore()
    for o in range(1, ny):
        pl.semaphore_signal(barrier, inc=1, device_id=(*row, red_y(lax.rem(ym + o, ny))), device_id_type=MESH)
    for o in range(1, nx):
        pl.semaphore_signal(barrier, inc=1, device_id=(*row, red_x(lax.rem(xm + o, nx))), device_id_type=MESH)
    pl.semaphore_wait(barrier, ny - 1 + nx - 1)

    def copy(src, dst, stage, pos, dev):
        return pltpu.make_async_remote_copy(
            src_ref=src,
            dst_ref=dst,
            send_sem=send_sem.at[stage, pos],
            recv_sem=recv_sem.at[stage, pos],
            device_id=(*row, dev),
            device_id_type=MESH,
        )

    sent = []
    for o in range(1, ny):
        g = lax.rem(ym + o, ny)
        c = pltpu.make_async_remote_copy(
            src_ref=src_ref.at[first], dst_ref=out_ref.at[xm, ym, first],
            send_sem=send_sem.at[0, g], recv_sem=recv_sem.at[0, ym],
            device_id=(*row, red_y(g)), device_id_type=MESH,
        )
        c.start()
        sent.append(c)
    for o in range(1, nx):
        g = lax.rem(xm + o, nx)
        c = pltpu.make_async_remote_copy(
            src_ref=src_ref.at[second], dst_ref=out_ref.at[xm, ym, second],
            send_sem=send_sem.at[1, g], recv_sem=recv_sem.at[1, xm],
            device_id=(*row, red_x(g)), device_id_type=MESH,
        )
        c.start()
        sent.append(c)
    own = [
        pltpu.make_async_copy(src_ref.at[first], out_ref.at[xm, ym, first], local_sem.at[0]),
        pltpu.make_async_copy(src_ref.at[second], out_ref.at[xm, ym, second], local_sem.at[1]),
    ]
    for c in own:
        c.start()
    for c in own:
        c.wait()

    for o in range(1, ny):
        g = lax.rem(ym + o, ny)
        copy(src_ref.at[first], out_ref.at[xm, g, first], 0, g, red_y(g)).wait_recv()
    for o in range(1, nx):
        g = lax.rem(xm + o, nx)
        c = pltpu.make_async_remote_copy(
            src_ref=out_ref.at[xm, :, first], dst_ref=out_ref.at[xm, :, first],
            send_sem=send_sem.at[2, g], recv_sem=recv_sem.at[2, xm],
            device_id=(*row, red_x(g)), device_id_type=MESH,
        )
        c.start()
        sent.append(c)
    for o in range(1, nx):
        g = lax.rem(xm + o, nx)
        copy(src_ref.at[second], out_ref.at[g, ym, second], 1, g, red_x(g)).wait_recv()
    for o in range(1, ny):
        g = lax.rem(ym + o, ny)
        c = pltpu.make_async_remote_copy(
            src_ref=out_ref.at[:, ym, second], dst_ref=out_ref.at[:, ym, second],
            send_sem=send_sem.at[3, g], recv_sem=recv_sem.at[3, ym],
            device_id=(*row, red_y(g)), device_id_type=MESH,
        )
        c.start()
        sent.append(c)

    for c in sent:
        c.wait_send()
    for o in range(1, nx):
        g = lax.rem(xm + o, nx)
        copy(out_ref.at[g, :, first], out_ref.at[g, :, first], 2, g, red_x(g)).wait_recv()
    for o in range(1, ny):
        g = lax.rem(ym + o, ny)
        copy(out_ref.at[:, g, second], out_ref.at[:, g, second], 3, g, red_y(g)).wait_recv()


def _gather(block, n_red, collective_id):
    n_x = n_red // NY
    nbytes = block.size * block.dtype.itemsize
    return pl.pallas_call(
        functools.partial(_gather_kernel, n_red),
        out_shape=jax.ShapeDtypeStruct((n_x, NY) + block.shape, block.dtype),
        in_specs=[pl.BlockSpec(memory_space=pl.ANY)],
        out_specs=pl.BlockSpec(memory_space=pl.ANY),
        scratch_shapes=[
            pltpu.SemaphoreType.DMA((4, max(n_x, NY))),
            pltpu.SemaphoreType.DMA((4, max(n_x, NY))),
            pltpu.SemaphoreType.DMA((2,)),
        ],
        compiler_params=pltpu.CompilerParams(collective_id=collective_id, has_side_effects=True),
        cost_estimate=pl.CostEstimate(flops=0, bytes_accessed=2 * n_red * nbytes, transcendentals=0),
    )(block)


def _reduce_kernel(n_red, amp_ref, ints_ref, out_ref, ra, rb, pa, pb, sa, sb, qa, qb, send1, recv1, send2, recv2):
    row = _row()
    ym, ny, red_y = _group("y", n_red)
    xm, nx, red_x = _group("x", n_red)
    half = ra.shape[2]
    first, second = pl.ds(0, half), pl.ds(half, half)

    barrier = pltpu.get_barrier_semaphore()
    for o in range(1, ny):
        pl.semaphore_signal(barrier, inc=1, device_id=(*row, red_y(lax.rem(ym + o, ny))), device_id_type=MESH)
    for o in range(1, nx):
        pl.semaphore_signal(barrier, inc=1, device_id=(*row, red_x(lax.rem(xm + o, nx))), device_id_type=MESH)

    def copy(src, dst, send, recv, dev):
        return pltpu.make_async_remote_copy(
            src_ref=src, dst_ref=dst, send_sem=send, recv_sem=recv,
            device_id=(*row, dev), device_id_type=MESH,
        )

    width = ints_ref.shape[1]

    def block(lhs):
        slots = lhs.shape[0]
        flat = lhs.reshape(slots * half, lhs.shape[2])
        product = jnp.dot(flat, ints_ref[...], preferred_element_type=jnp.float32)
        return product.reshape(slots, half, width)

    pa[lax.rem(ym + 1, ny)] = block(amp_ref[:, lax.rem(ym + 1, ny), first])
    pb[lax.rem(xm + 1, nx)] = block(amp_ref[lax.rem(xm + 1, nx), :, second])
    pl.semaphore_wait(barrier, ny - 1 + nx - 1)
    sent = []
    for o in range(1, max(nx, ny)):
        if o < ny:
            g = lax.rem(ym + o, ny)
            if o > 1:
                pa[g] = block(amp_ref[:, g, first])
            c = copy(pa.at[g], ra.at[ym], send1.at[0, g], recv1.at[0, ym], red_y(g))
            c.start()
            sent.append(c)
        if o < nx:
            g = lax.rem(xm + o, nx)
            if o > 1:
                pb[g] = block(amp_ref[g, :, second])
            c = copy(pb.at[g], rb.at[xm], send1.at[1, g], recv1.at[1, xm], red_x(g))
            c.start()
            sent.append(c)
    ra[ym] = block(amp_ref[:, ym, first])
    rb[xm] = block(amp_ref[xm, :, second])

    for o in range(1, ny):
        g = lax.rem(ym + o, ny)
        copy(pa.at[g], ra.at[g], send1.at[0, g], recv1.at[0, g], red_y(g)).wait_recv()
    for o in range(1, nx):
        g = lax.rem(xm + o, nx)
        sa[g] = ra[0, g] + ra[1, g] + ra[2, g] + ra[3, g]
        c = copy(sa.at[g], qa.at[xm], send2.at[0, g], recv2.at[0, xm], red_x(g))
        c.start()
        sent.append(c)
    sa[xm] = ra[0, xm] + ra[1, xm] + ra[2, xm] + ra[3, xm]

    for o in range(1, nx):
        g = lax.rem(xm + o, nx)
        copy(pb.at[g], rb.at[g], send1.at[1, g], recv1.at[1, g], red_x(g)).wait_recv()
    for o in range(1, ny):
        g = lax.rem(ym + o, ny)
        sb[g] = rb[0, g] + rb[1, g] + rb[2, g] + rb[3, g]
        c = copy(sb.at[g], qb.at[ym], send2.at[1, g], recv2.at[1, ym], red_y(g))
        c.start()
        sent.append(c)
    sb[ym] = rb[0, ym] + rb[1, ym] + rb[2, ym] + rb[3, ym]

    for c in sent:
        c.wait_send()
    total_a = sa[xm]
    for o in range(1, nx):
        g = lax.rem(xm + o, nx)
        copy(sa.at[g], qa.at[g], send2.at[0, g], recv2.at[0, g], red_x(g)).wait_recv()
        total_a = total_a + qa[g]
    total_b = sb[ym]
    for o in range(1, ny):
        g = lax.rem(ym + o, ny)
        copy(sb.at[g], qb.at[g], send2.at[1, g], recv2.at[1, g], red_y(g)).wait_recv()
        total_b = total_b + qb[g]
    out_ref[first] = total_a
    out_ref[second] = total_b


def _reduce(amp, ints, n_red, collective_id):
    n_x, n_y, rows, _ = amp.shape
    cols = ints.shape[1]
    half = rows // 2
    f32 = jnp.float32
    return pl.pallas_call(
        functools.partial(_reduce_kernel, n_red),
        out_shape=jax.ShapeDtypeStruct((rows, cols), f32),
        in_specs=[pl.BlockSpec(memory_space=pltpu.VMEM)] * 2,
        out_specs=pl.BlockSpec(memory_space=pltpu.VMEM),
        scratch_shapes=[
            pltpu.VMEM((n_y, n_x, half, cols), f32),
            pltpu.VMEM((n_x, n_y, half, cols), f32),
            pltpu.VMEM((n_y, n_x, half, cols), f32),
            pltpu.VMEM((n_x, n_y, half, cols), f32),
            pltpu.VMEM((n_x, half, cols), f32),
            pltpu.VMEM((n_y, half, cols), f32),
            pltpu.VMEM((n_x, half, cols), f32),
            pltpu.VMEM((n_y, half, cols), f32),
            pltpu.SemaphoreType.DMA((2, max(n_x, n_y))),
            pltpu.SemaphoreType.DMA((2, max(n_x, n_y))),
            pltpu.SemaphoreType.DMA((2, max(n_x, n_y))),
            pltpu.SemaphoreType.DMA((2, max(n_x, n_y))),
        ],
        compiler_params=pltpu.CompilerParams(
            collective_id=collective_id, has_side_effects=True, vmem_limit_bytes=60 * 1024 * 1024
        ),
        cost_estimate=pl.CostEstimate(
            flops=2 * amp.size * cols, bytes_accessed=amp.size * 2 + ints.size * 2 + rows * cols * 4,
            transcendentals=0,
        ),
    )(amp, ints)


def _core_reduce_kernel(amp_ref, ints_ref, out_ref, mine_sent, theirs, send_sem, recv_sem):
    z, core = _row()
    red = lax.axis_index("red")
    other = CORES - 1 - core
    n_z, _, rows, _ = amp_ref.shape
    width = ints_ref.shape[1]
    step = n_z // 2
    barrier = pltpu.get_barrier_semaphore()
    pl.semaphore_signal(barrier, inc=1, device_id=(z, other, red), device_id_type=MESH)

    def block(k, which):
        lhs = amp_ref[pl.ds(k * step, step), which]
        product = jnp.dot(
            lhs.reshape(step * rows, lhs.shape[2]), ints_ref[...], preferred_element_type=jnp.float32
        )
        return product.reshape(step, rows, width)

    sends = []
    for k in range(2):
        mine_sent[pl.ds(k * step, step)] = block(k, other)
        if k == 0:
            pl.semaphore_wait(barrier, 1)
        c = pltpu.make_async_remote_copy(
            src_ref=mine_sent.at[pl.ds(k * step, step)], dst_ref=theirs.at[pl.ds(k * step, step)],
            send_sem=send_sem.at[k], recv_sem=recv_sem.at[k],
            device_id=(z, other, red), device_id_type=MESH,
        )
        c.start()
        sends.append(c)
    for k in range(2):
        out_ref[pl.ds(k * step, step)] = block(k, core)
    for k, c in enumerate(sends):
        c.wait()
        for i in range(k * step, (k + 1) * step):
            out_ref[i] = out_ref[i] + theirs[i]


def _core_reduce(amp, ints, collective_id):
    n_z, _, rows, _ = amp.shape
    cols = ints.shape[1]
    f32 = jnp.float32
    return pl.pallas_call(
        _core_reduce_kernel,
        out_shape=jax.ShapeDtypeStruct((n_z, rows, cols), f32),
        in_specs=[pl.BlockSpec(memory_space=pltpu.VMEM)] * 2,
        out_specs=pl.BlockSpec(memory_space=pltpu.VMEM),
        scratch_shapes=[
            pltpu.VMEM((n_z, rows, cols), f32),
            pltpu.VMEM((n_z, rows, cols), f32),
            pltpu.SemaphoreType.DMA((2,)),
            pltpu.SemaphoreType.DMA((2,)),
        ],
        compiler_params=pltpu.CompilerParams(
            collective_id=collective_id, has_side_effects=True, vmem_limit_bytes=60 * 1024 * 1024
        ),
        cost_estimate=pl.CostEstimate(
            flops=2 * amp.size * cols, bytes_accessed=amp.size * 2 + ints.size * 2 + n_z * rows * cols * 4,
            transcendentals=0,
        ),
    )(amp, ints)


def shards(amplitudes, ladder_ints, cycle_ints, occ_energy, vir_energy, slab_index):
    slab_rows, occ_local, vir_local, virt_width = amplitudes.shape
    n_red = lax.axis_size("red")
    n_blk = lax.axis_size("z") * lax.axis_size("core")
    occ_all = occ_local * n_blk
    occ_red = occ_all // n_red
    n_x = n_red // NY

    swapped = jnp.transpose(amplitudes, (0, 2, 1, 3)).reshape(
        slab_rows * vir_local, occ_local * virt_width
    )
    gathered = _gather(swapped, n_red, 0)
    operand = gathered.reshape(n_blk // CORES, CORES, slab_rows * vir_local, occ_local * virt_width)
    product = _core_reduce(operand, cycle_ints, 4)
    cycle_own = lax.psum_scatter(product, "z", scatter_dimension=0, tiled=True)[0]
    cycle_own = jnp.transpose(
        cycle_own.reshape(slab_rows, vir_local, occ_red, virt_width), (0, 2, 1, 3)
    )

    rows = slab_rows * occ_local
    flat = amplitudes.reshape(rows, vir_local * virt_width)
    shard_piece = lax.all_gather(flat, ("z", "core"), axis=0, tiled=False)
    ladder_own = _reduce(shard_piece.reshape(n_x, NY, rows, -1), ladder_ints, n_red, 1)
    ladder_own = ladder_own.reshape(slab_rows, occ_red, -1, virt_width)

    vir_block = cycle_own.shape[2]
    orbital_ids = jnp.arange(occ_energy.shape[0], dtype=jnp.int32)
    chosen = slab_index[:, None] == orbital_ids[None, :]
    slab_energy = jnp.sum(jnp.where(chosen, occ_energy[None, :], jnp.float32(0.0)), axis=1)
    pair_energy = lax.dynamic_slice_in_dim(occ_energy, lax.axis_index("red") * occ_red, occ_red)
    first_virtual = lax.dynamic_slice_in_dim(
        vir_energy, (lax.axis_index("z") * CORES + lax.axis_index("core")) * vir_block, vir_block
    )
    denominator = (
        first_virtual[None, None, :, None]
        + vir_energy[None, None, None, :]
        - slab_energy[:, None, None, None]
        - pair_energy[None, :, None, None]
    )
    return (ladder_own + cycle_own) / denominator


def solution(mesh):
    blk = ("z", "core")
    split = Mesh(
        mesh.devices.reshape(mesh.shape["blk"] // CORES, CORES, mesh.shape["red"]),
        ("z", "core", "red"),
    )
    placed = (P(None, blk, "red", None), P("red", blk), P(blk, "red"), P(), P(), P())
    return jax.shard_map(
        shards, mesh=split, in_specs=placed, out_specs=P(None, "red", blk, None), check_vma=False
    )
```

```python
import functools

import jax
import jax.numpy as jnp
from jax import lax
from jax.experimental import pallas as pl
from jax.experimental.pallas import tpu as pltpu
from jax.sharding import Mesh, PartitionSpec as P

MESH = pl.DeviceIdType.MESH


NY = 4
CORES = 2
LANES = 128


def _row():
    return lax.axis_index("z"), lax.axis_index("core")


def _group(kind, n_red):
    r = lax.axis_index("red")
    x, y = r // NY, lax.rem(r, NY)
    if kind == "y":
        return y, NY, lambda pos: x * NY + pos
    if kind == "x":
        return x, n_red // NY, lambda pos: pos * NY + y
    return r, n_red, lambda pos: pos


def _gather_kernel(n_red, src_ref, out_ref, send_sem, recv_sem, local_sem):
    row = _row()
    ym, ny, red_y = _group("y", n_red)
    xm, nx, red_x = _group("x", n_red)
    part = src_ref.shape[0] // 2
    first, second = pl.ds(0, part), pl.ds(part, part)

    barrier = pltpu.get_barrier_semaphore()
    for o in range(1, ny):
        pl.semaphore_signal(barrier, inc=1, device_id=(*row, red_y(lax.rem(ym + o, ny))), device_id_type=MESH)
    for o in range(1, nx):
        pl.semaphore_signal(barrier, inc=1, device_id=(*row, red_x(lax.rem(xm + o, nx))), device_id_type=MESH)
    pl.semaphore_wait(barrier, ny - 1 + nx - 1)

    def copy(src, dst, stage, pos, dev):
        return pltpu.make_async_remote_copy(
            src_ref=src,
            dst_ref=dst,
            send_sem=send_sem.at[stage, pos],
            recv_sem=recv_sem.at[stage, pos],
            device_id=(*row, dev),
            device_id_type=MESH,
        )

    sent = []
    for o in range(1, ny):
        g = lax.rem(ym + o, ny)
        c = pltpu.make_async_remote_copy(
            src_ref=src_ref.at[first], dst_ref=out_ref.at[xm, ym, first],
            send_sem=send_sem.at[0, g], recv_sem=recv_sem.at[0, ym],
            device_id=(*row, red_y(g)), device_id_type=MESH,
        )
        c.start()
        sent.append(c)
    for o in range(1, nx):
        g = lax.rem(xm + o, nx)
        c = pltpu.make_async_remote_copy(
            src_ref=src_ref.at[second], dst_ref=out_ref.at[xm, ym, second],
            send_sem=send_sem.at[1, g], recv_sem=recv_sem.at[1, xm],
            device_id=(*row, red_x(g)), device_id_type=MESH,
        )
        c.start()
        sent.append(c)
    own = [
        pltpu.make_async_copy(src_ref.at[first], out_ref.at[xm, ym, first], local_sem.at[0]),
        pltpu.make_async_copy(src_ref.at[second], out_ref.at[xm, ym, second], local_sem.at[1]),
    ]
    for c in own:
        c.start()
    for c in own:
        c.wait()

    for o in range(1, ny):
        g = lax.rem(ym + o, ny)
        copy(src_ref.at[first], out_ref.at[xm, g, first], 0, g, red_y(g)).wait_recv()
    for o in range(1, nx):
        g = lax.rem(xm + o, nx)
        c = pltpu.make_async_remote_copy(
            src_ref=out_ref.at[xm, :, first], dst_ref=out_ref.at[xm, :, first],
            send_sem=send_sem.at[2, g], recv_sem=recv_sem.at[2, xm],
            device_id=(*row, red_x(g)), device_id_type=MESH,
        )
        c.start()
        sent.append(c)
    for o in range(1, nx):
        g = lax.rem(xm + o, nx)
        copy(src_ref.at[second], out_ref.at[g, ym, second], 1, g, red_x(g)).wait_recv()
    for o in range(1, ny):
        g = lax.rem(ym + o, ny)
        c = pltpu.make_async_remote_copy(
            src_ref=out_ref.at[:, ym, second], dst_ref=out_ref.at[:, ym, second],
            send_sem=send_sem.at[3, g], recv_sem=recv_sem.at[3, ym],
            device_id=(*row, red_y(g)), device_id_type=MESH,
        )
        c.start()
        sent.append(c)

    for c in sent:
        c.wait_send()
    for o in range(1, nx):
        g = lax.rem(xm + o, nx)
        copy(out_ref.at[g, :, first], out_ref.at[g, :, first], 2, g, red_x(g)).wait_recv()
    for o in range(1, ny):
        g = lax.rem(ym + o, ny)
        copy(out_ref.at[:, g, second], out_ref.at[:, g, second], 3, g, red_y(g)).wait_recv()


def _gather(block, n_red, collective_id):
    n_x = n_red // NY
    nbytes = block.size * block.dtype.itemsize
    return pl.pallas_call(
        functools.partial(_gather_kernel, n_red),
        out_shape=jax.ShapeDtypeStruct((n_x, NY) + block.shape, block.dtype),
        in_specs=[pl.BlockSpec(memory_space=pl.ANY)],
        out_specs=pl.BlockSpec(memory_space=pl.ANY),
        scratch_shapes=[
            pltpu.SemaphoreType.DMA((4, max(n_x, NY))),
            pltpu.SemaphoreType.DMA((4, max(n_x, NY))),
            pltpu.SemaphoreType.DMA((2,)),
        ],
        compiler_params=pltpu.CompilerParams(collective_id=collective_id, has_side_effects=True),
        cost_estimate=pl.CostEstimate(flops=0, bytes_accessed=2 * n_red * nbytes, transcendentals=0),
    )(block)


def _reduce_kernel(n_red, amp_ref, ints_ref, out_ref, ra, rb, pa, pb, sa, sb, qa, qb, send1, recv1, send2, recv2):
    row = _row()
    ym, ny, red_y = _group("y", n_red)
    xm, nx, red_x = _group("x", n_red)
    half = ra.shape[2]
    first, second = pl.ds(0, half), pl.ds(half, half)

    barrier = pltpu.get_barrier_semaphore()
    for o in range(1, ny):
        pl.semaphore_signal(barrier, inc=1, device_id=(*row, red_y(lax.rem(ym + o, ny))), device_id_type=MESH)
    for o in range(1, nx):
        pl.semaphore_signal(barrier, inc=1, device_id=(*row, red_x(lax.rem(xm + o, nx))), device_id_type=MESH)

    def copy(src, dst, send, recv, dev):
        return pltpu.make_async_remote_copy(
            src_ref=src, dst_ref=dst, send_sem=send, recv_sem=recv,
            device_id=(*row, dev), device_id_type=MESH,
        )

    width = ints_ref.shape[1]

    def block(lhs):
        slots = lhs.shape[0]
        flat = lhs.reshape(slots * half, lhs.shape[2])
        product = jnp.dot(flat, ints_ref[...], preferred_element_type=jnp.float32)
        return product.reshape(slots, half, width)

    pa[lax.rem(ym + 1, ny)] = block(amp_ref[:, lax.rem(ym + 1, ny), first])
    pb[lax.rem(xm + 1, nx)] = block(amp_ref[lax.rem(xm + 1, nx), :, second])
    pl.semaphore_wait(barrier, ny - 1 + nx - 1)
    sent = []
    for o in range(1, max(nx, ny)):
        if o < ny:
            g = lax.rem(ym + o, ny)
            if o > 1:
                pa[g] = block(amp_ref[:, g, first])
            c = copy(pa.at[g], ra.at[ym], send1.at[0, g], recv1.at[0, ym], red_y(g))
            c.start()
            sent.append(c)
        if o < nx:
            g = lax.rem(xm + o, nx)
            if o > 1:
                pb[g] = block(amp_ref[g, :, second])
            c = copy(pb.at[g], rb.at[xm], send1.at[1, g], recv1.at[1, xm], red_x(g))
            c.start()
            sent.append(c)
    ra[ym] = block(amp_ref[:, ym, first])
    rb[xm] = block(amp_ref[xm, :, second])

    for o in range(1, ny):
        g = lax.rem(ym + o, ny)
        copy(pa.at[g], ra.at[g], send1.at[0, g], recv1.at[0, g], red_y(g)).wait_recv()
    for o in range(1, nx):
        g = lax.rem(xm + o, nx)
        sa[g] = ra[0, g] + ra[1, g] + ra[2, g] + ra[3, g]
        c = copy(sa.at[g], qa.at[xm], send2.at[0, g], recv2.at[0, xm], red_x(g))
        c.start()
        sent.append(c)
    sa[xm] = ra[0, xm] + ra[1, xm] + ra[2, xm] + ra[3, xm]

    for o in range(1, nx):
        g = lax.rem(xm + o, nx)
        copy(pb.at[g], rb.at[g], send1.at[1, g], recv1.at[1, g], red_x(g)).wait_recv()
    for o in range(1, ny):
        g = lax.rem(ym + o, ny)
        sb[g] = rb[0, g] + rb[1, g] + rb[2, g] + rb[3, g]
        c = copy(sb.at[g], qb.at[ym], send2.at[1, g], recv2.at[1, ym], red_y(g))
        c.start()
        sent.append(c)
    sb[ym] = rb[0, ym] + rb[1, ym] + rb[2, ym] + rb[3, ym]

    for c in sent:
        c.wait_send()
    total_a = sa[xm]
    for o in range(1, nx):
        g = lax.rem(xm + o, nx)
        copy(sa.at[g], qa.at[g], send2.at[0, g], recv2.at[0, g], red_x(g)).wait_recv()
        total_a = total_a + qa[g]
    total_b = sb[ym]
    for o in range(1, ny):
        g = lax.rem(ym + o, ny)
        copy(sb.at[g], qb.at[g], send2.at[1, g], recv2.at[1, g], red_y(g)).wait_recv()
        total_b = total_b + qb[g]
    lanes = out_ref.shape[2]
    out_ref[first] = total_a.reshape(half, width // lanes, lanes)
    out_ref[second] = total_b.reshape(half, width // lanes, lanes)


def _reduce(amp, ints, n_red, collective_id):
    n_x, n_y, rows, _ = amp.shape
    cols = ints.shape[1]
    half = rows // 2
    f32 = jnp.float32
    return pl.pallas_call(
        functools.partial(_reduce_kernel, n_red),
        out_shape=jax.ShapeDtypeStruct((rows, cols // LANES, LANES), f32),
        in_specs=[pl.BlockSpec(memory_space=pltpu.VMEM)] * 2,
        out_specs=pl.BlockSpec(memory_space=pltpu.VMEM),
        scratch_shapes=[
            pltpu.VMEM((n_y, n_x, half, cols), f32),
            pltpu.VMEM((n_x, n_y, half, cols), f32),
            pltpu.VMEM((n_y, n_x, half, cols), f32),
            pltpu.VMEM((n_x, n_y, half, cols), f32),
            pltpu.VMEM((n_x, half, cols), f32),
            pltpu.VMEM((n_y, half, cols), f32),
            pltpu.VMEM((n_x, half, cols), f32),
            pltpu.VMEM((n_y, half, cols), f32),
            pltpu.SemaphoreType.DMA((2, max(n_x, n_y))),
            pltpu.SemaphoreType.DMA((2, max(n_x, n_y))),
            pltpu.SemaphoreType.DMA((2, max(n_x, n_y))),
            pltpu.SemaphoreType.DMA((2, max(n_x, n_y))),
        ],
        compiler_params=pltpu.CompilerParams(
            collective_id=collective_id, has_side_effects=True, vmem_limit_bytes=60 * 1024 * 1024
        ),
        cost_estimate=pl.CostEstimate(
            flops=2 * amp.size * cols, bytes_accessed=amp.size * 2 + ints.size * 2 + rows * cols * 4,
            transcendentals=0,
        ),
    )(amp, ints)


def _core_reduce_kernel(amp_ref, ints_ref, out_ref, mine_sent, theirs, send_sem, recv_sem):
    z, core = _row()
    red = lax.axis_index("red")
    other = CORES - 1 - core
    n_z, _, rows, _ = amp_ref.shape
    width = ints_ref.shape[1]
    step = n_z // 2
    barrier = pltpu.get_barrier_semaphore()
    pl.semaphore_signal(barrier, inc=1, device_id=(z, other, red), device_id_type=MESH)

    def block(k, which):
        lhs = amp_ref[pl.ds(k * step, step), which]
        product = jnp.dot(
            lhs.reshape(step * rows, lhs.shape[2]), ints_ref[...], preferred_element_type=jnp.float32
        )
        return product.reshape(step, rows, width)

    sends = []
    for k in range(2):
        mine_sent[pl.ds(k * step, step)] = block(k, other)
        if k == 0:
            pl.semaphore_wait(barrier, 1)
        c = pltpu.make_async_remote_copy(
            src_ref=mine_sent.at[pl.ds(k * step, step)], dst_ref=theirs.at[pl.ds(k * step, step)],
            send_sem=send_sem.at[k], recv_sem=recv_sem.at[k],
            device_id=(z, other, red), device_id_type=MESH,
        )
        c.start()
        sends.append(c)
    for k in range(2):
        out_ref[pl.ds(k * step, step)] = block(k, core)
    for k, c in enumerate(sends):
        c.wait()
        for i in range(k * step, (k + 1) * step):
            out_ref[i] = out_ref[i] + theirs[i]


def _core_reduce(amp, ints, collective_id):
    n_z, _, rows, _ = amp.shape
    cols = ints.shape[1]
    f32 = jnp.float32
    return pl.pallas_call(
        _core_reduce_kernel,
        out_shape=jax.ShapeDtypeStruct((n_z, rows, cols), f32),
        in_specs=[pl.BlockSpec(memory_space=pltpu.VMEM)] * 2,
        out_specs=pl.BlockSpec(memory_space=pltpu.VMEM),
        scratch_shapes=[
            pltpu.VMEM((n_z, rows, cols), f32),
            pltpu.VMEM((n_z, rows, cols), f32),
            pltpu.SemaphoreType.DMA((2,)),
            pltpu.SemaphoreType.DMA((2,)),
        ],
        compiler_params=pltpu.CompilerParams(
            collective_id=collective_id, has_side_effects=True, vmem_limit_bytes=60 * 1024 * 1024
        ),
        cost_estimate=pl.CostEstimate(
            flops=2 * amp.size * cols, bytes_accessed=amp.size * 2 + ints.size * 2 + n_z * rows * cols * 4,
            transcendentals=0,
        ),
    )(amp, ints)


def shards(amplitudes, ladder_ints, cycle_ints, occ_energy, vir_energy, slab_index):
    slab_rows, occ_local, vir_local, virt_width = amplitudes.shape
    n_red = lax.axis_size("red")
    n_blk = lax.axis_size("z") * lax.axis_size("core")
    occ_all = occ_local * n_blk
    occ_red = occ_all // n_red
    n_x = n_red // NY

    swapped = jnp.transpose(amplitudes, (0, 2, 1, 3)).reshape(
        slab_rows * vir_local, occ_local * virt_width
    )
    gathered = _gather(swapped, n_red, 0)
    operand = gathered.reshape(n_blk // CORES, CORES, slab_rows * vir_local, occ_local * virt_width)
    product = _core_reduce(operand, cycle_ints, 4)
    cycle_own = lax.psum_scatter(product, "z", scatter_dimension=0, tiled=True)[0]
    cycle_own = jnp.transpose(
        cycle_own.reshape(slab_rows, vir_local, occ_red, virt_width), (0, 2, 1, 3)
    )

    rows = slab_rows * occ_local
    flat = amplitudes.reshape(rows, vir_local * virt_width)
    shard_piece = lax.all_gather(flat, ("z", "core"), axis=0, tiled=False)
    ladder_own = _reduce(shard_piece.reshape(n_x, NY, rows, -1), ladder_ints, n_red, 1)
    ladder_own = ladder_own.reshape(slab_rows, occ_red, -1, virt_width)

    vir_block = cycle_own.shape[2]
    orbital_ids = jnp.arange(occ_energy.shape[0], dtype=jnp.int32)
    chosen = slab_index[:, None] == orbital_ids[None, :]
    slab_energy = jnp.sum(jnp.where(chosen, occ_energy[None, :], jnp.float32(0.0)), axis=1)
    pair_energy = lax.dynamic_slice_in_dim(occ_energy, lax.axis_index("red") * occ_red, occ_red)
    first_virtual = lax.dynamic_slice_in_dim(
        vir_energy, (lax.axis_index("z") * CORES + lax.axis_index("core")) * vir_block, vir_block
    )
    denominator = (
        first_virtual[None, None, :, None]
        + vir_energy[None, None, None, :]
        - slab_energy[:, None, None, None]
        - pair_energy[None, :, None, None]
    )
    return (ladder_own + cycle_own) / denominator


def solution(mesh):
    blk = ("z", "core")
    split = Mesh(
        mesh.devices.reshape(mesh.shape["blk"] // CORES, CORES, mesh.shape["red"]),
        ("z", "core", "red"),
    )
    placed = (P(None, blk, "red", None), P("red", blk), P(blk, "red"), P(), P(), P())
    return jax.shard_map(
        shards, mesh=split, in_specs=placed, out_specs=P(None, "red", blk, None), check_vma=False
    )
```

```python
import functools

import jax
import jax.numpy as jnp
from jax import lax
from jax.experimental import pallas as pl
from jax.experimental.pallas import tpu as pltpu
from jax.sharding import Mesh, PartitionSpec as P

MESH = pl.DeviceIdType.MESH


NY = 4
CORES = 2
LANES = 128


def _row():
    return lax.axis_index("z"), lax.axis_index("core")


def _group(kind, n_red):
    r = lax.axis_index("red")
    x, y = r // NY, lax.rem(r, NY)
    if kind == "y":
        return y, NY, lambda pos: x * NY + pos
    if kind == "x":
        return x, n_red // NY, lambda pos: pos * NY + y
    return r, n_red, lambda pos: pos


def _gather_kernel(n_red, src_ref, out_ref, send_sem, recv_sem, local_sem):
    row = _row()
    ym, ny, red_y = _group("y", n_red)
    xm, nx, red_x = _group("x", n_red)
    part = src_ref.shape[0] // 2
    first, second = pl.ds(0, part), pl.ds(part, part)

    barrier = pltpu.get_barrier_semaphore()
    for o in range(1, ny):
        pl.semaphore_signal(barrier, inc=1, device_id=(*row, red_y(lax.rem(ym + o, ny))), device_id_type=MESH)
    for o in range(1, nx):
        pl.semaphore_signal(barrier, inc=1, device_id=(*row, red_x(lax.rem(xm + o, nx))), device_id_type=MESH)
    pl.semaphore_wait(barrier, ny - 1 + nx - 1)

    def copy(src, dst, stage, pos, dev):
        return pltpu.make_async_remote_copy(
            src_ref=src,
            dst_ref=dst,
            send_sem=send_sem.at[stage, pos],
            recv_sem=recv_sem.at[stage, pos],
            device_id=(*row, dev),
            device_id_type=MESH,
        )

    sent = []
    for o in range(1, ny):
        g = lax.rem(ym + o, ny)
        c = pltpu.make_async_remote_copy(
            src_ref=src_ref.at[first], dst_ref=out_ref.at[xm, ym, first],
            send_sem=send_sem.at[0, g], recv_sem=recv_sem.at[0, ym],
            device_id=(*row, red_y(g)), device_id_type=MESH,
        )
        c.start()
        sent.append(c)
    for o in range(1, nx):
        g = lax.rem(xm + o, nx)
        c = pltpu.make_async_remote_copy(
            src_ref=src_ref.at[second], dst_ref=out_ref.at[xm, ym, second],
            send_sem=send_sem.at[1, g], recv_sem=recv_sem.at[1, xm],
            device_id=(*row, red_x(g)), device_id_type=MESH,
        )
        c.start()
        sent.append(c)
    own = [
        pltpu.make_async_copy(src_ref.at[first], out_ref.at[xm, ym, first], local_sem.at[0]),
        pltpu.make_async_copy(src_ref.at[second], out_ref.at[xm, ym, second], local_sem.at[1]),
    ]
    for c in own:
        c.start()
    for c in own:
        c.wait()

    for o in range(1, ny):
        g = lax.rem(ym + o, ny)
        copy(src_ref.at[first], out_ref.at[xm, g, first], 0, g, red_y(g)).wait_recv()
    for o in range(1, nx):
        g = lax.rem(xm + o, nx)
        c = pltpu.make_async_remote_copy(
            src_ref=out_ref.at[xm, :, first], dst_ref=out_ref.at[xm, :, first],
            send_sem=send_sem.at[2, g], recv_sem=recv_sem.at[2, xm],
            device_id=(*row, red_x(g)), device_id_type=MESH,
        )
        c.start()
        sent.append(c)
    for o in range(1, nx):
        g = lax.rem(xm + o, nx)
        copy(src_ref.at[second], out_ref.at[g, ym, second], 1, g, red_x(g)).wait_recv()
    for o in range(1, ny):
        g = lax.rem(ym + o, ny)
        c = pltpu.make_async_remote_copy(
            src_ref=out_ref.at[:, ym, second], dst_ref=out_ref.at[:, ym, second],
            send_sem=send_sem.at[3, g], recv_sem=recv_sem.at[3, ym],
            device_id=(*row, red_y(g)), device_id_type=MESH,
        )
        c.start()
        sent.append(c)

    for c in sent:
        c.wait_send()
    for o in range(1, nx):
        g = lax.rem(xm + o, nx)
        copy(out_ref.at[g, :, first], out_ref.at[g, :, first], 2, g, red_x(g)).wait_recv()
    for o in range(1, ny):
        g = lax.rem(ym + o, ny)
        copy(out_ref.at[:, g, second], out_ref.at[:, g, second], 3, g, red_y(g)).wait_recv()


def _gather(block, n_red, collective_id):
    n_x = n_red // NY
    nbytes = block.size * block.dtype.itemsize
    return pl.pallas_call(
        functools.partial(_gather_kernel, n_red),
        out_shape=jax.ShapeDtypeStruct((n_x, NY) + block.shape, block.dtype),
        in_specs=[pl.BlockSpec(memory_space=pl.ANY)],
        out_specs=pl.BlockSpec(memory_space=pl.ANY),
        scratch_shapes=[
            pltpu.SemaphoreType.DMA((4, max(n_x, NY))),
            pltpu.SemaphoreType.DMA((4, max(n_x, NY))),
            pltpu.SemaphoreType.DMA((2,)),
        ],
        compiler_params=pltpu.CompilerParams(collective_id=collective_id, has_side_effects=True),
        cost_estimate=pl.CostEstimate(flops=0, bytes_accessed=2 * n_red * nbytes, transcendentals=0),
    )(block)


def _reduce_kernel(n_red, amp_ref, ints_ref, out_ref, ra, rb, pa, pb, sa, sb, qa, qb, send1, recv1, send2, recv2):
    row = _row()
    ym, ny, red_y = _group("y", n_red)
    xm, nx, red_x = _group("x", n_red)
    half = ra.shape[2]
    first, second = pl.ds(0, half), pl.ds(half, half)

    barrier = pltpu.get_barrier_semaphore()
    for o in range(1, ny):
        pl.semaphore_signal(barrier, inc=1, device_id=(*row, red_y(lax.rem(ym + o, ny))), device_id_type=MESH)
    for o in range(1, nx):
        pl.semaphore_signal(barrier, inc=1, device_id=(*row, red_x(lax.rem(xm + o, nx))), device_id_type=MESH)

    def copy(src, dst, send, recv, dev):
        return pltpu.make_async_remote_copy(
            src_ref=src, dst_ref=dst, send_sem=send, recv_sem=recv,
            device_id=(*row, dev), device_id_type=MESH,
        )

    width = ints_ref.shape[1]

    def block(lhs):
        slots = lhs.shape[0]
        flat = lhs.reshape(slots * half, lhs.shape[2])
        product = jnp.dot(flat, ints_ref[...], preferred_element_type=jnp.float32)
        return product.reshape(slots, half, width)

    pa[lax.rem(ym + 1, ny)] = block(amp_ref[:, lax.rem(ym + 1, ny), first])
    pb[lax.rem(xm + 1, nx)] = block(amp_ref[lax.rem(xm + 1, nx), :, second])
    pl.semaphore_wait(barrier, ny - 1 + nx - 1)
    sent = []
    for o in range(1, max(nx, ny)):
        if o < ny:
            g = lax.rem(ym + o, ny)
            if o > 1:
                pa[g] = block(amp_ref[:, g, first])
            c = copy(pa.at[g], ra.at[ym], send1.at[0, g], recv1.at[0, ym], red_y(g))
            c.start()
            sent.append(c)
        if o < nx:
            g = lax.rem(xm + o, nx)
            if o > 1:
                pb[g] = block(amp_ref[g, :, second])
            c = copy(pb.at[g], rb.at[xm], send1.at[1, g], recv1.at[1, xm], red_x(g))
            c.start()
            sent.append(c)
    ra[ym] = block(amp_ref[:, ym, first])
    rb[xm] = block(amp_ref[xm, :, second])

    for o in range(1, ny):
        g = lax.rem(ym + o, ny)
        copy(pa.at[g], ra.at[g], send1.at[0, g], recv1.at[0, g], red_y(g)).wait_recv()
    for o in range(1, nx):
        g = lax.rem(xm + o, nx)
        sa[g] = ra[0, g] + ra[1, g] + ra[2, g] + ra[3, g]
        c = copy(sa.at[g], qa.at[xm], send2.at[0, g], recv2.at[0, xm], red_x(g))
        c.start()
        sent.append(c)
    sa[xm] = ra[0, xm] + ra[1, xm] + ra[2, xm] + ra[3, xm]

    for o in range(1, nx):
        g = lax.rem(xm + o, nx)
        copy(pb.at[g], rb.at[g], send1.at[1, g], recv1.at[1, g], red_x(g)).wait_recv()
    for o in range(1, ny):
        g = lax.rem(ym + o, ny)
        sb[g] = rb[0, g] + rb[1, g] + rb[2, g] + rb[3, g]
        c = copy(sb.at[g], qb.at[ym], send2.at[1, g], recv2.at[1, ym], red_y(g))
        c.start()
        sent.append(c)
    sb[ym] = rb[0, ym] + rb[1, ym] + rb[2, ym] + rb[3, ym]

    for c in sent:
        c.wait_send()
    total_a = sa[xm]
    for o in range(1, nx):
        g = lax.rem(xm + o, nx)
        copy(sa.at[g], qa.at[g], send2.at[0, g], recv2.at[0, g], red_x(g)).wait_recv()
        total_a = total_a + qa[g]
    total_b = sb[ym]
    for o in range(1, ny):
        g = lax.rem(ym + o, ny)
        copy(sb.at[g], qb.at[g], send2.at[1, g], recv2.at[1, g], red_y(g)).wait_recv()
        total_b = total_b + qb[g]
    lanes = out_ref.shape[2]
    out_ref[first] = total_a.reshape(half, width // lanes, lanes)
    out_ref[second] = total_b.reshape(half, width // lanes, lanes)


def _reduce(amp, ints, n_red, collective_id):
    n_x, n_y, rows, _ = amp.shape
    cols = ints.shape[1]
    half = rows // 2
    f32 = jnp.float32
    return pl.pallas_call(
        functools.partial(_reduce_kernel, n_red),
        out_shape=jax.ShapeDtypeStruct((rows, cols // LANES, LANES), f32),
        in_specs=[pl.BlockSpec(memory_space=pltpu.VMEM)] * 2,
        out_specs=pl.BlockSpec(memory_space=pltpu.VMEM),
        scratch_shapes=[
            pltpu.VMEM((n_y, n_x, half, cols), f32),
            pltpu.VMEM((n_x, n_y, half, cols), f32),
            pltpu.VMEM((n_y, n_x, half, cols), f32),
            pltpu.VMEM((n_x, n_y, half, cols), f32),
            pltpu.VMEM((n_x, half, cols), f32),
            pltpu.VMEM((n_y, half, cols), f32),
            pltpu.VMEM((n_x, half, cols), f32),
            pltpu.VMEM((n_y, half, cols), f32),
            pltpu.SemaphoreType.DMA((2, max(n_x, n_y))),
            pltpu.SemaphoreType.DMA((2, max(n_x, n_y))),
            pltpu.SemaphoreType.DMA((2, max(n_x, n_y))),
            pltpu.SemaphoreType.DMA((2, max(n_x, n_y))),
        ],
        compiler_params=pltpu.CompilerParams(
            collective_id=collective_id, has_side_effects=True, vmem_limit_bytes=60 * 1024 * 1024
        ),
        cost_estimate=pl.CostEstimate(
            flops=2 * amp.size * cols, bytes_accessed=amp.size * 2 + ints.size * 2 + rows * cols * 4,
            transcendentals=0,
        ),
    )(amp, ints)


def _core_reduce_kernel(amp_ref, ints_ref, out_ref, mine_sent, theirs, send_sem, recv_sem):
    z, core = _row()
    red = lax.axis_index("red")
    other = CORES - 1 - core
    n_z, _, rows, _ = amp_ref.shape
    width = ints_ref.shape[1]
    step = n_z // 2
    barrier = pltpu.get_barrier_semaphore()
    pl.semaphore_signal(barrier, inc=1, device_id=(z, other, red), device_id_type=MESH)

    def block(k, which):
        lhs = amp_ref[pl.ds(k * step, step), which]
        product = jnp.dot(
            lhs.reshape(step * rows, lhs.shape[2]), ints_ref[...], preferred_element_type=jnp.float32
        )
        return product.reshape(step, rows, width)

    sends = []
    for k in range(2):
        mine_sent[pl.ds(k * step, step)] = block(k, other)
        if k == 0:
            pl.semaphore_wait(barrier, 1)
        c = pltpu.make_async_remote_copy(
            src_ref=mine_sent.at[pl.ds(k * step, step)], dst_ref=theirs.at[pl.ds(k * step, step)],
            send_sem=send_sem.at[k], recv_sem=recv_sem.at[k],
            device_id=(z, other, red), device_id_type=MESH,
        )
        c.start()
        sends.append(c)
    for k, c in enumerate(sends):
        c.wait()
        out_ref[pl.ds(k * step, step)] = block(k, core) + theirs[pl.ds(k * step, step)]


def _core_reduce(amp, ints, collective_id):
    n_z, _, rows, _ = amp.shape
    cols = ints.shape[1]
    f32 = jnp.float32
    return pl.pallas_call(
        _core_reduce_kernel,
        out_shape=jax.ShapeDtypeStruct((n_z, rows, cols), f32),
        in_specs=[pl.BlockSpec(memory_space=pltpu.VMEM)] * 2,
        out_specs=pl.BlockSpec(memory_space=pltpu.VMEM),
        scratch_shapes=[
            pltpu.VMEM((n_z, rows, cols), f32),
            pltpu.VMEM((n_z, rows, cols), f32),
            pltpu.SemaphoreType.DMA((2,)),
            pltpu.SemaphoreType.DMA((2,)),
        ],
        compiler_params=pltpu.CompilerParams(
            collective_id=collective_id, has_side_effects=True, vmem_limit_bytes=60 * 1024 * 1024
        ),
        cost_estimate=pl.CostEstimate(
            flops=2 * amp.size * cols, bytes_accessed=amp.size * 2 + ints.size * 2 + n_z * rows * cols * 4,
            transcendentals=0,
        ),
    )(amp, ints)


def shards(amplitudes, ladder_ints, cycle_ints, occ_energy, vir_energy, slab_index):
    slab_rows, occ_local, vir_local, virt_width = amplitudes.shape
    n_red = lax.axis_size("red")
    n_blk = lax.axis_size("z") * lax.axis_size("core")
    occ_all = occ_local * n_blk
    occ_red = occ_all // n_red
    n_x = n_red // NY

    swapped = jnp.transpose(amplitudes, (0, 2, 1, 3)).reshape(
        slab_rows * vir_local, occ_local * virt_width
    )
    gathered = _gather(swapped, n_red, 0)
    operand = gathered.reshape(n_blk // CORES, CORES, slab_rows * vir_local, occ_local * virt_width)
    product = _core_reduce(operand, cycle_ints, 4)
    cycle_own = lax.psum_scatter(product, "z", scatter_dimension=0, tiled=True)[0]
    cycle_own = jnp.transpose(
        cycle_own.reshape(slab_rows, vir_local, occ_red, virt_width), (0, 2, 1, 3)
    )

    rows = slab_rows * occ_local
    flat = amplitudes.reshape(rows, vir_local * virt_width)
    shard_piece = lax.all_gather(flat, ("z", "core"), axis=0, tiled=False)
    ladder_own = _reduce(shard_piece.reshape(n_x, NY, rows, -1), ladder_ints, n_red, 1)
    ladder_own = ladder_own.reshape(slab_rows, occ_red, -1, virt_width)

    vir_block = cycle_own.shape[2]
    orbital_ids = jnp.arange(occ_energy.shape[0], dtype=jnp.int32)
    chosen = slab_index[:, None] == orbital_ids[None, :]
    slab_energy = jnp.sum(jnp.where(chosen, occ_energy[None, :], jnp.float32(0.0)), axis=1)
    pair_energy = lax.dynamic_slice_in_dim(occ_energy, lax.axis_index("red") * occ_red, occ_red)
    first_virtual = lax.dynamic_slice_in_dim(
        vir_energy, (lax.axis_index("z") * CORES + lax.axis_index("core")) * vir_block, vir_block
    )
    denominator = (
        first_virtual[None, None, :, None]
        + vir_energy[None, None, None, :]
        - slab_energy[:, None, None, None]
        - pair_energy[None, :, None, None]
    )
    return (ladder_own + cycle_own) / denominator


def solution(mesh):
    blk = ("z", "core")
    split = Mesh(
        mesh.devices.reshape(mesh.shape["blk"] // CORES, CORES, mesh.shape["red"]),
        ("z", "core", "red"),
    )
    placed = (P(None, blk, "red", None), P("red", blk), P(blk, "red"), P(), P(), P())
    return jax.shard_map(
        shards, mesh=split, in_specs=placed, out_specs=P(None, "red", blk, None), check_vma=False
    )
```

```python
import functools

import jax
import jax.numpy as jnp
from jax import lax
from jax.experimental import pallas as pl
from jax.experimental.pallas import tpu as pltpu
from jax.sharding import Mesh, PartitionSpec as P

MESH = pl.DeviceIdType.MESH


NY = 4
CORES = 2
LANES = 128


def _row():
    return lax.axis_index("z"), lax.axis_index("core")


def _group(kind, n_red):
    r = lax.axis_index("red")
    x, y = r // NY, lax.rem(r, NY)
    if kind == "y":
        return y, NY, lambda pos: x * NY + pos
    if kind == "x":
        return x, n_red // NY, lambda pos: pos * NY + y
    return r, n_red, lambda pos: pos


def _gather_kernel(n_red, src_ref, out_ref, send_sem, recv_sem, local_sem):
    row = _row()
    ym, ny, red_y = _group("y", n_red)
    xm, nx, red_x = _group("x", n_red)
    part = src_ref.shape[0] // 2
    first, second = pl.ds(0, part), pl.ds(part, part)

    barrier = pltpu.get_barrier_semaphore()
    for o in range(1, ny):
        pl.semaphore_signal(barrier, inc=1, device_id=(*row, red_y(lax.rem(ym + o, ny))), device_id_type=MESH)
    for o in range(1, nx):
        pl.semaphore_signal(barrier, inc=1, device_id=(*row, red_x(lax.rem(xm + o, nx))), device_id_type=MESH)
    pl.semaphore_wait(barrier, ny - 1 + nx - 1)

    def copy(src, dst, stage, pos, dev):
        return pltpu.make_async_remote_copy(
            src_ref=src,
            dst_ref=dst,
            send_sem=send_sem.at[stage, pos],
            recv_sem=recv_sem.at[stage, pos],
            device_id=(*row, dev),
            device_id_type=MESH,
        )

    sent = []
    for o in range(1, ny):
        g = lax.rem(ym + o, ny)
        c = pltpu.make_async_remote_copy(
            src_ref=src_ref.at[first], dst_ref=out_ref.at[xm, ym, first],
            send_sem=send_sem.at[0, g], recv_sem=recv_sem.at[0, ym],
            device_id=(*row, red_y(g)), device_id_type=MESH,
        )
        c.start()
        sent.append(c)
    for o in range(1, nx):
        g = lax.rem(xm + o, nx)
        c = pltpu.make_async_remote_copy(
            src_ref=src_ref.at[second], dst_ref=out_ref.at[xm, ym, second],
            send_sem=send_sem.at[1, g], recv_sem=recv_sem.at[1, xm],
            device_id=(*row, red_x(g)), device_id_type=MESH,
        )
        c.start()
        sent.append(c)
    own = [
        pltpu.make_async_copy(src_ref.at[first], out_ref.at[xm, ym, first], local_sem.at[0]),
        pltpu.make_async_copy(src_ref.at[second], out_ref.at[xm, ym, second], local_sem.at[1]),
    ]
    for c in own:
        c.start()
    for c in own:
        c.wait()

    for o in range(1, ny):
        g = lax.rem(ym + o, ny)
        copy(src_ref.at[first], out_ref.at[xm, g, first], 0, g, red_y(g)).wait_recv()
    for o in range(1, nx):
        g = lax.rem(xm + o, nx)
        c = pltpu.make_async_remote_copy(
            src_ref=out_ref.at[xm, :, first], dst_ref=out_ref.at[xm, :, first],
            send_sem=send_sem.at[2, g], recv_sem=recv_sem.at[2, xm],
            device_id=(*row, red_x(g)), device_id_type=MESH,
        )
        c.start()
        sent.append(c)
    for o in range(1, nx):
        g = lax.rem(xm + o, nx)
        copy(src_ref.at[second], out_ref.at[g, ym, second], 1, g, red_x(g)).wait_recv()
    for o in range(1, ny):
        g = lax.rem(ym + o, ny)
        c = pltpu.make_async_remote_copy(
            src_ref=out_ref.at[:, ym, second], dst_ref=out_ref.at[:, ym, second],
            send_sem=send_sem.at[3, g], recv_sem=recv_sem.at[3, ym],
            device_id=(*row, red_y(g)), device_id_type=MESH,
        )
        c.start()
        sent.append(c)

    for c in sent:
        c.wait_send()
    for o in range(1, nx):
        g = lax.rem(xm + o, nx)
        copy(out_ref.at[g, :, first], out_ref.at[g, :, first], 2, g, red_x(g)).wait_recv()
    for o in range(1, ny):
        g = lax.rem(ym + o, ny)
        copy(out_ref.at[:, g, second], out_ref.at[:, g, second], 3, g, red_y(g)).wait_recv()


def _gather(block, n_red, collective_id):
    n_x = n_red // NY
    nbytes = block.size * block.dtype.itemsize
    return pl.pallas_call(
        functools.partial(_gather_kernel, n_red),
        out_shape=jax.ShapeDtypeStruct((n_x, NY) + block.shape, block.dtype),
        in_specs=[pl.BlockSpec(memory_space=pl.ANY)],
        out_specs=pl.BlockSpec(memory_space=pl.ANY),
        scratch_shapes=[
            pltpu.SemaphoreType.DMA((4, max(n_x, NY))),
            pltpu.SemaphoreType.DMA((4, max(n_x, NY))),
            pltpu.SemaphoreType.DMA((2,)),
        ],
        compiler_params=pltpu.CompilerParams(collective_id=collective_id, has_side_effects=True),
        cost_estimate=pl.CostEstimate(flops=0, bytes_accessed=2 * n_red * nbytes, transcendentals=0),
    )(block)


def _reduce_kernel(n_red, amp_ref, ints_ref, out_ref, ra, rb, pa, pb, sa, sb, qa, qb, send1, recv1, send2, recv2):
    row = _row()
    ym, ny, red_y = _group("y", n_red)
    xm, nx, red_x = _group("x", n_red)
    half = ra.shape[2]
    first, second = pl.ds(0, half), pl.ds(half, half)

    barrier = pltpu.get_barrier_semaphore()
    for o in range(1, ny):
        pl.semaphore_signal(barrier, inc=1, device_id=(*row, red_y(lax.rem(ym + o, ny))), device_id_type=MESH)
    for o in range(1, nx):
        pl.semaphore_signal(barrier, inc=1, device_id=(*row, red_x(lax.rem(xm + o, nx))), device_id_type=MESH)

    def copy(src, dst, send, recv, dev):
        return pltpu.make_async_remote_copy(
            src_ref=src, dst_ref=dst, send_sem=send, recv_sem=recv,
            device_id=(*row, dev), device_id_type=MESH,
        )

    width = ints_ref.shape[1]

    def block(lhs):
        slots = lhs.shape[0]
        flat = lhs.reshape(slots * half, lhs.shape[2])
        product = jnp.dot(flat, ints_ref[...], preferred_element_type=jnp.float32)
        return product.reshape(slots, half, width)

    pa[lax.rem(ym + 1, ny)] = block(amp_ref[:, lax.rem(ym + 1, ny), first])
    pb[lax.rem(xm + 1, nx)] = block(amp_ref[lax.rem(xm + 1, nx), :, second])
    pl.semaphore_wait(barrier, ny - 1 + nx - 1)
    sent = []
    for o in range(1, max(nx, ny)):
        if o < ny:
            g = lax.rem(ym + o, ny)
            if o > 1:
                pa[g] = block(amp_ref[:, g, first])
            c = copy(pa.at[g], ra.at[ym], send1.at[0, g], recv1.at[0, ym], red_y(g))
            c.start()
            sent.append(c)
        if o < nx:
            g = lax.rem(xm + o, nx)
            if o > 1:
                pb[g] = block(amp_ref[g, :, second])
            c = copy(pb.at[g], rb.at[xm], send1.at[1, g], recv1.at[1, xm], red_x(g))
            c.start()
            sent.append(c)
    ra[ym] = block(amp_ref[:, ym, first])
    rb[xm] = block(amp_ref[xm, :, second])

    for o in range(1, ny):
        g = lax.rem(ym + o, ny)
        copy(pa.at[g], ra.at[g], send1.at[0, g], recv1.at[0, g], red_y(g)).wait_recv()
    for o in range(1, nx):
        g = lax.rem(xm + o, nx)
        sa[g] = ra[0, g] + ra[1, g] + ra[2, g] + ra[3, g]
        c = copy(sa.at[g], qa.at[xm], send2.at[0, g], recv2.at[0, xm], red_x(g))
        c.start()
        sent.append(c)
    sa[xm] = ra[0, xm] + ra[1, xm] + ra[2, xm] + ra[3, xm]

    for o in range(1, nx):
        g = lax.rem(xm + o, nx)
        copy(pb.at[g], rb.at[g], send1.at[1, g], recv1.at[1, g], red_x(g)).wait_recv()
    for o in range(1, ny):
        g = lax.rem(ym + o, ny)
        sb[g] = rb[0, g] + rb[1, g] + rb[2, g] + rb[3, g]
        c = copy(sb.at[g], qb.at[ym], send2.at[1, g], recv2.at[1, ym], red_y(g))
        c.start()
        sent.append(c)
    sb[ym] = rb[0, ym] + rb[1, ym] + rb[2, ym] + rb[3, ym]

    for c in sent:
        c.wait_send()
    total_a = sa[xm]
    for o in range(1, nx):
        g = lax.rem(xm + o, nx)
        copy(sa.at[g], qa.at[g], send2.at[0, g], recv2.at[0, g], red_x(g)).wait_recv()
        total_a = total_a + qa[g]
    total_b = sb[ym]
    for o in range(1, ny):
        g = lax.rem(ym + o, ny)
        copy(sb.at[g], qb.at[g], send2.at[1, g], recv2.at[1, g], red_y(g)).wait_recv()
        total_b = total_b + qb[g]
    lanes = out_ref.shape[2]
    out_ref[first] = total_a.reshape(half, width // lanes, lanes)
    out_ref[second] = total_b.reshape(half, width // lanes, lanes)


def _reduce(amp, ints, n_red, collective_id):
    n_x, n_y, rows, _ = amp.shape
    cols = ints.shape[1]
    half = rows // 2
    f32 = jnp.float32
    return pl.pallas_call(
        functools.partial(_reduce_kernel, n_red),
        out_shape=jax.ShapeDtypeStruct((rows, cols // LANES, LANES), f32),
        in_specs=[pl.BlockSpec(memory_space=pltpu.VMEM)] * 2,
        out_specs=pl.BlockSpec(memory_space=pltpu.VMEM),
        scratch_shapes=[
            pltpu.VMEM((n_y, n_x, half, cols), f32),
            pltpu.VMEM((n_x, n_y, half, cols), f32),
            pltpu.VMEM((n_y, n_x, half, cols), f32),
            pltpu.VMEM((n_x, n_y, half, cols), f32),
            pltpu.VMEM((n_x, half, cols), f32),
            pltpu.VMEM((n_y, half, cols), f32),
            pltpu.VMEM((n_x, half, cols), f32),
            pltpu.VMEM((n_y, half, cols), f32),
            pltpu.SemaphoreType.DMA((2, max(n_x, n_y))),
            pltpu.SemaphoreType.DMA((2, max(n_x, n_y))),
            pltpu.SemaphoreType.DMA((2, max(n_x, n_y))),
            pltpu.SemaphoreType.DMA((2, max(n_x, n_y))),
        ],
        compiler_params=pltpu.CompilerParams(
            collective_id=collective_id, has_side_effects=True, vmem_limit_bytes=60 * 1024 * 1024
        ),
        cost_estimate=pl.CostEstimate(
            flops=2 * amp.size * cols, bytes_accessed=amp.size * 2 + ints.size * 2 + rows * cols * 4,
            transcendentals=0,
        ),
    )(amp, ints)


def _core_reduce_kernel(amp_ref, ints_ref, out_ref, mine_sent, theirs, send_sem, recv_sem):
    z, core = _row()
    red = lax.axis_index("red")
    other = CORES - 1 - core
    n_z, _, rows, _ = amp_ref.shape
    width = ints_ref.shape[1]
    pieces = send_sem.shape[0]
    barrier = pltpu.get_barrier_semaphore()
    pl.semaphore_signal(barrier, inc=1, device_id=(z, other, red), device_id_type=MESH)

    def block(start, size, which):
        lhs = amp_ref[pl.ds(start, size), which]
        product = jnp.dot(
            lhs.reshape(size * rows, lhs.shape[2]), ints_ref[...], preferred_element_type=jnp.float32
        )
        return product.reshape(size, rows, width)

    step = n_z // pieces
    sends = []
    for k in range(pieces):
        mine_sent[pl.ds(k * step, step)] = block(k * step, step, other)
        if k == 0:
            pl.semaphore_wait(barrier, 1)
        c = pltpu.make_async_remote_copy(
            src_ref=mine_sent.at[pl.ds(k * step, step)], dst_ref=theirs.at[pl.ds(k * step, step)],
            send_sem=send_sem.at[k], recv_sem=recv_sem.at[k],
            device_id=(z, other, red), device_id_type=MESH,
        )
        c.start()
        sends.append(c)
    for k in range(2):
        out_ref[pl.ds(k * (n_z // 2), n_z // 2)] = block(k * (n_z // 2), n_z // 2, core)
    for k, c in enumerate(sends):
        c.wait()
        for i in range(k * step, (k + 1) * step):
            out_ref[i] = out_ref[i] + theirs[i]


def _core_reduce(amp, ints, collective_id):
    n_z, _, rows, _ = amp.shape
    cols = ints.shape[1]
    f32 = jnp.float32
    return pl.pallas_call(
        _core_reduce_kernel,
        out_shape=jax.ShapeDtypeStruct((n_z, rows, cols), f32),
        in_specs=[pl.BlockSpec(memory_space=pltpu.VMEM)] * 2,
        out_specs=pl.BlockSpec(memory_space=pltpu.VMEM),
        scratch_shapes=[
            pltpu.VMEM((n_z, rows, cols), f32),
            pltpu.VMEM((n_z, rows, cols), f32),
            pltpu.SemaphoreType.DMA((4,)),
            pltpu.SemaphoreType.DMA((4,)),
        ],
        compiler_params=pltpu.CompilerParams(
            collective_id=collective_id, has_side_effects=True, vmem_limit_bytes=60 * 1024 * 1024
        ),
        cost_estimate=pl.CostEstimate(
            flops=2 * amp.size * cols, bytes_accessed=amp.size * 2 + ints.size * 2 + n_z * rows * cols * 4,
            transcendentals=0,
        ),
    )(amp, ints)


def shards(amplitudes, ladder_ints, cycle_ints, occ_energy, vir_energy, slab_index):
    slab_rows, occ_local, vir_local, virt_width = amplitudes.shape
    n_red = lax.axis_size("red")
    n_blk = lax.axis_size("z") * lax.axis_size("core")
    occ_all = occ_local * n_blk
    occ_red = occ_all // n_red
    n_x = n_red // NY

    swapped = jnp.transpose(amplitudes, (0, 2, 1, 3)).reshape(
        slab_rows * vir_local, occ_local * virt_width
    )
    gathered = _gather(swapped, n_red, 0)
    operand = gathered.reshape(n_blk // CORES, CORES, slab_rows * vir_local, occ_local * virt_width)
    product = _core_reduce(operand, cycle_ints, 4)
    cycle_own = lax.psum_scatter(product, "z", scatter_dimension=0, tiled=True)[0]
    cycle_own = jnp.transpose(
        cycle_own.reshape(slab_rows, vir_local, occ_red, virt_width), (0, 2, 1, 3)
    )

    rows = slab_rows * occ_local
    flat = amplitudes.reshape(rows, vir_local * virt_width)
    shard_piece = lax.all_gather(flat, ("z", "core"), axis=0, tiled=False)
    ladder_own = _reduce(shard_piece.reshape(n_x, NY, rows, -1), ladder_ints, n_red, 1)
    ladder_own = ladder_own.reshape(slab_rows, occ_red, -1, virt_width)

    vir_block = cycle_own.shape[2]
    orbital_ids = jnp.arange(occ_energy.shape[0], dtype=jnp.int32)
    chosen = slab_index[:, None] == orbital_ids[None, :]
    slab_energy = jnp.sum(jnp.where(chosen, occ_energy[None, :], jnp.float32(0.0)), axis=1)
    pair_energy = lax.dynamic_slice_in_dim(occ_energy, lax.axis_index("red") * occ_red, occ_red)
    first_virtual = lax.dynamic_slice_in_dim(
        vir_energy, (lax.axis_index("z") * CORES + lax.axis_index("core")) * vir_block, vir_block
    )
    denominator = (
        first_virtual[None, None, :, None]
        + vir_energy[None, None, None, :]
        - slab_energy[:, None, None, None]
        - pair_energy[None, :, None, None]
    )
    return (ladder_own + cycle_own) / denominator


def solution(mesh):
    blk = ("z", "core")
    split = Mesh(
        mesh.devices.reshape(mesh.shape["blk"] // CORES, CORES, mesh.shape["red"]),
        ("z", "core", "red"),
    )
    placed = (P(None, blk, "red", None), P("red", blk), P(blk, "red"), P(), P(), P())
    return jax.shard_map(
        shards, mesh=split, in_specs=placed, out_specs=P(None, "red", blk, None), check_vma=False
    )
```

```python
import functools

import jax
import jax.numpy as jnp
from jax import lax
from jax.experimental import pallas as pl
from jax.experimental.pallas import tpu as pltpu
from jax.sharding import Mesh, PartitionSpec as P

MESH = pl.DeviceIdType.MESH


NY = 4
CORES = 2
LANES = 128


def _row():
    return lax.axis_index("z"), lax.axis_index("core")


def _group(kind, n_red):
    r = lax.axis_index("red")
    x, y = r // NY, lax.rem(r, NY)
    if kind == "y":
        return y, NY, lambda pos: x * NY + pos
    if kind == "x":
        return x, n_red // NY, lambda pos: pos * NY + y
    return r, n_red, lambda pos: pos


def _gather_kernel(n_red, src_ref, out_ref, send_sem, recv_sem, local_sem):
    row = _row()
    ym, ny, red_y = _group("y", n_red)
    xm, nx, red_x = _group("x", n_red)
    part = src_ref.shape[0] // 2
    first, second = pl.ds(0, part), pl.ds(part, part)

    barrier = pltpu.get_barrier_semaphore()
    for o in range(1, ny):
        pl.semaphore_signal(barrier, inc=1, device_id=(*row, red_y(lax.rem(ym + o, ny))), device_id_type=MESH)
    for o in range(1, nx):
        pl.semaphore_signal(barrier, inc=1, device_id=(*row, red_x(lax.rem(xm + o, nx))), device_id_type=MESH)
    pl.semaphore_wait(barrier, ny - 1 + nx - 1)

    def copy(src, dst, stage, pos, dev):
        return pltpu.make_async_remote_copy(
            src_ref=src,
            dst_ref=dst,
            send_sem=send_sem.at[stage, pos],
            recv_sem=recv_sem.at[stage, pos],
            device_id=(*row, dev),
            device_id_type=MESH,
        )

    sent = []
    for o in range(1, ny):
        g = lax.rem(ym + o, ny)
        c = pltpu.make_async_remote_copy(
            src_ref=src_ref.at[first], dst_ref=out_ref.at[xm, ym, first],
            send_sem=send_sem.at[0, g], recv_sem=recv_sem.at[0, ym],
            device_id=(*row, red_y(g)), device_id_type=MESH,
        )
        c.start()
        sent.append(c)
    for o in range(1, nx):
        g = lax.rem(xm + o, nx)
        c = pltpu.make_async_remote_copy(
            src_ref=src_ref.at[second], dst_ref=out_ref.at[xm, ym, second],
            send_sem=send_sem.at[1, g], recv_sem=recv_sem.at[1, xm],
            device_id=(*row, red_x(g)), device_id_type=MESH,
        )
        c.start()
        sent.append(c)
    own = [
        pltpu.make_async_copy(src_ref.at[first], out_ref.at[xm, ym, first], local_sem.at[0]),
        pltpu.make_async_copy(src_ref.at[second], out_ref.at[xm, ym, second], local_sem.at[1]),
    ]
    for c in own:
        c.start()
    for c in own:
        c.wait()

    for o in range(1, ny):
        g = lax.rem(ym + o, ny)
        copy(src_ref.at[first], out_ref.at[xm, g, first], 0, g, red_y(g)).wait_recv()
    for o in range(1, nx):
        g = lax.rem(xm + o, nx)
        c = pltpu.make_async_remote_copy(
            src_ref=out_ref.at[xm, :, first], dst_ref=out_ref.at[xm, :, first],
            send_sem=send_sem.at[2, g], recv_sem=recv_sem.at[2, xm],
            device_id=(*row, red_x(g)), device_id_type=MESH,
        )
        c.start()
        sent.append(c)
    for o in range(1, nx):
        g = lax.rem(xm + o, nx)
        copy(src_ref.at[second], out_ref.at[g, ym, second], 1, g, red_x(g)).wait_recv()
    for o in range(1, ny):
        g = lax.rem(ym + o, ny)
        c = pltpu.make_async_remote_copy(
            src_ref=out_ref.at[:, ym, second], dst_ref=out_ref.at[:, ym, second],
            send_sem=send_sem.at[3, g], recv_sem=recv_sem.at[3, ym],
            device_id=(*row, red_y(g)), device_id_type=MESH,
        )
        c.start()
        sent.append(c)

    for c in sent:
        c.wait_send()
    for o in range(1, nx):
        g = lax.rem(xm + o, nx)
        copy(out_ref.at[g, :, first], out_ref.at[g, :, first], 2, g, red_x(g)).wait_recv()
    for o in range(1, ny):
        g = lax.rem(ym + o, ny)
        copy(out_ref.at[:, g, second], out_ref.at[:, g, second], 3, g, red_y(g)).wait_recv()


def _gather(block, n_red, collective_id):
    n_x = n_red // NY
    nbytes = block.size * block.dtype.itemsize
    return pl.pallas_call(
        functools.partial(_gather_kernel, n_red),
        out_shape=jax.ShapeDtypeStruct((n_x, NY) + block.shape, block.dtype),
        in_specs=[pl.BlockSpec(memory_space=pl.ANY)],
        out_specs=pl.BlockSpec(memory_space=pl.ANY),
        scratch_shapes=[
            pltpu.SemaphoreType.DMA((4, max(n_x, NY))),
            pltpu.SemaphoreType.DMA((4, max(n_x, NY))),
            pltpu.SemaphoreType.DMA((2,)),
        ],
        compiler_params=pltpu.CompilerParams(collective_id=collective_id, has_side_effects=True),
        cost_estimate=pl.CostEstimate(flops=0, bytes_accessed=2 * n_red * nbytes, transcendentals=0),
    )(block)


def _reduce_kernel(n_red, amp_ref, ints_ref, out_ref, ra, rb, pa, pb, sa, sb, qa, qb, send1, recv1, send2, recv2):
    row = _row()
    ym, ny, red_y = _group("y", n_red)
    xm, nx, red_x = _group("x", n_red)
    half = ra.shape[2]
    first, second = pl.ds(0, half), pl.ds(half, half)

    barrier = pltpu.get_barrier_semaphore()
    for o in range(1, ny):
        pl.semaphore_signal(barrier, inc=1, device_id=(*row, red_y(lax.rem(ym + o, ny))), device_id_type=MESH)
    for o in range(1, nx):
        pl.semaphore_signal(barrier, inc=1, device_id=(*row, red_x(lax.rem(xm + o, nx))), device_id_type=MESH)

    def copy(src, dst, send, recv, dev):
        return pltpu.make_async_remote_copy(
            src_ref=src, dst_ref=dst, send_sem=send, recv_sem=recv,
            device_id=(*row, dev), device_id_type=MESH,
        )

    width = ints_ref.shape[1]

    def block(lhs):
        slots = lhs.shape[0]
        flat = lhs.reshape(slots * half, lhs.shape[2])
        product = jnp.dot(flat, ints_ref[...], preferred_element_type=jnp.float32)
        return product.reshape(slots, half, width)

    pa[lax.rem(ym + 1, ny)] = block(amp_ref[:, lax.rem(ym + 1, ny), first])
    pb[lax.rem(xm + 1, nx)] = block(amp_ref[lax.rem(xm + 1, nx), :, second])
    pl.semaphore_wait(barrier, ny - 1 + nx - 1)
    sent = []
    for o in range(1, max(nx, ny)):
        if o < ny:
            g = lax.rem(ym + o, ny)
            if o > 1:
                pa[g] = block(amp_ref[:, g, first])
            c = copy(pa.at[g], ra.at[ym], send1.at[0, g], recv1.at[0, ym], red_y(g))
            c.start()
            sent.append(c)
        if o < nx:
            g = lax.rem(xm + o, nx)
            if o > 1:
                pb[g] = block(amp_ref[g, :, second])
            c = copy(pb.at[g], rb.at[xm], send1.at[1, g], recv1.at[1, xm], red_x(g))
            c.start()
            sent.append(c)
    ra[ym] = block(amp_ref[:, ym, first])
    rb[xm] = block(amp_ref[xm, :, second])

    for o in range(1, ny):
        g = lax.rem(ym + o, ny)
        copy(pa.at[g], ra.at[g], send1.at[0, g], recv1.at[0, g], red_y(g)).wait_recv()
    for o in range(1, nx):
        g = lax.rem(xm + o, nx)
        sa[g] = ra[0, g] + ra[1, g] + ra[2, g] + ra[3, g]
        c = copy(sa.at[g], qa.at[xm], send2.at[0, g], recv2.at[0, xm], red_x(g))
        c.start()
        sent.append(c)
    sa[xm] = ra[0, xm] + ra[1, xm] + ra[2, xm] + ra[3, xm]

    for o in range(1, nx):
        g = lax.rem(xm + o, nx)
        copy(pb.at[g], rb.at[g], send1.at[1, g], recv1.at[1, g], red_x(g)).wait_recv()
    for o in range(1, ny):
        g = lax.rem(ym + o, ny)
        sb[g] = rb[0, g] + rb[1, g] + rb[2, g] + rb[3, g]
        c = copy(sb.at[g], qb.at[ym], send2.at[1, g], recv2.at[1, ym], red_y(g))
        c.start()
        sent.append(c)
    sb[ym] = rb[0, ym] + rb[1, ym] + rb[2, ym] + rb[3, ym]

    for c in sent:
        c.wait_send()
    total_a = sa[xm]
    for o in range(1, nx):
        g = lax.rem(xm + o, nx)
        copy(sa.at[g], qa.at[g], send2.at[0, g], recv2.at[0, g], red_x(g)).wait_recv()
        total_a = total_a + qa[g]
    total_b = sb[ym]
    for o in range(1, ny):
        g = lax.rem(ym + o, ny)
        copy(sb.at[g], qb.at[g], send2.at[1, g], recv2.at[1, g], red_y(g)).wait_recv()
        total_b = total_b + qb[g]
    lanes = out_ref.shape[2]
    out_ref[first] = total_a.reshape(half, width // lanes, lanes)
    out_ref[second] = total_b.reshape(half, width // lanes, lanes)


def _reduce(amp, ints, n_red, collective_id):
    n_x, n_y, rows, _ = amp.shape
    cols = ints.shape[1]
    half = rows // 2
    f32 = jnp.float32
    return pl.pallas_call(
        functools.partial(_reduce_kernel, n_red),
        out_shape=jax.ShapeDtypeStruct((rows, cols // LANES, LANES), f32),
        in_specs=[pl.BlockSpec(memory_space=pltpu.VMEM)] * 2,
        out_specs=pl.BlockSpec(memory_space=pltpu.VMEM),
        scratch_shapes=[
            pltpu.VMEM((n_y, n_x, half, cols), f32),
            pltpu.VMEM((n_x, n_y, half, cols), f32),
            pltpu.VMEM((n_y, n_x, half, cols), f32),
            pltpu.VMEM((n_x, n_y, half, cols), f32),
            pltpu.VMEM((n_x, half, cols), f32),
            pltpu.VMEM((n_y, half, cols), f32),
            pltpu.VMEM((n_x, half, cols), f32),
            pltpu.VMEM((n_y, half, cols), f32),
            pltpu.SemaphoreType.DMA((2, max(n_x, n_y))),
            pltpu.SemaphoreType.DMA((2, max(n_x, n_y))),
            pltpu.SemaphoreType.DMA((2, max(n_x, n_y))),
            pltpu.SemaphoreType.DMA((2, max(n_x, n_y))),
        ],
        compiler_params=pltpu.CompilerParams(
            collective_id=collective_id, has_side_effects=True, vmem_limit_bytes=60 * 1024 * 1024
        ),
        cost_estimate=pl.CostEstimate(
            flops=2 * amp.size * cols, bytes_accessed=amp.size * 2 + ints.size * 2 + rows * cols * 4,
            transcendentals=0,
        ),
    )(amp, ints)


def _core_reduce_kernel(amp_ref, ints_ref, out_ref, mine_sent, theirs, send_sem, recv_sem):
    z, core = _row()
    red = lax.axis_index("red")
    other = CORES - 1 - core
    n_z, _, rows, _ = amp_ref.shape
    width = ints_ref.shape[1]
    pieces = send_sem.shape[0]
    barrier = pltpu.get_barrier_semaphore()
    pl.semaphore_signal(barrier, inc=1, device_id=(z, other, red), device_id_type=MESH)

    def block(start, size, which):
        lhs = amp_ref[pl.ds(start, size), which]
        product = jnp.dot(
            lhs.reshape(size * rows, lhs.shape[2]), ints_ref[...], preferred_element_type=jnp.float32
        )
        return product.reshape(size, rows, width)

    step = n_z // pieces
    sends = []
    for k in range(pieces):
        mine_sent[pl.ds(k * step, step)] = block(k * step, step, other)
        if k == 0:
            pl.semaphore_wait(barrier, 1)
        c = pltpu.make_async_remote_copy(
            src_ref=mine_sent.at[pl.ds(k * step, step)], dst_ref=theirs.at[pl.ds(k * step, step)],
            send_sem=send_sem.at[k], recv_sem=recv_sem.at[k],
            device_id=(z, other, red), device_id_type=MESH,
        )
        c.start()
        sends.append(c)
    for k in range(2):
        out_ref[pl.ds(k * (n_z // 2), n_z // 2)] = block(k * (n_z // 2), n_z // 2, core)
    for k, c in enumerate(sends):
        c.wait()
        for i in range(k * step, (k + 1) * step):
            out_ref[i] = out_ref[i] + theirs[i]


def _core_reduce(amp, ints, collective_id):
    n_z, _, rows, _ = amp.shape
    cols = ints.shape[1]
    f32 = jnp.float32
    return pl.pallas_call(
        _core_reduce_kernel,
        out_shape=jax.ShapeDtypeStruct((n_z, rows, cols), f32),
        in_specs=[pl.BlockSpec(memory_space=pltpu.VMEM)] * 2,
        out_specs=pl.BlockSpec(memory_space=pltpu.VMEM),
        scratch_shapes=[
            pltpu.VMEM((n_z, rows, cols), f32),
            pltpu.VMEM((n_z, rows, cols), f32),
            pltpu.SemaphoreType.DMA((4,)),
            pltpu.SemaphoreType.DMA((4,)),
        ],
        compiler_params=pltpu.CompilerParams(
            collective_id=collective_id, has_side_effects=True, vmem_limit_bytes=60 * 1024 * 1024
        ),
        cost_estimate=pl.CostEstimate(
            flops=2 * amp.size * cols, bytes_accessed=amp.size * 2 + ints.size * 2 + n_z * rows * cols * 4,
            transcendentals=0,
        ),
    )(amp, ints)


def shards(amplitudes, ladder_ints, cycle_ints, occ_energy, vir_energy, slab_index):
    slab_rows, occ_local, vir_local, virt_width = amplitudes.shape
    n_red = lax.axis_size("red")
    n_blk = lax.axis_size("z") * lax.axis_size("core")
    occ_all = occ_local * n_blk
    occ_red = occ_all // n_red
    n_x = n_red // NY

    swapped = jnp.transpose(amplitudes, (0, 2, 1, 3)).reshape(
        slab_rows * vir_local, occ_local * virt_width
    )
    gathered = _gather(swapped, n_red, 0)
    operand = gathered.reshape(n_blk // CORES, CORES, slab_rows * vir_local, occ_local * virt_width)
    product = _core_reduce(operand, cycle_ints, 4)
    cycle_own = lax.psum_scatter(product, "z", scatter_dimension=0, tiled=True)[0]
    cycle_own = jnp.transpose(
        cycle_own.reshape(slab_rows, vir_local, occ_red, virt_width), (0, 2, 1, 3)
    )

    rows = slab_rows * occ_local
    flat = amplitudes.reshape(rows, vir_local * virt_width)
    shard_piece = lax.all_gather(flat, ("z", "core"), axis=0, tiled=False)
    ladder_own = _reduce(shard_piece.reshape(n_x, NY, rows, -1), ladder_ints, n_red, 1)
    ladder_own = ladder_own.reshape(slab_rows, occ_red, -1, virt_width)

    vir_block = cycle_own.shape[2]
    orbital_ids = jnp.arange(occ_energy.shape[0], dtype=jnp.int32)
    chosen = slab_index[:, None] == orbital_ids[None, :]
    slab_energy = jnp.sum(jnp.where(chosen, occ_energy[None, :], jnp.float32(0.0)), axis=1)
    pair_energy = lax.dynamic_slice_in_dim(occ_energy, lax.axis_index("red") * occ_red, occ_red)
    first_virtual = lax.dynamic_slice_in_dim(
        vir_energy, (lax.axis_index("z") * CORES + lax.axis_index("core")) * vir_block, vir_block
    )
    denominator = (
        first_virtual[None, None, :, None]
        + vir_energy[None, None, None, :]
        - slab_energy[:, None, None, None]
        - pair_energy[None, :, None, None]
    )
    denominator = lax.optimization_barrier(denominator)
    return (ladder_own + cycle_own) / denominator


def solution(mesh):
    blk = ("z", "core")
    split = Mesh(
        mesh.devices.reshape(mesh.shape["blk"] // CORES, CORES, mesh.shape["red"]),
        ("z", "core", "red"),
    )
    placed = (P(None, blk, "red", None), P("red", blk), P(blk, "red"), P(), P(), P())
    return jax.shard_map(
        shards, mesh=split, in_specs=placed, out_specs=P(None, "red", blk, None), check_vma=False
    )
```

```python
import functools

import jax
import jax.numpy as jnp
from jax import lax
from jax.experimental import pallas as pl
from jax.experimental.pallas import tpu as pltpu
from jax.sharding import Mesh, PartitionSpec as P

MESH = pl.DeviceIdType.MESH


NY = 4
CORES = 2
LANES = 128


def _row():
    return lax.axis_index("z"), lax.axis_index("core")


def _group(kind, n_red):
    r = lax.axis_index("red")
    x, y = r // NY, lax.rem(r, NY)
    if kind == "y":
        return y, NY, lambda pos: x * NY + pos
    if kind == "x":
        return x, n_red // NY, lambda pos: pos * NY + y
    return r, n_red, lambda pos: pos


def _gather_kernel(n_red, src_ref, out_ref, send_sem, recv_sem, local_sem):
    row = _row()
    ym, ny, red_y = _group("y", n_red)
    xm, nx, red_x = _group("x", n_red)
    part = src_ref.shape[0] // 2
    first, second = pl.ds(0, part), pl.ds(part, part)

    barrier = pltpu.get_barrier_semaphore()
    for o in range(1, ny):
        pl.semaphore_signal(barrier, inc=1, device_id=(*row, red_y(lax.rem(ym + o, ny))), device_id_type=MESH)
    for o in range(1, nx):
        pl.semaphore_signal(barrier, inc=1, device_id=(*row, red_x(lax.rem(xm + o, nx))), device_id_type=MESH)
    pl.semaphore_wait(barrier, ny - 1 + nx - 1)

    def copy(src, dst, stage, pos, dev):
        return pltpu.make_async_remote_copy(
            src_ref=src,
            dst_ref=dst,
            send_sem=send_sem.at[stage, pos],
            recv_sem=recv_sem.at[stage, pos],
            device_id=(*row, dev),
            device_id_type=MESH,
        )

    sent = []
    for o in range(1, ny):
        g = lax.rem(ym + o, ny)
        c = pltpu.make_async_remote_copy(
            src_ref=src_ref.at[first], dst_ref=out_ref.at[xm, ym, first],
            send_sem=send_sem.at[0, g], recv_sem=recv_sem.at[0, ym],
            device_id=(*row, red_y(g)), device_id_type=MESH,
        )
        c.start()
        sent.append(c)
    for o in range(1, nx):
        g = lax.rem(xm + o, nx)
        c = pltpu.make_async_remote_copy(
            src_ref=src_ref.at[second], dst_ref=out_ref.at[xm, ym, second],
            send_sem=send_sem.at[1, g], recv_sem=recv_sem.at[1, xm],
            device_id=(*row, red_x(g)), device_id_type=MESH,
        )
        c.start()
        sent.append(c)
    own = [
        pltpu.make_async_copy(src_ref.at[first], out_ref.at[xm, ym, first], local_sem.at[0]),
        pltpu.make_async_copy(src_ref.at[second], out_ref.at[xm, ym, second], local_sem.at[1]),
    ]
    for c in own:
        c.start()
    for c in own:
        c.wait()

    for o in range(1, ny):
        g = lax.rem(ym + o, ny)
        copy(src_ref.at[first], out_ref.at[xm, g, first], 0, g, red_y(g)).wait_recv()
    for o in range(1, nx):
        g = lax.rem(xm + o, nx)
        c = pltpu.make_async_remote_copy(
            src_ref=out_ref.at[xm, :, first], dst_ref=out_ref.at[xm, :, first],
            send_sem=send_sem.at[2, g], recv_sem=recv_sem.at[2, xm],
            device_id=(*row, red_x(g)), device_id_type=MESH,
        )
        c.start()
        sent.append(c)
    for o in range(1, nx):
        g = lax.rem(xm + o, nx)
        copy(src_ref.at[second], out_ref.at[g, ym, second], 1, g, red_x(g)).wait_recv()
    for o in range(1, ny):
        g = lax.rem(ym + o, ny)
        c = pltpu.make_async_remote_copy(
            src_ref=out_ref.at[:, ym, second], dst_ref=out_ref.at[:, ym, second],
            send_sem=send_sem.at[3, g], recv_sem=recv_sem.at[3, ym],
            device_id=(*row, red_y(g)), device_id_type=MESH,
        )
        c.start()
        sent.append(c)

    for c in sent:
        c.wait_send()
    for o in range(1, nx):
        g = lax.rem(xm + o, nx)
        copy(out_ref.at[g, :, first], out_ref.at[g, :, first], 2, g, red_x(g)).wait_recv()
    for o in range(1, ny):
        g = lax.rem(ym + o, ny)
        copy(out_ref.at[:, g, second], out_ref.at[:, g, second], 3, g, red_y(g)).wait_recv()


def _gather(block, n_red, collective_id):
    n_x = n_red // NY
    nbytes = block.size * block.dtype.itemsize
    return pl.pallas_call(
        functools.partial(_gather_kernel, n_red),
        out_shape=jax.ShapeDtypeStruct((n_x, NY) + block.shape, block.dtype),
        in_specs=[pl.BlockSpec(memory_space=pl.ANY)],
        out_specs=pl.BlockSpec(memory_space=pl.ANY),
        scratch_shapes=[
            pltpu.SemaphoreType.DMA((4, max(n_x, NY))),
            pltpu.SemaphoreType.DMA((4, max(n_x, NY))),
            pltpu.SemaphoreType.DMA((2,)),
        ],
        compiler_params=pltpu.CompilerParams(collective_id=collective_id, has_side_effects=True),
        cost_estimate=pl.CostEstimate(flops=0, bytes_accessed=2 * n_red * nbytes, transcendentals=0),
    )(block)


def _reduce_kernel(n_red, amp_ref, ints_ref, out_ref, ra, rb, pa, pb, sa, sb, qa, qb, send1, recv1, send2, recv2):
    row = _row()
    ym, ny, red_y = _group("y", n_red)
    xm, nx, red_x = _group("x", n_red)
    half = ra.shape[2]
    first, second = pl.ds(0, half), pl.ds(half, half)

    barrier = pltpu.get_barrier_semaphore()
    for o in range(1, ny):
        pl.semaphore_signal(barrier, inc=1, device_id=(*row, red_y(lax.rem(ym + o, ny))), device_id_type=MESH)
    for o in range(1, nx):
        pl.semaphore_signal(barrier, inc=1, device_id=(*row, red_x(lax.rem(xm + o, nx))), device_id_type=MESH)

    def copy(src, dst, send, recv, dev):
        return pltpu.make_async_remote_copy(
            src_ref=src, dst_ref=dst, send_sem=send, recv_sem=recv,
            device_id=(*row, dev), device_id_type=MESH,
        )

    width = ints_ref.shape[1]

    def block(lhs):
        slots = lhs.shape[0]
        flat = lhs.reshape(slots * half, lhs.shape[2])
        product = jnp.dot(flat, ints_ref[...], preferred_element_type=jnp.float32)
        return product.reshape(slots, half, width)

    pa[lax.rem(ym + 1, ny)] = block(amp_ref[:, lax.rem(ym + 1, ny), first])
    pb[lax.rem(xm + 1, nx)] = block(amp_ref[lax.rem(xm + 1, nx), :, second])
    pl.semaphore_wait(barrier, ny - 1 + nx - 1)
    sent = []
    for o in range(1, max(nx, ny)):
        if o < ny:
            g = lax.rem(ym + o, ny)
            if o > 1:
                pa[g] = block(amp_ref[:, g, first])
            c = copy(pa.at[g], ra.at[ym], send1.at[0, g], recv1.at[0, ym], red_y(g))
            c.start()
            sent.append(c)
        if o < nx:
            g = lax.rem(xm + o, nx)
            if o > 1:
                pb[g] = block(amp_ref[g, :, second])
            c = copy(pb.at[g], rb.at[xm], send1.at[1, g], recv1.at[1, xm], red_x(g))
            c.start()
            sent.append(c)
    ra[ym] = block(amp_ref[:, ym, first])
    rb[xm] = block(amp_ref[xm, :, second])

    for o in range(1, ny):
        g = lax.rem(ym + o, ny)
        copy(pa.at[g], ra.at[g], send1.at[0, g], recv1.at[0, g], red_y(g)).wait_recv()
    for o in range(1, nx):
        g = lax.rem(xm + o, nx)
        sa[g] = ra[0, g] + ra[1, g] + ra[2, g] + ra[3, g]
        c = copy(sa.at[g], qa.at[xm], send2.at[0, g], recv2.at[0, xm], red_x(g))
        c.start()
        sent.append(c)
    sa[xm] = ra[0, xm] + ra[1, xm] + ra[2, xm] + ra[3, xm]

    for o in range(1, nx):
        g = lax.rem(xm + o, nx)
        copy(pb.at[g], rb.at[g], send1.at[1, g], recv1.at[1, g], red_x(g)).wait_recv()
    for o in range(1, ny):
        g = lax.rem(ym + o, ny)
        sb[g] = rb[0, g] + rb[1, g] + rb[2, g] + rb[3, g]
        c = copy(sb.at[g], qb.at[ym], send2.at[1, g], recv2.at[1, ym], red_y(g))
        c.start()
        sent.append(c)
    sb[ym] = rb[0, ym] + rb[1, ym] + rb[2, ym] + rb[3, ym]

    for c in sent:
        c.wait_send()
    total_a = sa[xm]
    for o in range(1, nx):
        g = lax.rem(xm + o, nx)
        copy(sa.at[g], qa.at[g], send2.at[0, g], recv2.at[0, g], red_x(g)).wait_recv()
        total_a = total_a + qa[g]
    total_b = sb[ym]
    for o in range(1, ny):
        g = lax.rem(ym + o, ny)
        copy(sb.at[g], qb.at[g], send2.at[1, g], recv2.at[1, g], red_y(g)).wait_recv()
        total_b = total_b + qb[g]
    lanes = out_ref.shape[2]
    out_ref[first] = total_a.reshape(half, width // lanes, lanes)
    out_ref[second] = total_b.reshape(half, width // lanes, lanes)


def _reduce(amp, ints, n_red, collective_id):
    n_x, n_y, rows, _ = amp.shape
    cols = ints.shape[1]
    half = rows // 2
    f32 = jnp.float32
    return pl.pallas_call(
        functools.partial(_reduce_kernel, n_red),
        out_shape=jax.ShapeDtypeStruct((rows, cols // LANES, LANES), f32),
        in_specs=[pl.BlockSpec(memory_space=pltpu.VMEM)] * 2,
        out_specs=pl.BlockSpec(memory_space=pltpu.VMEM),
        scratch_shapes=[
            pltpu.VMEM((n_y, n_x, half, cols), f32),
            pltpu.VMEM((n_x, n_y, half, cols), f32),
            pltpu.VMEM((n_y, n_x, half, cols), f32),
            pltpu.VMEM((n_x, n_y, half, cols), f32),
            pltpu.VMEM((n_x, half, cols), f32),
            pltpu.VMEM((n_y, half, cols), f32),
            pltpu.VMEM((n_x, half, cols), f32),
            pltpu.VMEM((n_y, half, cols), f32),
            pltpu.SemaphoreType.DMA((2, max(n_x, n_y))),
            pltpu.SemaphoreType.DMA((2, max(n_x, n_y))),
            pltpu.SemaphoreType.DMA((2, max(n_x, n_y))),
            pltpu.SemaphoreType.DMA((2, max(n_x, n_y))),
        ],
        compiler_params=pltpu.CompilerParams(
            collective_id=collective_id, has_side_effects=True, vmem_limit_bytes=60 * 1024 * 1024
        ),
        cost_estimate=pl.CostEstimate(
            flops=2 * amp.size * cols, bytes_accessed=amp.size * 2 + ints.size * 2 + rows * cols * 4,
            transcendentals=0,
        ),
    )(amp, ints)


def _core_reduce_kernel(amp_ref, ints_ref, out_ref, mine_sent, theirs, send_sem, recv_sem):
    z, core = _row()
    red = lax.axis_index("red")
    other = CORES - 1 - core
    n_z, _, rows, _ = amp_ref.shape
    width = ints_ref.shape[1]
    pieces = send_sem.shape[0]
    barrier = pltpu.get_barrier_semaphore()
    pl.semaphore_signal(barrier, inc=1, device_id=(z, other, red), device_id_type=MESH)

    def block(start, size, which):
        lhs = amp_ref[pl.ds(start, size), which]
        product = jnp.dot(
            lhs.reshape(size * rows, lhs.shape[2]), ints_ref[...], preferred_element_type=jnp.float32
        )
        return product.reshape(size, rows, width)

    step = n_z // pieces
    sends = []
    for k in range(pieces):
        mine_sent[pl.ds(k * step, step)] = block(k * step, step, other)
        if k == 0:
            pl.semaphore_wait(barrier, 1)
        c = pltpu.make_async_remote_copy(
            src_ref=mine_sent.at[pl.ds(k * step, step)], dst_ref=theirs.at[pl.ds(k * step, step)],
            send_sem=send_sem.at[k], recv_sem=recv_sem.at[k],
            device_id=(z, other, red), device_id_type=MESH,
        )
        c.start()
        sends.append(c)
    for k in range(2):
        out_ref[pl.ds(k * (n_z // 2), n_z // 2)] = block(k * (n_z // 2), n_z // 2, core)
    for k, c in enumerate(sends):
        c.wait()
        for i in range(k * step, (k + 1) * step):
            out_ref[i] = out_ref[i] + theirs[i]


def _core_reduce(amp, ints, collective_id):
    n_z, _, rows, _ = amp.shape
    cols = ints.shape[1]
    f32 = jnp.float32
    return pl.pallas_call(
        _core_reduce_kernel,
        out_shape=jax.ShapeDtypeStruct((n_z, rows, cols), f32),
        in_specs=[pl.BlockSpec(memory_space=pltpu.VMEM)] * 2,
        out_specs=pl.BlockSpec(memory_space=pltpu.VMEM),
        scratch_shapes=[
            pltpu.VMEM((n_z, rows, cols), f32),
            pltpu.VMEM((n_z, rows, cols), f32),
            pltpu.SemaphoreType.DMA((4,)),
            pltpu.SemaphoreType.DMA((4,)),
        ],
        compiler_params=pltpu.CompilerParams(
            collective_id=collective_id, has_side_effects=True, vmem_limit_bytes=60 * 1024 * 1024
        ),
        cost_estimate=pl.CostEstimate(
            flops=2 * amp.size * cols, bytes_accessed=amp.size * 2 + ints.size * 2 + n_z * rows * cols * 4,
            transcendentals=0,
        ),
    )(amp, ints)


def shards(amplitudes, ladder_ints, cycle_ints, occ_energy, vir_energy, slab_index):
    slab_rows, occ_local, vir_local, virt_width = amplitudes.shape
    n_red = lax.axis_size("red")
    n_blk = lax.axis_size("z") * lax.axis_size("core")
    occ_all = occ_local * n_blk
    occ_red = occ_all // n_red
    n_x = n_red // NY

    swapped = jnp.transpose(amplitudes, (0, 2, 1, 3)).reshape(
        slab_rows * vir_local, occ_local * virt_width
    )
    gathered = _gather(swapped, n_red, 0)
    operand = gathered.reshape(n_blk // CORES, CORES, slab_rows * vir_local, occ_local * virt_width)
    product = _core_reduce(operand, cycle_ints, 4)
    cycle_own = lax.psum_scatter(product, "z", scatter_dimension=0, tiled=True)[0]
    cycle_own = jnp.transpose(
        cycle_own.reshape(slab_rows, vir_local, occ_red, virt_width), (0, 2, 1, 3)
    )

    rows = slab_rows * occ_local
    flat = amplitudes.reshape(rows, vir_local * virt_width)
    shard_piece = lax.all_gather(flat, ("z", "core"), axis=0, tiled=True)
    ladder_own = _reduce(shard_piece.reshape(n_x, NY, rows, -1), ladder_ints, n_red, 1)
    ladder_own = ladder_own.reshape(slab_rows, occ_red, -1, virt_width)

    vir_block = cycle_own.shape[2]
    orbital_ids = jnp.arange(occ_energy.shape[0], dtype=jnp.int32)
    chosen = slab_index[:, None] == orbital_ids[None, :]
    slab_energy = jnp.sum(jnp.where(chosen, occ_energy[None, :], jnp.float32(0.0)), axis=1)
    pair_energy = lax.dynamic_slice_in_dim(occ_energy, lax.axis_index("red") * occ_red, occ_red)
    first_virtual = lax.dynamic_slice_in_dim(
        vir_energy, (lax.axis_index("z") * CORES + lax.axis_index("core")) * vir_block, vir_block
    )
    denominator = (
        first_virtual[None, None, :, None]
        + vir_energy[None, None, None, :]
        - slab_energy[:, None, None, None]
        - pair_energy[None, :, None, None]
    )
    return (ladder_own + cycle_own) / denominator


def solution(mesh):
    blk = ("z", "core")
    split = Mesh(
        mesh.devices.reshape(mesh.shape["blk"] // CORES, CORES, mesh.shape["red"]),
        ("z", "core", "red"),
    )
    placed = (P(None, blk, "red", None), P("red", blk), P(blk, "red"), P(), P(), P())
    return jax.shard_map(
        shards, mesh=split, in_specs=placed, out_specs=P(None, "red", blk, None), check_vma=False
    )
```
